32 devices in a mesh: seq: 4 (over y, core), head: 8 (over z, x).
Axes of the slice: x: 2, y: 2, z: 4, core: 2. Of those that a mesh axis runs over, the one named last changes fastest.
Arguments:
- inputs: bfloat16 [4096, 3, 2048], P(('seq', 'head')), may hold values from -6 to 6
- attn_gain: float32 [2048], replicated, may hold values from 0.25 to 1.75
- w_query: bfloat16 [2048, 256], P(None, 'head'), may hold values from -0.125 to 0.125
- w_key: bfloat16 [2048, 256], P(None, 'head'), may hold values from -0.125 to 0.125
- w_value: bfloat16 [2048, 2048], P(None, 'head'), may hold values from -0.125 to 0.125
- w_out: bfloat16 [2048, 2048], P('head'), may hold values from -1.5 to 1.5
- out_bias: float32 [2048], replicated, may hold values from -1.5 to 1.5
- mlp_gain: float32 [2048], replicated, may hold values from 0.25 to 1.75
- gate_weight: bfloat16 [2048, 5504], P(None, 'head'), may hold values from -0.125 to 0.125
- up_weight: bfloat16 [2048, 5504], P(None, 'head'), may hold values from -0.125 to 0.125
- down_weight: bfloat16 [5504, 2048], P('head'), may hold values from -0.078125 to 0.078125
- cotangent: bfloat16 [4096, 3, 2048], P(('seq', 'head')), may hold values from -6 to 6
- doc_lengths: int32 [3, 8], replicated, may hold values from 1 to 1536, 4096 in all within a row
Outputs:
- output: bfloat16 [4096, 3, 2048], P(('seq', 'head'))
- input_grad: bfloat16 [4096, 3, 2048], P(('seq', 'head'))
- attn_gain_grad: float32 [2048], P(('seq', 'head'))
- w_query_grad: float32 [2048, 256], P('seq', 'head')
- w_key_grad: float32 [2048, 256], P('seq', 'head')
- w_value_grad: float32 [2048, 2048], P('seq', 'head')
- w_out_grad: float32 [2048, 2048], P('head', 'seq')
- out_bias_grad: float32 [2048], P(('seq', 'head'))
- mlp_gain_grad: float32 [2048], P(('seq', 'head'))
- w_gate_grad: float32 [2048, 5504], P('seq', 'head')
- w_up_grad: float32 [2048, 5504], P('seq', 'head')
- w_down_grad: float32 [5504, 2048], P('head', 'seq')
The draws below stay inside these ranges and needn't reach their ends.
Inputs may be any that keep to these rules, and one draw needn't show every extreme that they name: `doc_lengths`: in each row the 8 lengths sum to 4096 and the longest is exactly 1536.
All inputs are finite; a program needn't handle non-finite values.
Results may differ from the reference program's by a relative error of at most 0.02.
Values may be sent and summed in bfloat16 or wider, within the bound.
A program may use at most 320 MiB of HBM per device.

```python
import math
import jax
import jax.numpy as jnp
import numpy as np
from jax import lax

D = 2048
HEADS = 16
FEAT = 16
VHEAD = 128
FF = 5504
ROW_LEN = 4096
ROWS = 3
DOCS = 8
MOST = 1536
N_SEQ = 4


def steps_of(stream_key, shape, cuts, smallest, largest):
    level = 1.0
    for position, blocks in cuts:
        heights = jax.random.uniform(jax.random.fold_in(jax.random.fold_in(stream_key, 6), position), (blocks,), jnp.float32, smallest / len(cuts), largest / len(cuts))
        level = level * jnp.repeat(jnp.exp(heights), shape[position] // blocks).reshape((-1,) + (1,) * (len(shape) - 1 - position))
    return level


def profile(amount, total, reach, slope):
    weights = [(1 << 20) // math.isqrt(standing ** slope) + 1 for standing in range(2, amount + 1)]
    surplus, counts = total - reach - (amount - 1), [1] * (amount - 1)
    while surplus > 0:
        free = [i for i in range(amount - 1) if counts[i] < reach]
        whole, left = sum([weights[i] for i in free]), surplus
        for i in free:
            more = min(reach - counts[i], max(1, left * weights[i] // whole), surplus)
            counts[i] = counts[i] + more
            surplus = surplus - more
    return np.array([reach] + counts)


def ragged_sizes(stream_key, count, total, reach, lean):
    if count == 2:
        one = jax.random.randint(stream_key, (), max(1, total - reach), min(reach, total - 1) + 1)
        return jnp.stack([one, total - one])
    tallies = jnp.asarray(profile(count, total, reach, lean), jnp.int32)
    twos = (count - 1) // 2
    giver, receiver = tallies[1:1 + 2 * twos:2], tallies[2:2 + 2 * twos:2]
    room = jnp.minimum(giver - 1, reach - receiver)
    moved = jax.random.randint(jax.random.fold_in(stream_key, 1), (twos,), 0, 1 << 20) % (room + 1)
    tallies = tallies.at[1:1 + 2 * twos:2].set(giver - moved).at[2:2 + 2 * twos:2].set(receiver + moved)
    return tallies[jax.random.permutation(jax.random.fold_in(stream_key, 2), count)]


def bell_draw(key, extent, scale, reach, split=(), kind=jnp.bfloat16):
    entries = jax.random.normal(key, extent, jnp.float32) * scale
    if len(split) > 0:
        entries = steps_of(key, extent, split, -0.22, 0.18) * entries
    return jnp.clip(entries, min=-reach, max=reach).astype(kind)


def setup_inputs(seed: int = 0) -> dict:
    key_of = jax.random.split(jax.random.key(seed), 14)
    inputs = bell_draw(key_of[0], (ROW_LEN, ROWS, D), 1.0, 6.0, ((0, 32),))
    attn_gain = jnp.clip(1.0 + 0.15 * jax.random.normal(key_of[1], (D,), jnp.float32), 0.25, 1.75)
    w_query = bell_draw(key_of[2], (D, HEADS * FEAT), D ** -0.5, 0.125, ((1, 8),))
    w_key = bell_draw(key_of[3], (D, HEADS * FEAT), D ** -0.5, 0.125, ((1, 8),))
    w_value = bell_draw(key_of[4], (D, HEADS * VHEAD), D ** -0.5, 0.125, ((1, 8),))
    w_out = bell_draw(key_of[5], (HEADS * VHEAD, D), (D // 128) ** -0.5, 1.5, ((0, 8),))
    out_bias = bell_draw(key_of[6], (D,), 0.3, 1.5, (), jnp.float32)
    mlp_gain = jnp.clip(1.0 + 0.15 * jax.random.normal(key_of[7], (D,), jnp.float32), 0.25, 1.75)
    gate_weight = bell_draw(key_of[8], (D, FF), D ** -0.5, 0.125, ((1, 8),))
    up_weight = bell_draw(key_of[9], (D, FF), D ** -0.5, 0.125, ((1, 8),))
    down_weight = bell_draw(key_of[10], (FF, D), FF ** -0.5, 0.078125, ((0, 8),))
    cotangent = bell_draw(key_of[11], (ROW_LEN, ROWS, D), 1.0, 6.0, ((0, 32),))
    doc_lengths = jax.vmap(lambda own: ragged_sizes(own, DOCS, ROW_LEN, MOST, 2))(jax.random.split(key_of[12], ROWS)).reshape((ROWS, DOCS)).astype(jnp.int32)
    return {"inputs": inputs, "attn_gain": attn_gain, "w_query": w_query, "w_key": w_key, "w_value": w_value, "w_out": w_out, "out_bias": out_bias, "mlp_gain": mlp_gain, "gate_weight": gate_weight, "up_weight": up_weight, "down_weight": down_weight, "cotangent": cotangent, "doc_lengths": doc_lengths}


epsilon = 1e-05
root_half = 0.7071067811865476
exact_precision_flag = lax.Precision.HIGHEST

@jax.custom_vjp
def low(v):
    return lax.optimization_barrier(v.astype(jnp.bfloat16)).astype(jnp.float32)

@jax.custom_vjp
def reduced_precision_return(v):
    return v

def low_keep(v):
    return (low(v), None)

def low_pass(kept, grad):
    return (grad,)

def back_keep(v):
    return (v, None)

def back_low(kept, grad):
    return (low(grad),)
low.defvjp(low_keep, low_pass)
reduced_precision_return.defvjp(back_keep, back_low)

def features(inputs):
    halved = inputs * 0.5
    size_in = inputs.shape[-1]
    squares = (halved[..., :, None] * halved[..., None, :]).reshape(inputs.shape[:-1] + (size_in * size_in,)) * root_half
    return jnp.concatenate([jnp.ones(inputs.shape[:-1] + (1,), inputs.dtype), halved, squares], axis=-1)

def doc_layout(doc_lengths, group_begin, group_len):
    doc_ends = jnp.cumsum(doc_lengths, axis=-1).astype(jnp.int32)
    positions = group_begin + jnp.arange(group_len, dtype=jnp.int32)
    passed = (doc_ends[..., :, None] <= positions).astype(jnp.int32)
    doc_index = lax.optimization_barrier(jnp.sum(passed, axis=-2)).astype(jnp.int32)
    doc_begin = lax.optimization_barrier(jnp.sum(passed * doc_lengths[..., :, None], axis=-2)).astype(jnp.int32)
    return (doc_index, doc_begin)

def group_step(carried_in, pieces, lengths_row):
    state_prev, sum_prev = carried_in
    query_c, key_c, value_c, group_begin = pieces
    group_len = query_c.shape[0]
    doc_index, doc_begin = doc_layout(lengths_row, group_begin, group_len)
    carried = (doc_begin < group_begin).astype(jnp.float32)
    trailing = (doc_index == doc_index[-1]).astype(jnp.float32)
    restart = (doc_begin[-1] >= group_begin).astype(jnp.float32)
    positions = jnp.arange(group_len, dtype=jnp.int32)
    visible = (positions[None, :] <= positions[:, None]) & (doc_index[:, None] == doc_index[None, :])
    scores = reduced_precision_return(jnp.einsum('thf,uhf->htu', query_c, key_c, precision=exact_precision_flag) * 0.25)
    weights = low(jnp.where(visible[None], 1.0 + scores + 0.5 * scores * scores, 0.0))
    query_feat = low(features(query_c))
    key_feat = low(features(key_c))
    state_low = low(state_prev)
    numerator = jnp.einsum('htu,uhv->thv', weights, value_c, precision=exact_precision_flag)
    numerator = numerator + carried[:, None, None] * jnp.einsum('thf,hfv->thv', query_feat, state_low, precision=exact_precision_flag)
    numerator = reduced_precision_return(numerator)
    denominator = lax.optimization_barrier(jnp.sum(weights, axis=-1)).T + carried[:, None] * jnp.einsum('thf,hf->th', query_feat, sum_prev, precision=exact_precision_flag)
    result = numerator / denominator[:, :, None]
    trail_keys = key_feat * trailing[:, None, None]
    local_state = reduced_precision_return(jnp.einsum('thf,thv->hfv', trail_keys, value_c, precision=exact_precision_flag))
    local_sum = lax.optimization_barrier(jnp.sum(trail_keys, axis=0))
    state_next = local_state + (1.0 - restart) * state_prev
    sum_next = local_sum + (1.0 - restart) * sum_prev
    return ((state_next, sum_next), result)

def row_attention(query_r, key_r, value_r, lengths_row):
    row_len = query_r.shape[0]
    group_len = row_len // N_SEQ
    query_c = query_r.reshape(N_SEQ, group_len, HEADS, FEAT)
    key_c = key_r.reshape(N_SEQ, group_len, HEADS, FEAT)
    value_c = value_r.reshape(N_SEQ, group_len, HEADS, VHEAD)
    begins = (jnp.arange(N_SEQ, dtype=jnp.int32) * group_len).astype(jnp.int32)

    def stepper(carried_in, pieces):
        return group_step(carried_in, pieces, lengths_row)
    start_state = (jnp.zeros((HEADS, 1 + FEAT + FEAT * FEAT, VHEAD), jnp.float32), jnp.zeros((HEADS, 1 + FEAT + FEAT * FEAT), jnp.float32))
    _, results = lax.scan(jax.checkpoint(stepper), start_state, (query_c, key_c, value_c, begins))
    return results.reshape(row_len, HEADS, VHEAD)

def forward(inputs, attn_gain, w_query, w_key, w_value, w_out, out_bias, mlp_gain, gate_weight, up_weight, down_weight, doc_lengths):
    row_len = inputs.shape[0]
    row_count = inputs.shape[1]
    normed = low(inputs * lax.rsqrt(lax.optimization_barrier(jnp.mean(inputs * inputs, axis=-1, keepdims=True)) + epsilon) * attn_gain)
    queries = reduced_precision_return(low(jnp.einsum('trd,dc->trc', normed, w_query, precision=exact_precision_flag)))
    key_proj = reduced_precision_return(low(jnp.einsum('trd,dc->trc', normed, w_key, precision=exact_precision_flag)))
    value_proj = reduced_precision_return(low(jnp.einsum('trd,dc->trc', normed, w_value, precision=exact_precision_flag)))
    query_rows = jnp.transpose(queries.reshape(row_len, row_count, HEADS, FEAT), (1, 0, 2, 3))
    key_rows = jnp.transpose(key_proj.reshape(row_len, row_count, HEADS, FEAT), (1, 0, 2, 3))
    value_rows = jnp.transpose(value_proj.reshape(row_len, row_count, HEADS, VHEAD), (1, 0, 2, 3))

    def row_bundle(bundle):
        return row_attention(bundle[0], bundle[1], bundle[2], bundle[3])
    results = lax.map(row_bundle, (query_rows, key_rows, value_rows, doc_lengths))
    attended = low(jnp.transpose(results, (1, 0, 2, 3)).reshape(row_len, row_count, HEADS * VHEAD))
    attn_branch = reduced_precision_return(jnp.einsum('trc,cd->trd', attended, w_out, precision=exact_precision_flag))
    middle = inputs + attn_branch + out_bias
    second_normed = low(middle * lax.rsqrt(lax.optimization_barrier(jnp.mean(middle * middle, axis=-1, keepdims=True)) + epsilon) * mlp_gain)
    gate_projected = reduced_precision_return(jnp.einsum('czm,my->czy', second_normed, gate_weight, precision=exact_precision_flag))
    up_projected = reduced_precision_return(jnp.einsum('czm,my->czy', second_normed, up_weight, precision=exact_precision_flag))
    hidden_activation = low(jax.nn.silu(gate_projected) * up_projected)
    perceptron_branch = reduced_precision_return(jnp.einsum('nzh,hi->nzi', hidden_activation, down_weight, precision=exact_precision_flag))
    return middle + perceptron_branch

def reference(inputs, attn_gain, w_query, w_key, w_value, w_out, out_bias, mlp_gain, gate_weight, up_weight, down_weight, cotangent, doc_lengths):
    floats = [arr.astype(jnp.float32) for arr in (inputs, attn_gain, w_query, w_key, w_value, w_out, out_bias, mlp_gain, gate_weight, up_weight, down_weight)]

    def wrapped(*params):
        return forward(*params, doc_lengths)
    result, pullback = jax.vjp(wrapped, *floats)
    gradients = pullback(cotangent.astype(jnp.float32))
    return (result.astype(jnp.bfloat16), gradients[0].astype(jnp.bfloat16), gradients[1], gradients[2], gradients[3], gradients[4], gradients[5], gradients[6], gradients[7], gradients[8], gradients[9], gradients[10])
```

```python
import functools

import jax
import jax.numpy as jnp
import numpy as np
from jax import lax
from jax.experimental import pallas as pl
from jax.experimental.pallas import tpu as pltpu
from jax.sharding import Mesh
from jax.sharding import PartitionSpec as P

FEAT = 16
EPS = 1e-05
ROOT_HALF = 0.7071067811865476
TILE = 256
AUX = 136
BF = jnp.bfloat16
F32 = jnp.float32
MESH_ID = pl.DeviceIdType.MESH
NT = (((1,), (1,)), ((), ()))
TN = (((0,), (0,)), ((), ()))


def dot(a, b, dims=(((1,), (0,)), ((), ()))):
    return lax.dot_general(a, b, dims, preferred_element_type=F32)


def feature_tables(nh):
    cols = [(None, None)] + [(i, None) for i in range(FEAT)]
    cols += [(i, j) for i in range(FEAT) for j in range(i, FEAT)]
    pick_a = np.zeros((2 * nh, 128, TILE), np.float32)
    pick_b = np.zeros((2 * nh, 128, TILE), np.float32)
    rows = np.zeros((8, TILE), np.float32)
    for c, (i, j) in enumerate(cols):
        scale = 1.0 if i is None else 0.5 if j is None else 0.25 * ROOT_HALF
        rows[0, c] = 1.0 if i is None else 0.0
        rows[1, c] = 1.0 if j is None else 0.0
        rows[2, c] = scale * (2.0 if j is not None and i != j else 1.0)
        rows[3, c] = scale
        for n in range(2 * nh):
            if i is not None:
                pick_a[n, FEAT * n + i, c] = 1.0
            if j is not None:
                pick_b[n, FEAT * n + j, c] = 1.0
    align = np.zeros((4 * nh, 128, 128), np.float32)
    for h in range(nh):
        for f in range(FEAT):
            q, k = FEAT * h + f, FEAT * (nh + h) + f
            align[4 * h, q, f] = 0.25
            align[4 * h + 1, k, f] = 1.0
            align[4 * h + 2, k, q] = 0.25
            align[4 * h + 3, q, k] = 0.25
    to_low = lambda a: jnp.asarray(a, BF)
    return to_low(pick_a), to_low(pick_b), jnp.asarray(rows), to_low(align)


def begin_at(lens, row, docs, position, start_block):
    start = -start_block
    found = start + position * 0
    for j in range(docs):
        if j:
            start = start + lens[row, j - 1]
            found = jnp.where(start <= position, start, found)
    return found


def chain_weights(lens, row, docs, block, blocks, length, backward):
    out, alive = [], None
    for k in range(1, blocks):
        source = block + k if backward else block - k
        inside = (source < blocks) if backward else (source >= 0)
        here = inside if alive is None else jnp.logical_and(alive, inside)
        out.append(jnp.where(here, 1.0, 0.0).astype(F32))
        first = begin_at(lens, row, docs, length - 1, source * length)
        passes = first < 0
        alive = passes if alive is None else jnp.logical_and(alive, passes)
    return out


def lane_iota(shape):
    return lax.broadcasted_iota(jnp.int32, shape, len(shape) - 1)


def row_iota(shape):
    return lax.broadcasted_iota(jnp.int32, shape, len(shape) - 2)


def with_ones(v, lanes=(0, 1)):
    side = lane_iota(v.shape)
    ones = jnp.where((side >= lanes[0]) & (side <= lanes[1]), 1.0, 0.0).astype(BF)
    return jnp.concatenate([v, ones], axis=1)


def split_sum(state, total, third):
    rows = row_iota(state.shape)
    high = total.astype(BF).astype(F32)
    low = total - high
    out = jnp.where(rows < 128, state, 0.0)
    out = jnp.where(rows == 128, high, out)
    if third:
        out = jnp.where(rows == 129, high, out)
        out = jnp.where(rows == 130, low, out)
    else:
        out = jnp.where(rows == 129, low, out)
    return out.astype(BF)


def flat(ref):
    x = ref[...]
    return x.reshape(x.shape[0] * x.shape[2], x.shape[3])


def picks(qk, pa, pb, rows, n):
    a = dot(qk, pa[n]) + rows[0:1, :]
    b = dot(qk, pb[n]) + rows[1:2, :]
    return a, b


def state_kernel(nh, vd, docs, lens, meta, x_ref, pa, pb, rows, out):
    row = pl.program_id(0)
    x = flat(x_ref)
    length = x.shape[0]
    qk = x[:, nh * vd :]
    last = begin_at(lens, row, docs, length - 1, meta[0] * length)
    trail = row_iota((length, 2 * 128)) >= last
    for h in range(nh):
        a, b = picks(qk, pa, pb, rows, nh + h)
        kf = (a * b * rows[3:4, :]).astype(BF)
        va = jnp.where(trail, with_ones(x[:, h * vd : (h + 1) * vd]).astype(F32), 0.0).astype(BF)
        st = dot(va, kf, TN)[:AUX]
        out[0, h] = split_sum(st, st[128:129], False)


def intra_kernel(nh, vd, docs, lens, meta, x_ref, align, num_out, den_out):
    row = pl.program_id(0)
    x = flat(x_ref)
    length = x.shape[0]
    qk = x[:, nh * vd :]
    one16 = jnp.where(lane_iota((1, 128)) == FEAT, 1.0, 0.0)
    tile = min(TILE, length)
    dens = [jnp.zeros((tile, 128), F32) for _ in range(length // tile)]
    for h in range(nh):
        qa = (dot(qk, align[4 * h]) + one16).astype(BF)
        ka = (dot(qk, align[4 * h + 1]) + one16).astype(BF)
        va = with_ones(x[:, h * vd : (h + 1) * vd])
        for t in range(length // tile):
            lo, hi = t * tile, (t + 1) * tile
            s1 = dot(qa[lo:hi], ka[:hi], NT)
            w = 0.5 * (s1 * s1) + 0.5
            pos = lo + row_iota((tile, 1))
            beg = begin_at(lens, row, docs, pos, meta[0] * length)
            kpos = lane_iota(w.shape)
            w = jnp.where((kpos >= beg) & (kpos <= pos), w, 0.0).astype(BF)
            acc = dot(w, va[:hi])
            num_out[0, lo:hi, h * vd : (h + 1) * vd] = acc[:, :vd]
            lane = lane_iota((tile, 128))
            dens[t] = jnp.where(lane == h, acc[:, vd : vd + 1], dens[t])
    for t in range(length // tile):
        den_out[0, t * tile : (t + 1) * tile, :] = dens[t]


def gather_states(sts, weights, h):
    total = None
    for st, w in zip(sts, weights):
        part = st[0, h].astype(F32) * w
        total = part if total is None else total + part
    return total


def attend_kernel(nh, vd, docs, blocks, lens, meta, x_ref, num, den, pa, pb, rows, *rest):
    sts, (att_out, den_out, st_out) = rest[: blocks - 1], rest[blocks - 1 :]
    row = pl.program_id(0)
    x = flat(x_ref)
    length = x.shape[0]
    qk = x[:, nh * vd :]
    weights = chain_weights(lens, row, docs, meta[0], blocks, length, False)
    pos = row_iota((length, 1))
    carried = begin_at(lens, row, docs, pos, meta[0] * length) < 0
    lane = lane_iota((length, 128))
    dens = den[0]
    for h in range(nh):
        st = gather_states(sts, weights, h)
        st = split_sum(st, st[128:129] + st[129:130], True)
        st_out[0, h] = st
        a, b = picks(qk, pa, pb, rows, h)
        qf = (a * b * rows[2:3, :]).astype(BF)
        inter = dot(qf, st, NT)
        more = jnp.where(carried, inter[:, :vd], 0.0)
        more_den = jnp.where(carried, inter[:, 128:129] + inter[:, 130:131], 0.0)
        total = dens[:, h : h + 1] + more_den
        value = (num[0, :, h * vd : (h + 1) * vd] + more) / total
        att_out[:, 0, :, h * vd : (h + 1) * vd] = value.astype(BF).reshape(
            att_out.shape[0], att_out.shape[2], vd
        )
        dens = jnp.where(lane == h, total, dens)
    den_out[0] = dens


def back_state_kernel(nh, vd, docs, lens, meta, x_ref, ga_ref, att_ref, den, pa, pb, rows, gn_out, out):
    row = pl.program_id(0)
    x, ga, att = flat(x_ref), flat(ga_ref), flat(att_ref)
    length = x.shape[0]
    qk = x[:, nh * vd :]
    pos = row_iota((length, 1))
    carried = begin_at(lens, row, docs, pos, meta[0] * length) < 0
    side = lane_iota((length, 128))
    for h in range(nh):
        cut = slice(h * vd, (h + 1) * vd)
        inv = 1.0 / den[0, :, h : h + 1]
        gah = ga[:, cut].astype(F32) * inv
        gd = -jnp.sum(gah * att[:, cut].astype(F32), axis=1, keepdims=True)
        high = gd.astype(BF).astype(F32)
        aux = jnp.where((side == 0) | (side == 2), high, jnp.where(side == 1, gd - high, 0.0))
        gn = jnp.concatenate([gah, aux], axis=1)
        gn_out[0, :, h * 256 : (h + 1) * 256] = gn.astype(BF)
        a, b = picks(qk, pa, pb, rows, h)
        qf = (a * b * rows[2:3, :]).astype(BF)
        st = dot(jnp.where(carried, gn, 0.0).astype(BF), qf, TN)[:AUX]
        out[0, h] = split_sum(st, st[128:129] + st[129:130], False)


def back_intra_kernel(
    nh, vd, docs, lens, meta, x_ref, gn_ref, st_ref, pa, pb, rows, align, gqk_out, gv_out
):
    row = pl.program_id(0)
    x = flat(x_ref)
    length = x.shape[0]
    qk = x[:, nh * vd :]
    one16 = jnp.where(lane_iota((1, 128)) == FEAT, 1.0, 0.0)
    tile = min(TILE, length)
    pos = row_iota((length, 1))
    carried = begin_at(lens, row, docs, pos, meta[0] * length) < 0
    gqk = None
    for h in range(nh):
        qa = (dot(qk, align[4 * h]) + one16).astype(BF)
        ka = (dot(qk, align[4 * h + 1]) + one16).astype(BF)
        k_at_q = dot(qk, align[4 * h + 2]).astype(BF)
        q_at_k = dot(qk, align[4 * h + 3]).astype(BF)
        va = with_ones(x[:, h * vd : (h + 1) * vd])
        gn = gn_ref[0, :, h * 256 : (h + 1) * 256]
        st = st_ref[0, h]
        gqf = jnp.where(carried, dot(gn[:, :AUX], st), 0.0) * rows[2:3, :]
        a, b = picks(qk, pa, pb, rows, h)
        part = dot((gqf * b).astype(BF), pa[h], NT) + dot((gqf * a).astype(BF), pb[h], NT)
        gqk = part if gqk is None else gqk + part
        gk_parts = []
        gq_parts = [None] * (length // tile)
        for t in range(length // tile):
            lo, hi = t * tile, (t + 1) * tile
            s1 = dot(ka[lo:hi], qa[lo:], NT)
            w = 0.5 * (s1 * s1) + 0.5
            kpos = lo + row_iota((tile, 1))
            qpos = lo + lane_iota((1, length - lo))
            beg = begin_at(lens, row, docs, qpos, meta[0] * length)
            see = (kpos >= beg) & (kpos <= qpos)
            gw = dot(va[lo:hi], gn[lo:], NT)
            gs = jnp.where(see, gw * s1, 0.0).astype(BF)
            w = jnp.where(see, w, 0.0).astype(BF)
            gv_out[0, lo:hi, h * vd : (h + 1) * vd] = dot(w, gn[lo:, :vd])
            gk_parts.append(dot(gs, q_at_k[lo:]))
            gq = dot(gs, k_at_q[lo:hi], TN)
            for u in range(t, length // tile):
                piece = gq[(u - t) * tile : (u - t + 1) * tile]
                gq_parts[u] = piece if gq_parts[u] is None else gq_parts[u] + piece
        gqk = gqk + jnp.concatenate(gk_parts, axis=0) + jnp.concatenate(gq_parts, axis=0)
    gqk_out[0] = gqk


def back_key_kernel(nh, vd, docs, blocks, lens, meta, x_ref, gqk_ref, gv_ref, pa, pb, rows, *rest):
    sts, (out,) = rest[: blocks - 1], rest[blocks - 1 :]
    row = pl.program_id(0)
    x = flat(x_ref)
    length = x.shape[0]
    qk = x[:, nh * vd :]
    weights = chain_weights(lens, row, docs, meta[0], blocks, length, True)
    last = begin_at(lens, row, docs, length - 1, meta[0] * length)
    trail = row_iota((length, 1)) >= last
    gqk = gqk_ref[0]
    shape = (out.shape[0], out.shape[2])
    for h in range(nh):
        st = gather_states(sts, weights, h)
        st = split_sum(st, st[128:129] + st[129:130], False)
        va = with_ones(x[:, h * vd : (h + 1) * vd])
        gkf = jnp.where(trail, dot(va[:, :AUX], st), 0.0) * rows[3:4, :]
        a, b = picks(qk, pa, pb, rows, nh + h)
        gqk = gqk + dot((gkf * b).astype(BF), pa[nh + h], NT)
        gqk = gqk + dot((gkf * a).astype(BF), pb[nh + h], NT)
        kf = (a * b * rows[3:4, :]).astype(BF)
        more = jnp.where(trail, dot(kf, st[:vd], NT), 0.0)
        gv = gv_ref[0, :, h * vd : (h + 1) * vd] + more
        out[:, 0, :, h * vd : (h + 1) * vd] = gv.astype(BF).reshape(shape + (vd,))
    out[:, 0, :, nh * vd :] = gqk.astype(BF).reshape(shape + (128,))


def row_call(kernel, rows_n, scalars, ins, outs, flops):
    def spec(shape, dim):
        if dim is None:
            return pl.BlockSpec(shape, lambda r, *_: (0,) * len(shape))
        block = tuple(1 if d == dim else n for d, n in enumerate(shape))
        return pl.BlockSpec(block, lambda r, *_: tuple(r if d == dim else 0 for d in range(len(shape))))

    moved = sum(a.size * a.dtype.itemsize for a, _ in ins)
    moved += sum(int(np.prod(s)) * np.dtype(t).itemsize for s, t, _ in outs)
    return pl.pallas_call(
        kernel,
        out_shape=tuple(jax.ShapeDtypeStruct(s, t) for s, t, _ in outs),
        grid_spec=pltpu.PrefetchScalarGridSpec(
            num_scalar_prefetch=len(scalars),
            grid=(rows_n,),
            in_specs=[spec(a.shape, d) for a, d in ins],
            out_specs=[spec(s, d) for s, t, d in outs],
        ),
        compiler_params=pltpu.CompilerParams(vmem_limit_bytes=56 * 1024 * 1024),
        cost_estimate=pl.CostEstimate(flops=int(flops), bytes_accessed=int(moved), transcendentals=0),
    )(*scalars, *[a for a, _ in ins])


def exchange_kernel(to_blocks, width, src, dst, ssem, rsem, lsem):
    s, a, b = lax.axis_index("seq"), lax.axis_index("ha"), lax.axis_index("hb")
    size_a, size_b = lax.axis_size("ha"), lax.axis_size("hb")
    count = size_a * size_b
    bar = pltpu.get_barrier_semaphore()
    same = s == a

    def copy(k):
        base = a if to_blocks else s
        pa = lax.rem(base + k // size_b, size_a)
        pb = lax.rem(b + k % size_b, size_b)
        piece = pa * size_b + pb
        if to_blocks:
            source = src.at[:, pl.ds(pl.multiple_of(piece * width, 128), width)]
            place = dst.at[a * size_b + b]
            target, sender = (pa, s, pb), (a, pa, pb)
        else:
            source = src.at[piece]
            place = dst.at[:, pl.ds(pl.multiple_of((s * size_b + b) * width, 128), width)]
            target, sender = (a, pa, pb), (pa, s, pb)
        remote = functools.partial(
            pltpu.make_async_remote_copy,
            src_ref=source,
            dst_ref=place,
            send_sem=ssem.at[k],
            recv_sem=rsem.at[k],
            device_id=target,
            device_id_type=MESH_ID,
        )
        return sender, remote, functools.partial(pltpu.make_async_copy, source, place, lsem)

    def either(k, remote, local):
        if k:
            remote()
        else:
            pl.when(jnp.logical_not(same))(remote)
            pl.when(same)(local)

    for k in range(count):
        sender = copy(k)[0]
        signal = functools.partial(pl.semaphore_signal, bar, 1, device_id=sender, device_id_type=MESH_ID)
        either(k, signal, lambda: None)
    pl.semaphore_wait(bar, jnp.where(same, count - 1, count))
    for k in range(count):
        _, remote, local = copy(k)
        either(k, lambda: remote().start(), lambda: local().start())
    for k in range(count):
        _, remote, local = copy(k)
        either(k, lambda: remote().wait(), lambda: local().wait())


def exchange(x, to_blocks, width, collective):
    count = lax.axis_size("ha") * lax.axis_size("hb")
    tokens = x.shape[0] if to_blocks else x.shape[1]
    shape = (count, tokens, width) if to_blocks else (tokens, count * width)
    return pl.pallas_call(
        functools.partial(exchange_kernel, to_blocks, width),
        out_shape=jax.ShapeDtypeStruct(shape, x.dtype),
        in_specs=[pl.BlockSpec(memory_space=pl.ANY)],
        out_specs=pl.BlockSpec(memory_space=pl.ANY),
        scratch_shapes=[
            pltpu.SemaphoreType.DMA((count,)),
            pltpu.SemaphoreType.DMA((count,)),
            pltpu.SemaphoreType.DMA,
        ],
        compiler_params=pltpu.CompilerParams(collective_id=collective, has_side_effects=True),
        cost_estimate=pl.CostEstimate(flops=0, bytes_accessed=x.size * 2, transcendentals=0),
    )(x)


def transpose_perm(size):
    return [(s * size + z, z * size + s) for s in range(size) for z in range(size)]


def swap_home(x):
    return lax.ppermute(x, ("seq", "ha"), transpose_perm(lax.axis_size("seq")))


def chain_pieces(x, backward):
    size = lax.axis_size("ha")
    out = []
    for k in range(1, size):
        if backward:
            perm = [(i, i - k) for i in range(k, size)]
        else:
            perm = [(i, i + k) for i in range(size - k)]
        out.append(lax.ppermute(x, "ha", perm))
    return out


def sum_home(x):
    size = lax.axis_size("ha")
    a = lax.axis_index("ha")
    total = None
    for k in range(size):
        block = lax.dynamic_index_in_dim(x, lax.rem(a + k, size), 0, False)
        perm = [(s * size + z, ((z + k) % size) * size + s) for s in range(size) for z in range(size)]
        got = lax.ppermute(block, ("seq", "ha"), perm).astype(F32)
        total = got if total is None else total + got
    return total


def rms_scale(x):
    return lax.rsqrt(jnp.mean(x * x, axis=-1, keepdims=True) + EPS)


def on_device(
    inputs,
    attn_gain,
    w_query,
    w_key,
    w_value,
    w_out,
    out_bias,
    mlp_gain,
    gate_weight,
    up_weight,
    down_weight,
    cotangent,
    doc_lengths,
):
    blocks = lax.axis_size("seq")
    group = ("seq", "hb")
    count = blocks * lax.axis_size("hb")
    sub_len, rows_n, width = inputs.shape
    docs = doc_lengths.shape[1]
    nh = w_query.shape[1] // FEAT
    vd = w_value.shape[1] // nh
    vw = nh * vd
    xw = vw + 128
    length = sub_len * count
    tokens = rows_n * sub_len
    meta = lax.axis_index("ha").astype(jnp.int32).reshape(1)
    pa, pb, frows, align = feature_tables(nh)
    scalars = (doc_lengths, meta)

    x = jnp.transpose(inputs, (1, 0, 2)).astype(F32)
    cot = jnp.transpose(cotangent, (1, 0, 2))
    scale_one = rms_scale(x)
    normed_one = x * scale_one
    normed_low = (normed_one * attn_gain).astype(BF)
    normed_full = lax.all_gather(swap_home(normed_low), group, axis=0)
    pad = jnp.zeros((128 - 2 * nh * FEAT, width), BF)
    w_in = swap_home(jnp.concatenate([w_value.T, w_query.T, w_key.T, pad], axis=0))
    w_out_home = swap_home(w_out)
    gate_t, up_t, down = swap_home(gate_weight.T), swap_home(up_weight.T), swap_home(down_weight)
    w_out_full = lax.all_gather(w_out_home, group, axis=0, tiled=True)
    w_in_full = lax.all_gather(w_in, group, axis=0, tiled=True)

    qkv = jnp.einsum("grtd,cd->grtc", normed_full, w_in, preferred_element_type=F32).astype(BF)
    pair = nh * rows_n * length * length
    (states,) = row_call(
        functools.partial(state_kernel, nh, vd, docs),
        rows_n,
        scalars,
        [(qkv, 1), (pa, None), (pb, None), (frows, None)],
        [((rows_n, nh, AUX, TILE), BF, 0)],
        nh * rows_n * length * 256 * 256 * 4,
    )
    earlier = chain_pieces(states, False)
    num, den = row_call(
        functools.partial(intra_kernel, nh, vd, docs),
        rows_n,
        scalars,
        [(qkv, 1), (align, None)],
        [((rows_n, length, vw), F32, 0), ((rows_n, length, 128), F32, 0)],
        pair * 256 * 4,
    )
    att, den, state_in = row_call(
        functools.partial(attend_kernel, nh, vd, docs, blocks),
        rows_n,
        scalars,
        [(qkv, 1), (num, 0), (den, 0), (pa, None), (pb, None), (frows, None)]
        + [(e, 0) for e in earlier],
        [
            ((count, rows_n, sub_len, vw), BF, 1),
            ((rows_n, length, 128), F32, 0),
            ((rows_n, nh, AUX, TILE), BF, 0),
        ],
        nh * rows_n * length * 256 * 256 * 6,
    )
    attended = exchange(att.reshape(count, tokens, vw), False, vw, 0)
    attn_branch = dot(attended, w_out_full).reshape(rows_n, sub_len, width)
    middle = x + attn_branch + out_bias
    scale_two = rms_scale(middle)
    normed_two = middle * scale_two
    normed_two_low = (normed_two * mlp_gain).astype(BF)

    n2f = lax.all_gather(normed_two_low, group, axis=0).reshape(count * tokens, width)
    cotf = lax.all_gather(cot, group, axis=0).reshape(count * tokens, width)
    gate = dot(n2f, gate_t, NT)
    up = dot(n2f, up_t, NT)
    sig = jax.nn.sigmoid(gate)
    hidden = (gate * sig * up).astype(BF)
    grad_hidden = dot(cotf, down, NT)
    grad_gate = (grad_hidden * up * sig * (1.0 + gate * (1.0 - sig))).astype(BF)
    grad_up = (grad_hidden * gate * sig).astype(BF)
    grad_two = (dot(grad_gate, gate_t) + dot(grad_up, up_t)).astype(BF)
    grad_two = (
        lax.psum_scatter(grad_two, group, scatter_dimension=0, tiled=True)
        .astype(F32)
        .reshape(rows_n, sub_len, width)
    )
    branch = dot(hidden, down).astype(BF)
    branch = (
        lax.psum_scatter(branch, group, scatter_dimension=0, tiled=True)
        .astype(F32)
        .reshape(rows_n, sub_len, width)
    )
    output = (middle + branch).astype(BF)

    gain_two_part = jnp.sum(grad_two * normed_two, axis=(0, 1))
    scaled = grad_two * mlp_gain
    grad_middle = cot.astype(F32) + scale_two * (
        scaled - normed_two * jnp.mean(scaled * normed_two, axis=-1, keepdims=True)
    )
    bias_part = jnp.sum(grad_middle, axis=(0, 1))
    grad_branch = grad_middle.astype(BF)

    grad_att = dot(grad_branch.reshape(tokens, width), w_out_full, NT).astype(BF)
    grad_att = exchange(grad_att, True, vw, 1).reshape(count, rows_n, sub_len, vw)
    gn, grad_states = row_call(
        functools.partial(back_state_kernel, nh, vd, docs),
        rows_n,
        scalars,
        [(qkv, 1), (grad_att, 1), (att, 1), (den, 0), (pa, None), (pb, None), (frows, None)],
        [((rows_n, length, nh * 256), BF, 0), ((rows_n, nh, AUX, TILE), BF, 0)],
        nh * rows_n * length * 256 * 256 * 4,
    )
    later = chain_pieces(grad_states, True)
    gqk, gv = row_call(
        functools.partial(back_intra_kernel, nh, vd, docs),
        rows_n,
        scalars,
        [(qkv, 1), (gn, 0), (state_in, 0), (pa, None), (pb, None), (frows, None), (align, None)],
        [((rows_n, length, 128), F32, 0), ((rows_n, length, vw), F32, 0)],
        pair * 256 * 8,
    )
    (gqkv,) = row_call(
        functools.partial(back_key_kernel, nh, vd, docs, blocks),
        rows_n,
        scalars,
        [(qkv, 1), (gqk, 0), (gv, 0), (pa, None), (pb, None), (frows, None)] + [(e, 0) for e in later],
        [((count, rows_n, sub_len, xw), BF, 1)],
        nh * rows_n * length * 256 * 256 * 6,
    )
    grad_in = exchange(gqkv.reshape(count, tokens, xw), False, xw, 2)
    grad_one = dot(grad_in, w_in_full).reshape(rows_n, sub_len, width)
    gain_one_part = jnp.sum(grad_one * normed_one, axis=(0, 1))
    scaled = grad_one * attn_gain
    input_grad = (
        grad_middle
        + scale_one * (scaled - normed_one * jnp.mean(scaled * normed_one, axis=-1, keepdims=True))
    ).astype(BF)

    flat_tokens = count * tokens
    grad_w_in = dot(gqkv.reshape(flat_tokens, xw), normed_full.reshape(flat_tokens, width), TN)
    grad_w_in = sum_home(
        jnp.transpose(grad_w_in.astype(BF).reshape(xw, blocks, width // blocks), (1, 0, 2))
    )
    branch_full = lax.all_gather(swap_home(grad_branch), group, axis=0).reshape(flat_tokens, width)
    grad_w_out = dot(att.reshape(flat_tokens, vw), branch_full, TN)
    grad_w_out = sum_home(
        jnp.transpose(grad_w_out.astype(BF).reshape(vw, blocks, width // blocks), (1, 0, 2))
    )

    def ff_grad(a, b):
        part = dot(a, b, TN).astype(BF)
        part = lax.psum_scatter(part, "ha", scatter_dimension=1, tiled=True)
        return swap_home(part).astype(F32)

    grad_gate_w = ff_grad(grad_gate, n2f)
    grad_up_w = ff_grad(grad_up, n2f)
    grad_down_w = ff_grad(hidden, cotf)
    vectors = jnp.stack([gain_one_part, bias_part, gain_two_part])
    vectors = lax.psum_scatter(vectors, ("seq", "ha", "hb"), scatter_dimension=1, tiled=True)
    qk_cut = vw + nh * FEAT
    return (
        jnp.transpose(output, (1, 0, 2)),
        jnp.transpose(input_grad, (1, 0, 2)),
        vectors[0],
        grad_w_in[vw:qk_cut].T,
        grad_w_in[qk_cut : qk_cut + nh * FEAT].T,
        grad_w_in[:vw].T,
        grad_w_out,
        vectors[1],
        vectors[2],
        grad_gate_w.T,
        grad_up_w.T,
        grad_down_w,
    )


def solution(mesh):
    seq, head = mesh.shape["seq"], mesh.shape["head"]
    inner = Mesh(mesh.devices.reshape(seq, seq, head // seq), ("seq", "ha", "hb"))
    every, heads = ("seq", "ha", "hb"), ("ha", "hb")
    placed = (
        P(every, None, None),
        P(),
        P(None, heads),
        P(None, heads),
        P(None, heads),
        P(heads, None),
        P(),
        P(),
        P(None, heads),
        P(None, heads),
        P(heads, None),
        P(every, None, None),
        P(),
    )
    return jax.shard_map(
        on_device,
        mesh=inner,
        in_specs=placed,
        out_specs=(
            P(every, None, None),
            P(every, None, None),
            P(every),
            P("seq", heads),
            P("seq", heads),
            P("seq", heads),
            P(heads, "seq"),
            P(every),
            P(every),
            P("seq", heads),
            P("seq", heads),
            P(heads, "seq"),
        ),
        check_vma=False,
    )
```

```python
import functools

import jax
import jax.numpy as jnp
import numpy as np
from jax import lax
from jax.experimental import pallas as pl
from jax.experimental.pallas import tpu as pltpu
from jax.sharding import Mesh
from jax.sharding import PartitionSpec as P

FEAT = 16
EPS = 1e-05
ROOT_HALF = 0.7071067811865476
TILE = 256
AUX = 136
BF = jnp.bfloat16
F32 = jnp.float32
MESH_ID = pl.DeviceIdType.MESH
NT = (((1,), (1,)), ((), ()))
TN = (((0,), (0,)), ((), ()))


def dot(a, b, dims=(((1,), (0,)), ((), ()))):
    return lax.dot_general(a, b, dims, preferred_element_type=F32)


def feature_tables(nh):
    cols = [(None, None)] + [(i, None) for i in range(FEAT)]
    cols += [(i, j) for i in range(FEAT) for j in range(i, FEAT)]
    pick_a = np.zeros((2 * nh, 128, TILE), np.float32)
    pick_b = np.zeros((2 * nh, 128, TILE), np.float32)
    rows = np.zeros((8, TILE), np.float32)
    for c, (i, j) in enumerate(cols):
        scale = 1.0 if i is None else 0.5 if j is None else 0.25 * ROOT_HALF
        rows[0, c] = 1.0 if i is None else 0.0
        rows[1, c] = 1.0 if j is None else 0.0
        rows[2, c] = scale * (2.0 if j is not None and i != j else 1.0)
        rows[3, c] = scale
        for n in range(2 * nh):
            if i is not None:
                pick_a[n, FEAT * n + i, c] = 1.0
            if j is not None:
                pick_b[n, FEAT * n + j, c] = 1.0
    align = np.zeros((4 * nh, 128, 128), np.float32)
    for h in range(nh):
        for f in range(FEAT):
            q, k = FEAT * h + f, FEAT * (nh + h) + f
            align[4 * h, q, f] = 0.25
            align[4 * h + 1, k, f] = 1.0
            align[4 * h + 2, k, q] = 0.25
            align[4 * h + 3, q, k] = 0.25
    to_low = lambda a: jnp.asarray(a, BF)
    return to_low(pick_a), to_low(pick_b), jnp.asarray(rows), to_low(align)


def begin_at(lens, row, docs, position, start_block):
    start = -start_block
    found = start + position * 0
    for j in range(docs):
        if j:
            start = start + lens[row, j - 1]
            found = jnp.where(start <= position, start, found)
    return found


def chain_weights(lens, row, docs, block, blocks, length, backward):
    out, alive = [], None
    for k in range(1, blocks):
        source = block + k if backward else block - k
        inside = (source < blocks) if backward else (source >= 0)
        here = inside if alive is None else jnp.logical_and(alive, inside)
        out.append(jnp.where(here, 1.0, 0.0).astype(F32))
        first = begin_at(lens, row, docs, length - 1, source * length)
        passes = first < 0
        alive = passes if alive is None else jnp.logical_and(alive, passes)
    return out


def lane_iota(shape):
    return lax.broadcasted_iota(jnp.int32, shape, len(shape) - 1)


def row_iota(shape):
    return lax.broadcasted_iota(jnp.int32, shape, len(shape) - 2)


def with_ones(v, lanes=(0, 1)):
    side = lane_iota(v.shape)
    ones = jnp.where((side >= lanes[0]) & (side <= lanes[1]), 1.0, 0.0).astype(BF)
    return jnp.concatenate([v, ones], axis=1)


def split_sum(state, total, third):
    rows = row_iota(state.shape)
    high = total.astype(BF).astype(F32)
    low = total - high
    out = jnp.where(rows < 128, state, 0.0)
    out = jnp.where(rows == 128, high, out)
    if third:
        out = jnp.where(rows == 129, high, out)
        out = jnp.where(rows == 130, low, out)
    else:
        out = jnp.where(rows == 129, low, out)
    return out.astype(BF)


def flat(ref):
    x = ref[...]
    return x.reshape(x.shape[0] * x.shape[2], x.shape[3])


def picks(qk, pa, pb, rows, n):
    a = dot(qk, pa[n]) + rows[0:1, :]
    b = dot(qk, pb[n]) + rows[1:2, :]
    return a, b


def state_kernel(nh, vd, docs, lens, meta, x_ref, pa, pb, rows, out):
    row = pl.program_id(0)
    x = flat(x_ref)
    length = x.shape[0]
    qk = x[:, nh * vd :]
    last = begin_at(lens, row, docs, length - 1, meta[0] * length)
    trail = row_iota((length, 2 * 128)) >= last
    for h in range(nh):
        a, b = picks(qk, pa, pb, rows, nh + h)
        kf = (a * b * rows[3:4, :]).astype(BF)
        va = jnp.where(trail, with_ones(x[:, h * vd : (h + 1) * vd]).astype(F32), 0.0).astype(BF)
        st = dot(va, kf, TN)[:AUX]
        out[0, h] = split_sum(st, st[128:129], False)


def intra_kernel(nh, vd, docs, lens, meta, x_ref, align, num_out, den_out):
    row = pl.program_id(0)
    x = flat(x_ref)
    length = x.shape[0]
    qk = x[:, nh * vd :]
    one16 = jnp.where(lane_iota((1, 128)) == FEAT, 1.0, 0.0)
    tile = min(TILE, length)
    dens = [jnp.zeros((tile, 128), F32) for _ in range(length // tile)]
    for h in range(nh):
        qa = (dot(qk, align[4 * h]) + one16).astype(BF)
        ka = (dot(qk, align[4 * h + 1]) + one16).astype(BF)
        va = with_ones(x[:, h * vd : (h + 1) * vd])
        for t in range(length // tile):
            lo, hi = t * tile, (t + 1) * tile
            s1 = dot(qa[lo:hi], ka[:hi], NT)
            w = 0.5 * (s1 * s1) + 0.5
            pos = lo + row_iota((tile, 1))
            beg = begin_at(lens, row, docs, pos, meta[0] * length)
            kpos = lane_iota(w.shape)
            w = jnp.where((kpos >= beg) & (kpos <= pos), w, 0.0).astype(BF)
            acc = dot(w, va[:hi])
            num_out[0, lo:hi, h * vd : (h + 1) * vd] = acc[:, :vd]
            lane = lane_iota((tile, 128))
            dens[t] = jnp.where(lane == h, acc[:, vd : vd + 1], dens[t])
    for t in range(length // tile):
        den_out[0, t * tile : (t + 1) * tile, :] = dens[t]


def gather_states(sts, weights, h):
    total = None
    for st, w in zip(sts, weights):
        part = st[0, h].astype(F32) * w
        total = part if total is None else total + part
    return total


def attend_kernel(nh, vd, docs, blocks, lens, meta, x_ref, num, den, pa, pb, rows, *rest):
    sts, (att_out, den_out, st_out) = rest[: blocks - 1], rest[blocks - 1 :]
    row = pl.program_id(0)
    x = flat(x_ref)
    length = x.shape[0]
    qk = x[:, nh * vd :]
    weights = chain_weights(lens, row, docs, meta[0], blocks, length, False)
    pos = row_iota((length, 1))
    carried = begin_at(lens, row, docs, pos, meta[0] * length) < 0
    lane = lane_iota((length, 128))
    dens = den[0]
    for h in range(nh):
        st = gather_states(sts, weights, h)
        st = split_sum(st, st[128:129] + st[129:130], True)
        st_out[0, h] = st
        a, b = picks(qk, pa, pb, rows, h)
        qf = (a * b * rows[2:3, :]).astype(BF)
        inter = dot(qf, st, NT)
        more = jnp.where(carried, inter[:, :vd], 0.0)
        more_den = jnp.where(carried, inter[:, 128:129] + inter[:, 130:131], 0.0)
        total = dens[:, h : h + 1] + more_den
        value = (num[0, :, h * vd : (h + 1) * vd] + more) / total
        att_out[:, 0, :, h * vd : (h + 1) * vd] = value.astype(BF).reshape(
            att_out.shape[0], att_out.shape[2], vd
        )
        dens = jnp.where(lane == h, total, dens)
    den_out[0] = dens


def back_state_kernel(nh, vd, docs, lens, meta, x_ref, ga_ref, att_ref, den, pa, pb, rows, gn_out, out):
    row = pl.program_id(0)
    x, ga, att = flat(x_ref), flat(ga_ref), flat(att_ref)
    length = x.shape[0]
    qk = x[:, nh * vd :]
    pos = row_iota((length, 1))
    carried = begin_at(lens, row, docs, pos, meta[0] * length) < 0
    side = lane_iota((length, 128))
    for h in range(nh):
        cut = slice(h * vd, (h + 1) * vd)
        inv = 1.0 / den[0, :, h : h + 1]
        gah = ga[:, cut].astype(F32) * inv
        gd = -jnp.sum(gah * att[:, cut].astype(F32), axis=1, keepdims=True)
        high = gd.astype(BF).astype(F32)
        aux = jnp.where((side == 0) | (side == 2), high, jnp.where(side == 1, gd - high, 0.0))
        gn = jnp.concatenate([gah, aux], axis=1)
        gn_out[0, :, h * 256 : (h + 1) * 256] = gn.astype(BF)
        a, b = picks(qk, pa, pb, rows, h)
        qf = (a * b * rows[2:3, :]).astype(BF)
        st = dot(jnp.where(carried, gn, 0.0).astype(BF), qf, TN)[:AUX]
        out[0, h] = split_sum(st, st[128:129] + st[129:130], False)


def back_intra_kernel(
    nh, vd, docs, lens, meta, x_ref, gn_ref, st_ref, pa, pb, rows, align, gqk_out, gv_out
):
    row = pl.program_id(0)
    x = flat(x_ref)
    length = x.shape[0]
    qk = x[:, nh * vd :]
    one16 = jnp.where(lane_iota((1, 128)) == FEAT, 1.0, 0.0)
    tile = min(TILE, length)
    pos = row_iota((length, 1))
    carried = begin_at(lens, row, docs, pos, meta[0] * length) < 0
    gqk = None
    for h in range(nh):
        qa = (dot(qk, align[4 * h]) + one16).astype(BF)
        ka = (dot(qk, align[4 * h + 1]) + one16).astype(BF)
        k_at_q = dot(qk, align[4 * h + 2]).astype(BF)
        q_at_k = dot(qk, align[4 * h + 3]).astype(BF)
        va = with_ones(x[:, h * vd : (h + 1) * vd])
        gn = gn_ref[0, :, h * 256 : (h + 1) * 256]
        st = st_ref[0, h]
        gqf = jnp.where(carried, dot(gn[:, :AUX], st), 0.0) * rows[2:3, :]
        a, b = picks(qk, pa, pb, rows, h)
        part = dot((gqf * b).astype(BF), pa[h], NT) + dot((gqf * a).astype(BF), pb[h], NT)
        gqk = part if gqk is None else gqk + part
        gk_parts = []
        gq_parts = [None] * (length // tile)
        for t in range(length // tile):
            lo, hi = t * tile, (t + 1) * tile
            s1 = dot(ka[lo:hi], qa[lo:], NT)
            w = 0.5 * (s1 * s1) + 0.5
            kpos = lo + row_iota((tile, 1))
            qpos = lo + lane_iota((1, length - lo))
            beg = begin_at(lens, row, docs, qpos, meta[0] * length)
            see = (kpos >= beg) & (kpos <= qpos)
            gw = dot(va[lo:hi], gn[lo:], NT)
            gs = jnp.where(see, gw * s1, 0.0).astype(BF)
            w = jnp.where(see, w, 0.0).astype(BF)
            gv_out[0, lo:hi, h * vd : (h + 1) * vd] = dot(w, gn[lo:, :vd])
            gk_parts.append(dot(gs, q_at_k[lo:]))
            gq = dot(gs, k_at_q[lo:hi], TN)
            for u in range(t, length // tile):
                piece = gq[(u - t) * tile : (u - t + 1) * tile]
                gq_parts[u] = piece if gq_parts[u] is None else gq_parts[u] + piece
        gqk = gqk + jnp.concatenate(gk_parts, axis=0) + jnp.concatenate(gq_parts, axis=0)
    gqk_out[0] = gqk


def back_key_kernel(nh, vd, docs, blocks, lens, meta, x_ref, gqk_ref, gv_ref, pa, pb, rows, *rest):
    sts, (out,) = rest[: blocks - 1], rest[blocks - 1 :]
    row = pl.program_id(0)
    x = flat(x_ref)
    length = x.shape[0]
    qk = x[:, nh * vd :]
    weights = chain_weights(lens, row, docs, meta[0], blocks, length, True)
    last = begin_at(lens, row, docs, length - 1, meta[0] * length)
    trail = row_iota((length, 1)) >= last
    gqk = gqk_ref[0]
    shape = (out.shape[0], out.shape[2])
    for h in range(nh):
        st = gather_states(sts, weights, h)
        st = split_sum(st, st[128:129] + st[129:130], False)
        va = with_ones(x[:, h * vd : (h + 1) * vd])
        gkf = jnp.where(trail, dot(va[:, :AUX], st), 0.0) * rows[3:4, :]
        a, b = picks(qk, pa, pb, rows, nh + h)
        gqk = gqk + dot((gkf * b).astype(BF), pa[nh + h], NT)
        gqk = gqk + dot((gkf * a).astype(BF), pb[nh + h], NT)
        kf = (a * b * rows[3:4, :]).astype(BF)
        more = jnp.where(trail, dot(kf, st[:vd], NT), 0.0)
        gv = gv_ref[0, :, h * vd : (h + 1) * vd] + more
        out[:, 0, :, h * vd : (h + 1) * vd] = gv.astype(BF).reshape(shape + (vd,))
    out[:, 0, :, nh * vd :] = gqk.astype(BF).reshape(shape + (128,))


def row_call(kernel, rows_n, scalars, ins, outs, flops):
    def spec(shape, dim):
        if dim is None:
            return pl.BlockSpec(shape, lambda r, *_: (0,) * len(shape))
        block = tuple(1 if d == dim else n for d, n in enumerate(shape))
        return pl.BlockSpec(block, lambda r, *_: tuple(r if d == dim else 0 for d in range(len(shape))))

    moved = sum(a.size * a.dtype.itemsize for a, _ in ins)
    moved += sum(int(np.prod(s)) * np.dtype(t).itemsize for s, t, _ in outs)
    return pl.pallas_call(
        kernel,
        out_shape=tuple(jax.ShapeDtypeStruct(s, t) for s, t, _ in outs),
        grid_spec=pltpu.PrefetchScalarGridSpec(
            num_scalar_prefetch=len(scalars),
            grid=(rows_n,),
            in_specs=[spec(a.shape, d) for a, d in ins],
            out_specs=[spec(s, d) for s, t, d in outs],
        ),
        compiler_params=pltpu.CompilerParams(vmem_limit_bytes=56 * 1024 * 1024),
        cost_estimate=pl.CostEstimate(flops=int(flops), bytes_accessed=int(moved), transcendentals=0),
    )(*scalars, *[a for a, _ in ins])


SEQ = ("sy", "sc")
HEAD = ("ha", "hb")


def here():
    return tuple(lax.axis_index(n) for n in ("sy", "sc", "ha", "hb"))


def remote(src, dst, ssem, rsem, k, device):
    return pltpu.make_async_remote_copy(
        src_ref=src,
        dst_ref=dst,
        send_sem=ssem.at[k],
        recv_sem=rsem.at[k],
        device_id=device,
        device_id_type=MESH_ID,
    )


def greet(devices):
    bar = pltpu.get_barrier_semaphore()
    for device in devices:
        pl.semaphore_signal(bar, 1, device_id=device, device_id_type=MESH_ID)
    pl.semaphore_wait(bar, len(devices))


def exchange_kernel(to_blocks, width, src, dst, ssem, rsem, lsem):
    sy, sc, a, b = here()
    size_a, size_b = lax.axis_size("ha"), lax.axis_size("hb")
    count = size_a * size_b
    me = a * size_b + b

    def peer(k):
        return lax.rem(a + k // size_b, size_a), lax.rem(b + k % size_b, size_b)

    def ends(k):
        pa, pb = peer(k)
        piece = pa * size_b + pb
        if to_blocks:
            return src.at[:, pl.ds(pl.multiple_of(piece * width, 128), width)], dst.at[me]
        return src.at[piece], dst.at[:, pl.ds(pl.multiple_of(me * width, 128), width)]

    def at(k):
        pa, pb = peer(k)
        return sy, sc, pa, pb

    greet([at(k) for k in range(1, count)])
    copies = [remote(*ends(k), ssem, rsem, k - 1, at(k)) for k in range(1, count)]
    for copy in copies:
        copy.start()
    local = pltpu.make_async_copy(*ends(0), lsem)
    local.start()
    local.wait()
    for copy in copies:
        copy.wait()


def exchange(x, to_blocks, width, collective):
    count = lax.axis_size("ha") * lax.axis_size("hb")
    tokens = x.shape[0] if to_blocks else x.shape[1]
    shape = (count, tokens, width) if to_blocks else (tokens, count * width)
    return pl.pallas_call(
        functools.partial(exchange_kernel, to_blocks, width),
        out_shape=jax.ShapeDtypeStruct(shape, x.dtype),
        in_specs=[pl.BlockSpec(memory_space=pl.ANY)],
        out_specs=pl.BlockSpec(memory_space=pl.ANY),
        scratch_shapes=[
            pltpu.SemaphoreType.DMA((count - 1,)),
            pltpu.SemaphoreType.DMA((count - 1,)),
            pltpu.SemaphoreType.DMA,
        ],
        compiler_params=pltpu.CompilerParams(collective_id=collective, has_side_effects=True),
        cost_estimate=pl.CostEstimate(flops=0, bytes_accessed=x.size * 500, transcendentals=0),
    )(x)


def gather_kernel(arrays, *refs):
    srcs, dsts, (ssem, rsem, lsem) = refs[:arrays], refs[arrays : 2 * arrays], refs[2 * arrays :]
    sy, sc, a, b = here()
    size = lax.axis_size("ha")
    to_up, to_down, to_side = (sy, sc, a + 1, b), (sy, sc, a - 1, b), (sy, sc, a, 1 - b)
    has_up, has_down = a < size - 1, a > 0
    bar = pltpu.get_barrier_semaphore()

    def signal(device):
        pl.semaphore_signal(bar, 1, device_id=device, device_id_type=MESH_ID)

    def send(n, k, pa, device):
        ref = dsts[n].at[pa * 2 + b]
        return remote(ref, ref, ssem, rsem, 3 * size * n + k, device)

    local = [pltpu.make_async_copy(s, d.at[a * 2 + b], lsem.at[n]) for n, (s, d) in enumerate(zip(srcs, dsts))]
    for copy in local:
        copy.start()
    pl.when(has_up)(lambda: signal(to_up))
    pl.when(has_down)(lambda: signal(to_down))
    signal(to_side)
    pl.semaphore_wait(bar, 1 + has_up.astype(jnp.int32) + has_down.astype(jnp.int32))
    for copy in local:
        copy.wait()

    def spread(n, k, pa, up, down):
        if up:
            pl.when(has_up)(lambda: send(n, k, pa, to_up).start())
        if down:
            pl.when(has_down)(lambda: send(n, size + k, pa, to_down).start())
        send(n, 2 * size + pa, pa, to_side).start()

    for n in range(arrays):
        spread(n, 0, a, True, True)
    for k in range(1, size):
        for n in range(arrays):

            @pl.when(a - k >= 0)
            def _():
                send(n, k - 1, a - k, to_side).wait_recv()
                spread(n, k, a - k, True, False)

            @pl.when(a + k < size)
            def _():
                send(n, size + k - 1, a + k, to_side).wait_recv()
                spread(n, k, a + k, False, True)

    for n in range(arrays):
        for k in range(size):
            ref = dsts[n].at[k * 2 + 1 - b]
            remote(ref, ref, ssem, rsem, 3 * size * n + 2 * size + k, to_side).wait_recv()
        for k in range(size):
            send(n, 2 * size + k, k, to_side).wait_send()
            pl.when(jnp.logical_and(has_up, a - k >= 0))(lambda: send(n, k, a - k, to_side).wait_send())
            pl.when(jnp.logical_and(has_down, a + k < size))(
                lambda: send(n, size + k, a + k, to_side).wait_send()
            )


def gather_block(xs, collective):
    if (lax.axis_size("ha"), lax.axis_size("hb")) != (4, 2):
        return [lax.all_gather(x, HEAD, axis=0) for x in xs]
    n = len(xs)
    return pl.pallas_call(
        functools.partial(gather_kernel, n),
        out_shape=[jax.ShapeDtypeStruct((8,) + x.shape, x.dtype) for x in xs],
        in_specs=[pl.BlockSpec(memory_space=pl.ANY)] * n,
        out_specs=[pl.BlockSpec(memory_space=pl.ANY)] * n,
        scratch_shapes=[
            pltpu.SemaphoreType.DMA((12 * n,)),
            pltpu.SemaphoreType.DMA((12 * n,)),
            pltpu.SemaphoreType.DMA((n,)),
        ],
        compiler_params=pltpu.CompilerParams(collective_id=collective, has_side_effects=True),
        cost_estimate=pl.CostEstimate(flops=0, bytes_accessed=xs[0].size * 600, transcendentals=0),
    )(*xs)


def swap(x, axis):
    return lax.ppermute(x, axis, [(0, 1), (1, 0)])


def chain_pieces(x, backward):
    size = lax.axis_size("sy") * 2
    out = []
    for k in range(1, size):
        if backward:
            perm = [(i, i - k) for i in range(k, size)]
        else:
            perm = [(i, i + k) for i in range(size - k)]
        out.append(lax.ppermute(x, SEQ, perm))
    return out


def tie(x, *after):
    return lax.optimization_barrier((x, *jax.tree.leaves(after)))[0]


def my_columns(x):
    size = x.shape[1] // (lax.axis_size("sy") * 2)
    place = lax.axis_index("sy") * 2 + lax.axis_index("sc")
    return lax.dynamic_slice_in_dim(x, place * size, size, 1)


def seq_pieces(x):
    if lax.axis_size("sy") != 2:
        return list(lax.all_gather(x, SEQ, axis=0))
    along_y = swap(x, "sy")
    other, other_y = swap(x, "sc"), swap(along_y, "sc")
    return [x, along_y, other, other_y]


def piece_places(count):
    if lax.axis_size("sy") != 2:
        return list(range(count))
    y, c = lax.axis_index("sy"), lax.axis_index("sc")
    return [y * 2 + c, (1 - y) * 2 + c, y * 2 + 1 - c, (1 - y) * 2 + 1 - c]


def by_columns(a, pieces):
    parts = [dot(a, p) for p in pieces]
    if lax.axis_size("sy") == 2:
        y, c = lax.axis_index("sy") == 0, lax.axis_index("sc") == 0
        rows = [(jnp.where(y, parts[k], parts[k + 1]), jnp.where(y, parts[k + 1], parts[k])) for k in (0, 2)]
        parts = []
        for own, other in zip(*rows):
            parts += [jnp.where(c, own, other), jnp.where(c, other, own)]
    return jnp.concatenate(parts, axis=1)


def by_columns_back(a, pieces):
    size = pieces[0].shape[1]
    total = None
    for p, place in zip(pieces, piece_places(len(pieces))):
        part = dot(lax.dynamic_slice_in_dim(a, place * size, size, 1), p, NT)
        total = part if total is None else total + part
    return total


def unit_window(x, size):
    units = x.shape[0]
    window = -(-units // (size * 16)) * 16
    place = lax.axis_index("sy") * 2 + lax.axis_index("sc")
    start = jnp.minimum(place * window, units - window)
    part = lax.dynamic_slice_in_dim(x, start, window, 0)
    fresh = start + lax.broadcasted_iota(jnp.int32, part.shape, 0) >= place * window
    return jnp.where(fresh, part, jnp.zeros_like(part))


def windows_joined(parts, units):
    size, window = parts.shape[0], parts.shape[1]
    pieces = []
    for i in range(size):
        start = min(i * window, units - window)
        pieces.append(parts[i, max(i * window - start, 0) :])
    return jnp.concatenate(pieces, axis=0)


def ff_kernel(meta, n2, cot, mine, theirs, *rest):
    gg_out, gu_out, hid_out, n2_out, cot_out, part_out, acc = rest[-7:]
    shard = pl.program_id(0)

    def work(w, first):
        x, c = n2[...], cot[...]
        units, width = w.shape[0] * w.shape[2], w.shape[3]
        w_gate, w_up, w_down = (w[:, i].reshape(units, width) for i in range(3))
        gate, up, gh = dot(x, w_gate, NT), dot(x, w_up, NT), dot(c, w_down, NT)
        sig = jax.nn.sigmoid(gate)
        act = gate * sig
        hid_out[0, 0] = (act * up).astype(BF)
        gg = (gh * up * (sig + act * (1.0 - sig))).astype(BF)
        gu = (gh * act).astype(BF)
        gg_out[0, 0] = gg
        gu_out[0, 0] = gu
        back = dot(gg, w_gate) + dot(gu, w_up)
        if first:
            acc[...] = back
            n2_out[0] = x
            cot_out[0] = c
        else:
            part_out[...] = (acc[...] + back).astype(BF)

    @pl.when(shard == 0)
    def _():
        work(mine, True)

    @pl.when(shard == 1)
    def _():
        work(theirs, False)


def ff_chunk(n2, cot, mine, theirs, place, chunks, kept):
    tokens, width = n2.shape
    units = mine.shape[0] * mine.shape[2]
    keep = jax.ShapeDtypeStruct((2, chunks, tokens, units), BF)
    held_shape = jax.ShapeDtypeStruct((chunks, tokens, width), BF)
    whole = pl.BlockSpec((tokens, width), lambda i, m: (0, 0))
    weights = pl.BlockSpec(mine.shape, lambda i, m: (0, 0, 0, 0), pipeline_mode=pl.Buffered(1))
    piece = pl.BlockSpec((1, 1, tokens, units), lambda i, m: (i, m[0], 0, 0))
    held = pl.BlockSpec((1, tokens, width), lambda i, m: (m[0], 0, 0))
    old = [] if kept is None else list(kept)
    return pl.pallas_call(
        ff_kernel,
        out_shape=(keep, keep, keep, held_shape, held_shape, jax.ShapeDtypeStruct((tokens, width), BF)),
        grid_spec=pltpu.PrefetchScalarGridSpec(
            num_scalar_prefetch=1,
            grid=(2,),
            in_specs=[whole, whole, weights, weights] + [pl.BlockSpec(memory_space=pl.ANY)] * len(old),
            out_specs=[piece, piece, piece, held, held, whole],
            scratch_shapes=[pltpu.VMEM((tokens, width), F32)],
        ),
        input_output_aliases={5 + i: i for i in range(len(old))},
        compiler_params=pltpu.CompilerParams(vmem_limit_bytes=58 * 1024 * 1024),
        cost_estimate=pl.CostEstimate(
            flops=tokens * width * units * 20,
            bytes_accessed=12 * units * width + 8 * tokens * width,
            transcendentals=0,
        ),
    )(place, n2, cot, mine, theirs, *old)


def branch_kernel(hidden, mine, theirs, out):
    width = out.shape[1]
    part = dot(hidden[0, 0], mine[:, 0].reshape(-1, width)) + dot(hidden[1, 0], theirs[:, 0].reshape(-1, width))
    out[...] = part.astype(BF)


def branch_product(hidden, mine, theirs):
    _, chunks, tokens, units = hidden.shape
    width = mine.shape[3]
    weights = pl.BlockSpec(
        (mine.shape[0], 1) + mine.shape[2:], lambda i: (0, 2, 0, 0), pipeline_mode=pl.Buffered(1)
    )
    return pl.pallas_call(
        branch_kernel,
        out_shape=jax.ShapeDtypeStruct((chunks * tokens, width), BF),
        grid=(chunks,),
        in_specs=[pl.BlockSpec((2, 1, tokens, units), lambda i: (0, i, 0, 0)), weights, weights],
        out_specs=pl.BlockSpec((tokens, width), lambda i: (i, 0)),
        compiler_params=pltpu.CompilerParams(vmem_limit_bytes=40 * 1024 * 1024),
        cost_estimate=pl.CostEstimate(
            flops=chunks * tokens * units * width * 4, bytes_accessed=12 * units * width, transcendentals=0
        ),
    )(hidden, mine, theirs)


QUAD = ("sy", "hb")


def ring_gather(x):
    half = x.shape[0] // 2
    from_x, from_y = swap(x, "hb"), swap(x, "sy")
    across = jnp.concatenate([swap(from_y[:half], "hb"), swap(from_x[half:], "sy")], axis=0)
    return x, from_x, from_y, across


def add_low(a, b):
    return (a.astype(F32) + b.astype(F32)).astype(BF)


def ring_sum(parts, meanwhile=lambda stage: ()):
    own, to_x, to_y, across = parts
    half = own.shape[0] // 2
    via_x, via_y = swap(across[:half], "hb"), swap(across[half:], "sy")
    x_low, y_high = swap(to_x[:half], "hb"), swap(to_y[half:], "sy")
    work = meanwhile(0)
    via_x, via_y = tie(via_x, *work), tie(via_y, *work)
    y_low = swap(add_low(to_y[:half], via_x), "sy")
    x_high = swap(add_low(to_x[half:], via_y), "hb")
    work = meanwhile(1)
    y_low, x_high = tie(y_low, *work), tie(x_high, *work)
    low = own[:half].astype(F32) + x_low.astype(F32) + y_low.astype(F32)
    high = own[half:].astype(F32) + x_high.astype(F32) + y_high.astype(F32)
    return jnp.concatenate([low, high], axis=0)


def quad_gather(x):
    if (lax.axis_size("sy"), lax.axis_size("hb")) == (2, 2):
        return ring_gather(x)
    return (lax.all_gather(x, QUAD, axis=0, tiled=True),)


def quad_sum(parts, meanwhile=lambda stage: ()):
    if len(parts) == 4:
        return ring_sum(parts, meanwhile)
    for stage in (0, 1):
        meanwhile(stage)
    return lax.psum_scatter(parts[0], QUAD, scatter_dimension=0, tiled=True).astype(F32)


def ff_group(n2, cots, mine, theirs):
    kept, parts = None, []
    for i, (chunk, cot) in enumerate(zip(quad_gather(n2), cots)):
        place = jnp.full((1,), i, jnp.int32)
        *kept, part = ff_chunk(chunk, cot, mine, theirs, place, len(cots), kept)
        parts.append(part)
    grads, branch = [], []
    flat = [k.reshape((2, -1, k.shape[-1]) if k.ndim == 4 else (-1, k.shape[-1])) for k in kept]
    pairs = [(flat[0], flat[3]), (flat[1], flat[3]), (flat[2], flat[4])]

    def meanwhile(stage):
        if stage == 0:
            grads.extend(swap(dot(a[1], b, TN).astype(BF), "sc") for a, b in pairs)
            return grads
        for i, (a, b) in enumerate(pairs):
            grads[i] = (dot(a[0], b, TN) + grads[i].astype(F32)).astype(BF)
        branch.append(branch_product(kept[2], mine, theirs))
        return grads + branch

    return quad_sum(parts, meanwhile), grads, branch[0]


def rms_scale(x):
    return lax.rsqrt(jnp.mean(x * x, axis=-1, keepdims=True) + EPS)


def on_device(
    inputs,
    attn_gain,
    w_query,
    w_key,
    w_value,
    w_out,
    out_bias,
    mlp_gain,
    gate_weight,
    up_weight,
    down_weight,
    cotangent,
    doc_lengths,
):
    every = ("sy", "sc", "ha", "hb")
    blocks = lax.axis_size("sy") * 2
    size_a, size_b = lax.axis_size("ha"), lax.axis_size("hb")
    count = size_a * size_b
    sub_len, rows_n, width = inputs.shape
    docs = doc_lengths.shape[1]
    nh = w_query.shape[1] // FEAT
    vd = w_value.shape[1] // nh
    vw = nh * vd
    xw = vw + 128
    length = sub_len * count
    tokens = rows_n * sub_len
    meta = (lax.axis_index("sy") * 2 + lax.axis_index("sc")).astype(jnp.int32).reshape(1)
    pa, pb, frows, align = feature_tables(nh)
    scalars = (doc_lengths, meta)

    x = jnp.transpose(inputs, (1, 0, 2)).astype(F32)
    cot = jnp.transpose(cotangent, (1, 0, 2))
    scale_one = rms_scale(x)
    normed_one = x * scale_one
    pad = jnp.zeros((128 - 2 * nh * FEAT, width), BF)
    w_in = jnp.concatenate([w_value.T, w_query.T, w_key.T, pad], axis=0)
    units = down_weight.shape[0]
    windows = [unit_window(w, blocks) for w in (gate_weight.T, up_weight.T, down_weight)]
    w_in_piece = my_columns(w_in)
    to_fetch = jnp.concatenate(windows + [w_in_piece.reshape(-1, width)], axis=0)
    normed_full, w_out_piece = gather_block([(normed_one * attn_gain).astype(BF), my_columns(w_out)], 3)
    fetched = lax.all_gather(tie(to_fetch, normed_full), "ha", axis=0)
    w_out_pieces = seq_pieces(w_out_piece.reshape(-1, w_out_piece.shape[-1]))
    window = windows[0].shape[0]
    mine = fetched[:, : 3 * window].reshape(size_a, 3, window, width)

    qkv = jnp.einsum("grtd,cd->grtc", normed_full, w_in, preferred_element_type=F32).astype(BF)
    pair = nh * rows_n * length * length
    (states,) = row_call(
        functools.partial(state_kernel, nh, vd, docs),
        rows_n,
        scalars,
        [(qkv, 1), (pa, None), (pb, None), (frows, None)],
        [((rows_n, nh, AUX, TILE), BF, 0)],
        nh * rows_n * length * 256 * 256 * 4,
    )
    earlier = chain_pieces(states, False)
    num, den = row_call(
        functools.partial(intra_kernel, nh, vd, docs),
        rows_n,
        scalars,
        [(qkv, 1), (align, None)],
        [((rows_n, length, vw), F32, 0), ((rows_n, length, 128), F32, 0)],
        pair * 256 * 4,
    )
    att, den, state_in = row_call(
        functools.partial(attend_kernel, nh, vd, docs, blocks),
        rows_n,
        scalars,
        [(qkv, 1), (tie(num, w_out_pieces), 0), (den, 0), (pa, None), (pb, None), (frows, None)]
        + [(e, 0) for e in earlier],
        [
            ((count, rows_n, sub_len, vw), BF, 1),
            ((rows_n, length, 128), F32, 0),
            ((rows_n, nh, AUX, TILE), BF, 0),
        ],
        nh * rows_n * length * 256 * 256 * 6,
    )
    flat_cot = tie(cot.reshape(tokens, width), earlier)
    cots = quad_gather(flat_cot)
    attended = exchange(tie(att, cots).reshape(count, tokens, vw), False, vw, 0)
    attn_branch = by_columns(attended, w_out_pieces).reshape(rows_n, sub_len, width)
    middle = x + attn_branch + out_bias
    scale_two = rms_scale(middle)
    normed_two = middle * scale_two
    normed_two_low = (normed_two * mlp_gain).astype(BF)

    theirs = swap(tie(mine, attended), "sc")
    n2 = normed_two_low.reshape(tokens, width)
    grad_two, ff_grads, branch = ff_group(n2, cots, mine, theirs)
    grad_two = grad_two.reshape(rows_n, sub_len, width)
    gain_two_part = jnp.sum(grad_two * normed_two, axis=(0, 1))
    scaled = grad_two * mlp_gain
    grad_middle = cot.astype(F32) + scale_two * (
        scaled - normed_two * jnp.mean(scaled * normed_two, axis=-1, keepdims=True)
    )
    bias_part = jnp.sum(grad_middle, axis=(0, 1))
    grad_branch = grad_middle.astype(BF)

    flat_branch = grad_branch.reshape(tokens, width)
    grad_att = by_columns_back(flat_branch, w_out_pieces).astype(BF)
    step = branch.shape[0] // len(cots)
    branch = tie(branch, grad_att)
    branch = quad_sum([branch[i * step : (i + 1) * step] for i in range(len(cots))])
    output = (middle + branch.reshape(rows_n, sub_len, width)).astype(BF)
    grad_att = exchange(grad_att, True, vw, 1).reshape(count, rows_n, sub_len, vw)
    near = tie(fetched[:, 3 * window :].reshape((size_a,) + w_in_piece.shape), grad_att)
    side = lax.axis_index("hb") == 0
    aside = swap(near, "hb")
    w_in_piece = jnp.stack([jnp.where(side, near, aside), jnp.where(side, aside, near)], axis=1)
    w_in_pieces = seq_pieces(w_in_piece.reshape(-1, w_in_piece.shape[-1]))
    gn, grad_states = row_call(
        functools.partial(back_state_kernel, nh, vd, docs),
        rows_n,
        scalars,
        [(qkv, 1), (grad_att, 1), (att, 1), (den, 0), (pa, None), (pb, None), (frows, None)],
        [((rows_n, length, nh * 256), BF, 0), ((rows_n, nh, AUX, TILE), BF, 0)],
        nh * rows_n * length * 256 * 256 * 4,
    )
    later = chain_pieces(grad_states, True)
    gqk, gv = row_call(
        functools.partial(back_intra_kernel, nh, vd, docs),
        rows_n,
        scalars,
        [(qkv, 1), (gn, 0), (state_in, 0), (pa, None), (pb, None), (frows, None), (align, None)],
        [((rows_n, length, 128), F32, 0), ((rows_n, length, vw), F32, 0)],
        pair * 256 * 8,
    )
    (gqkv,) = row_call(
        functools.partial(back_key_kernel, nh, vd, docs, blocks),
        rows_n,
        scalars,
        [(qkv, 1), (gqk, 0), (gv, 0), (pa, None), (pb, None), (frows, None)] + [(e, 0) for e in later],
        [((count, rows_n, sub_len, xw), BF, 1)],
        nh * rows_n * length * 256 * 256 * 6,
    )
    grad_in = exchange(gqkv.reshape(count, tokens, xw), False, xw, 2)
    grad_one = by_columns(grad_in, w_in_pieces).reshape(rows_n, sub_len, width)
    gain_one_part = jnp.sum(grad_one * normed_one, axis=(0, 1))
    scaled = grad_one * attn_gain
    input_grad = (
        grad_middle
        + scale_one * (scaled - normed_one * jnp.mean(scaled * normed_one, axis=-1, keepdims=True))
    ).astype(BF)

    def seq_sum(a, b):
        part = dot(a, b, TN).astype(BF).reshape(a.shape[1], blocks // 2, 2, width // blocks)
        core = lax.axis_index("sc")
        ours, given = (
            lax.dynamic_index_in_dim(part, i, 2, False).reshape(a.shape[1], -1) for i in (core, 1 - core)
        )
        part = add_low(ours, swap(given, "sc"))
        if lax.axis_size("sy") != 2:
            return lax.psum_scatter(part, "sy", scatter_dimension=1, tiled=True)
        y = lax.axis_index("sy")
        size = width // blocks
        kept, sent = (lax.dynamic_slice_in_dim(part, i * size, size, 1) for i in (y, 1 - y))
        return (kept.astype(F32) + swap(sent, "sy").astype(F32)).astype(BF)

    flat_tokens = count * tokens
    grad_w_in = seq_sum(gqkv.reshape(flat_tokens, xw), normed_full.reshape(flat_tokens, width)).astype(F32)
    grad_w_out = seq_sum(attended, flat_branch)

    def ff_home(part):
        part = lax.psum_scatter(part, "ha", scatter_dimension=0, tiled=True)
        part = part.reshape(part.shape[0], blocks, width // blocks)
        part = lax.all_to_all(jnp.transpose(part, (1, 0, 2)), SEQ, 0, 0, tiled=True)
        return windows_joined(part.astype(F32), units)

    grad_gate_w, grad_up_w, grad_down_w = (ff_home(g) for g in ff_grads)
    grad_w_out = tie(grad_w_out, grad_down_w)
    grad_w_out = lax.psum_scatter(grad_w_out, HEAD, scatter_dimension=0, tiled=True).astype(F32)
    vectors = jnp.stack([gain_one_part, bias_part, gain_two_part])
    if (lax.axis_size("sy"), size_a, size_b) == (2, 4, 2):
        vectors = vectors.reshape(3, 2, 2, 4, 2, -1)
        for axis, where in (("sc", 2), ("sy", 1), ("hb", 4)):
            i = lax.axis_index(axis)
            given = swap(lax.dynamic_slice_in_dim(vectors, 1 - i, 1, where), axis)
            vectors = lax.dynamic_slice_in_dim(vectors, i, 1, where) + given
        vectors = vectors.reshape(3, 4, -1)
        i = lax.axis_index("ha")
        total = lax.dynamic_index_in_dim(vectors, i, 1, False)
        for k in range(1, 4):
            piece = lax.dynamic_index_in_dim(vectors, lax.rem(i + k, 4), 1, False)
            total = total + lax.ppermute(piece, "ha", [(z, (z + k) % 4) for z in range(4)])
        vectors = total
    else:
        vectors = lax.psum_scatter(vectors, every, scatter_dimension=1, tiled=True)
    qk_cut = vw + nh * FEAT
    return (
        jnp.transpose(output, (1, 0, 2)),
        jnp.transpose(input_grad, (1, 0, 2)),
        vectors[0],
        grad_w_in[vw:qk_cut].T,
        grad_w_in[qk_cut : qk_cut + nh * FEAT].T,
        grad_w_in[:vw].T,
        grad_w_out,
        vectors[1],
        vectors[2],
        grad_gate_w.T,
        grad_up_w.T,
        grad_down_w,
    )


def solution(mesh):
    seq, head = mesh.shape["seq"], mesh.shape["head"]
    inner = Mesh(mesh.devices.reshape(seq // 2, 2, seq, head // seq), ("sy", "sc", "ha", "hb"))
    every, heads = ("sy", "sc", "ha", "hb"), ("ha", "hb")
    placed = (
        P(every, None, None),
        P(),
        P(None, heads),
        P(None, heads),
        P(None, heads),
        P(heads, None),
        P(),
        P(),
        P(None, heads),
        P(None, heads),
        P(heads, None),
        P(every, None, None),
        P(),
    )
    return jax.shard_map(
        on_device,
        mesh=inner,
        in_specs=placed,
        out_specs=(
            P(every, None, None),
            P(every, None, None),
            P(every),
            P(SEQ, heads),
            P(SEQ, heads),
            P(SEQ, heads),
            P(heads, SEQ),
            P(every),
            P(every),
            P(SEQ, heads),
            P(SEQ, heads),
            P(heads, SEQ),
        ),
        check_vma=False,
    )
```

```python
import functools

import jax
import jax.numpy as jnp
import numpy as np
from jax import lax
from jax.experimental import pallas as pl
from jax.experimental.pallas import tpu as pltpu
from jax.sharding import Mesh
from jax.sharding import PartitionSpec as P

FEAT = 16
EPS = 1e-05
ROOT_HALF = 0.7071067811865476
TILE = 256
AUX = 136
BF = jnp.bfloat16
F32 = jnp.float32
MESH_ID = pl.DeviceIdType.MESH
NT = (((1,), (1,)), ((), ()))
TN = (((0,), (0,)), ((), ()))


def dot(a, b, dims=(((1,), (0,)), ((), ()))):
    return lax.dot_general(a, b, dims, preferred_element_type=F32)


def feature_tables(nh):
    cols = [(None, None)] + [(i, None) for i in range(FEAT)]
    cols += [(i, j) for i in range(FEAT) for j in range(i, FEAT)]
    pick_a = np.zeros((2 * nh, 128, TILE), np.float32)
    pick_b = np.zeros((2 * nh, 128, TILE), np.float32)
    rows = np.zeros((8, TILE), np.float32)
    for c, (i, j) in enumerate(cols):
        scale = 1.0 if i is None else 0.5 if j is None else 0.25 * ROOT_HALF
        rows[0, c] = 1.0 if i is None else 0.0
        rows[1, c] = 1.0 if j is None else 0.0
        rows[2, c] = scale * (2.0 if j is not None and i != j else 1.0)
        rows[3, c] = scale
        for n in range(2 * nh):
            if i is not None:
                pick_a[n, FEAT * n + i, c] = 1.0
            if j is not None:
                pick_b[n, FEAT * n + j, c] = 1.0
    align = np.zeros((4 * nh, 128, 128), np.float32)
    for h in range(nh):
        for f in range(FEAT):
            q, k = FEAT * h + f, FEAT * (nh + h) + f
            align[4 * h, q, f] = 0.25
            align[4 * h + 1, k, f] = 1.0
            align[4 * h + 2, k, q] = 0.25
            align[4 * h + 3, q, k] = 0.25
    to_low = lambda a: jnp.asarray(a, BF)
    return to_low(pick_a), to_low(pick_b), jnp.asarray(rows), to_low(align)


def begin_at(lens, row, docs, position, start_block):
    start = -start_block
    found = start + position * 0
    for j in range(docs):
        if j:
            start = start + lens[row, j - 1]
            found = jnp.where(start <= position, start, found)
    return found


def chain_weights(lens, row, docs, block, blocks, length, backward):
    out, alive = [], None
    for k in range(1, blocks):
        source = block + k if backward else block - k
        inside = (source < blocks) if backward else (source >= 0)
        here = inside if alive is None else jnp.logical_and(alive, inside)
        out.append(jnp.where(here, 1.0, 0.0).astype(F32))
        first = begin_at(lens, row, docs, length - 1, source * length)
        passes = first < 0
        alive = passes if alive is None else jnp.logical_and(alive, passes)
    return out


def lane_iota(shape):
    return lax.broadcasted_iota(jnp.int32, shape, len(shape) - 1)


def row_iota(shape):
    return lax.broadcasted_iota(jnp.int32, shape, len(shape) - 2)


def with_ones(v, lanes=(0, 1)):
    side = lane_iota(v.shape)
    ones = jnp.where((side >= lanes[0]) & (side <= lanes[1]), 1.0, 0.0).astype(BF)
    return jnp.concatenate([v, ones], axis=1)


def split_sum(state, total, third):
    rows = row_iota(state.shape)
    high = total.astype(BF).astype(F32)
    low = total - high
    out = jnp.where(rows < 128, state, 0.0)
    out = jnp.where(rows == 128, high, out)
    if third:
        out = jnp.where(rows == 129, high, out)
        out = jnp.where(rows == 130, low, out)
    else:
        out = jnp.where(rows == 129, low, out)
    return out.astype(BF)


def flat(ref):
    x = ref[...]
    return x.reshape(x.shape[0] * x.shape[2], x.shape[3])


def picks(qk, pa, pb, rows, n):
    a = dot(qk, pa[n]) + rows[0:1, :]
    b = dot(qk, pb[n]) + rows[1:2, :]
    return a, b


def state_kernel(nh, vd, docs, lens, meta, x_ref, pa, pb, rows, out):
    row = pl.program_id(0)
    x = flat(x_ref)
    length = x.shape[0]
    qk = x[:, nh * vd :]
    last = begin_at(lens, row, docs, length - 1, meta[0] * length)
    trail = row_iota((length, 2 * 128)) >= last
    for h in range(nh):
        a, b = picks(qk, pa, pb, rows, nh + h)
        kf = (a * b * rows[3:4, :]).astype(BF)
        va = jnp.where(trail, with_ones(x[:, h * vd : (h + 1) * vd]).astype(F32), 0.0).astype(BF)
        st = dot(va, kf, TN)[:AUX]
        out[0, h] = split_sum(st, st[128:129], False)


def intra_kernel(nh, vd, docs, lens, meta, x_ref, align, num_out, den_out):
    row = pl.program_id(0)
    x = flat(x_ref)
    length = x.shape[0]
    qk = x[:, nh * vd :]
    one16 = jnp.where(lane_iota((1, 128)) == FEAT, 1.0, 0.0)
    tile = min(TILE, length)
    dens = [jnp.zeros((tile, 128), F32) for _ in range(length // tile)]
    for h in range(nh):
        qa = (dot(qk, align[4 * h]) + one16).astype(BF)
        ka = (dot(qk, align[4 * h + 1]) + one16).astype(BF)
        va = with_ones(x[:, h * vd : (h + 1) * vd])
        for t in range(length // tile):
            lo, hi = t * tile, (t + 1) * tile
            s1 = dot(qa[lo:hi], ka[:hi], NT)
            w = 0.5 * (s1 * s1) + 0.5
            pos = lo + row_iota((tile, 1))
            beg = begin_at(lens, row, docs, pos, meta[0] * length)
            kpos = lane_iota(w.shape)
            w = jnp.where((kpos >= beg) & (kpos <= pos), w, 0.0).astype(BF)
            acc = dot(w, va[:hi])
            num_out[0, lo:hi, h * vd : (h + 1) * vd] = acc[:, :vd]
            lane = lane_iota((tile, 128))
            dens[t] = jnp.where(lane == h, acc[:, vd : vd + 1], dens[t])
    for t in range(length // tile):
        den_out[0, t * tile : (t + 1) * tile, :] = dens[t]


def gather_states(sts, weights, h):
    total = None
    for st, w in zip(sts, weights):
        part = st[0, h].astype(F32) * w
        total = part if total is None else total + part
    return total


def attend_kernel(nh, vd, docs, blocks, lens, meta, x_ref, num, den, pa, pb, rows, *rest):
    sts, (att_out, den_out, st_out) = rest[: blocks - 1], rest[blocks - 1 :]
    row = pl.program_id(0)
    x = flat(x_ref)
    length = x.shape[0]
    qk = x[:, nh * vd :]
    weights = chain_weights(lens, row, docs, meta[0], blocks, length, False)
    pos = row_iota((length, 1))
    carried = begin_at(lens, row, docs, pos, meta[0] * length) < 0
    lane = lane_iota((length, 128))
    dens = den[0]
    for h in range(nh):
        st = gather_states(sts, weights, h)
        st = split_sum(st, st[128:129] + st[129:130], True)
        st_out[0, h] = st
        a, b = picks(qk, pa, pb, rows, h)
        qf = (a * b * rows[2:3, :]).astype(BF)
        inter = dot(qf, st, NT)
        more = jnp.where(carried, inter[:, :vd], 0.0)
        more_den = jnp.where(carried, inter[:, 128:129] + inter[:, 130:131], 0.0)
        total = dens[:, h : h + 1] + more_den
        value = (num[0, :, h * vd : (h + 1) * vd] + more) / total
        att_out[:, 0, :, h * vd : (h + 1) * vd] = value.astype(BF).reshape(
            att_out.shape[0], att_out.shape[2], vd
        )
        dens = jnp.where(lane == h, total, dens)
    den_out[0] = dens


def back_state_kernel(nh, vd, docs, lens, meta, x_ref, ga_ref, att_ref, den, pa, pb, rows, gn_out, out):
    row = pl.program_id(0)
    x, ga, att = flat(x_ref), flat(ga_ref), flat(att_ref)
    length = x.shape[0]
    qk = x[:, nh * vd :]
    pos = row_iota((length, 1))
    carried = begin_at(lens, row, docs, pos, meta[0] * length) < 0
    side = lane_iota((length, 128))
    for h in range(nh):
        cut = slice(h * vd, (h + 1) * vd)
        inv = 1.0 / den[0, :, h : h + 1]
        gah = ga[:, cut].astype(F32) * inv
        gd = -jnp.sum(gah * att[:, cut].astype(F32), axis=1, keepdims=True)
        high = gd.astype(BF).astype(F32)
        aux = jnp.where((side == 0) | (side == 2), high, jnp.where(side == 1, gd - high, 0.0))
        gn = jnp.concatenate([gah, aux], axis=1)
        gn_out[0, :, h * 256 : (h + 1) * 256] = gn.astype(BF)
        a, b = picks(qk, pa, pb, rows, h)
        qf = (a * b * rows[2:3, :]).astype(BF)
        st = dot(jnp.where(carried, gn, 0.0).astype(BF), qf, TN)[:AUX]
        out[0, h] = split_sum(st, st[128:129] + st[129:130], False)


def back_intra_kernel(
    nh, vd, docs, lens, meta, x_ref, gn_ref, st_ref, pa, pb, rows, align, gqk_out, gv_out
):
    row = pl.program_id(0)
    x = flat(x_ref)
    length = x.shape[0]
    qk = x[:, nh * vd :]
    one16 = jnp.where(lane_iota((1, 128)) == FEAT, 1.0, 0.0)
    tile = min(TILE, length)
    pos = row_iota((length, 1))
    carried = begin_at(lens, row, docs, pos, meta[0] * length) < 0
    gqk = None
    for h in range(nh):
        qa = (dot(qk, align[4 * h]) + one16).astype(BF)
        ka = (dot(qk, align[4 * h + 1]) + one16).astype(BF)
        k_at_q = dot(qk, align[4 * h + 2]).astype(BF)
        q_at_k = dot(qk, align[4 * h + 3]).astype(BF)
        va = with_ones(x[:, h * vd : (h + 1) * vd])
        gn = gn_ref[0, :, h * 256 : (h + 1) * 256]
        st = st_ref[0, h]
        gqf = jnp.where(carried, dot(gn[:, :AUX], st), 0.0) * rows[2:3, :]
        a, b = picks(qk, pa, pb, rows, h)
        part = dot((gqf * b).astype(BF), pa[h], NT) + dot((gqf * a).astype(BF), pb[h], NT)
        gqk = part if gqk is None else gqk + part
        gk_parts = []
        gq_parts = [None] * (length // tile)
        for t in range(length // tile):
            lo, hi = t * tile, (t + 1) * tile
            s1 = dot(ka[lo:hi], qa[lo:], NT)
            w = 0.5 * (s1 * s1) + 0.5
            kpos = lo + row_iota((tile, 1))
            qpos = lo + lane_iota((1, length - lo))
            beg = begin_at(lens, row, docs, qpos, meta[0] * length)
            see = (kpos >= beg) & (kpos <= qpos)
            gw = dot(va[lo:hi], gn[lo:], NT)
            gs = jnp.where(see, gw * s1, 0.0).astype(BF)
            w = jnp.where(see, w, 0.0).astype(BF)
            gv_out[0, lo:hi, h * vd : (h + 1) * vd] = dot(w, gn[lo:, :vd])
            gk_parts.append(dot(gs, q_at_k[lo:]))
            gq = dot(gs, k_at_q[lo:hi], TN)
            for u in range(t, length // tile):
                piece = gq[(u - t) * tile : (u - t + 1) * tile]
                gq_parts[u] = piece if gq_parts[u] is None else gq_parts[u] + piece
        gqk = gqk + jnp.concatenate(gk_parts, axis=0) + jnp.concatenate(gq_parts, axis=0)
    gqk_out[0] = gqk


def back_key_kernel(nh, vd, docs, blocks, lens, meta, x_ref, gqk_ref, gv_ref, pa, pb, rows, *rest):
    sts, (out,) = rest[: blocks - 1], rest[blocks - 1 :]
    row = pl.program_id(0)
    x = flat(x_ref)
    length = x.shape[0]
    qk = x[:, nh * vd :]
    weights = chain_weights(lens, row, docs, meta[0], blocks, length, True)
    last = begin_at(lens, row, docs, length - 1, meta[0] * length)
    trail = row_iota((length, 1)) >= last
    gqk = gqk_ref[0]
    shape = (out.shape[0], out.shape[2])
    for h in range(nh):
        st = gather_states(sts, weights, h)
        st = split_sum(st, st[128:129] + st[129:130], False)
        va = with_ones(x[:, h * vd : (h + 1) * vd])
        gkf = jnp.where(trail, dot(va[:, :AUX], st), 0.0) * rows[3:4, :]
        a, b = picks(qk, pa, pb, rows, nh + h)
        gqk = gqk + dot((gkf * b).astype(BF), pa[nh + h], NT)
        gqk = gqk + dot((gkf * a).astype(BF), pb[nh + h], NT)
        kf = (a * b * rows[3:4, :]).astype(BF)
        more = jnp.where(trail, dot(kf, st[:vd], NT), 0.0)
        gv = gv_ref[0, :, h * vd : (h + 1) * vd] + more
        out[:, 0, :, h * vd : (h + 1) * vd] = gv.astype(BF).reshape(shape + (vd,))
    out[:, 0, :, nh * vd :] = gqk.astype(BF).reshape(shape + (128,))


def row_call(kernel, rows_n, scalars, ins, outs, flops):
    def spec(shape, dim):
        if dim is None:
            return pl.BlockSpec(shape, lambda r, *_: (0,) * len(shape))
        block = tuple(1 if d == dim else n for d, n in enumerate(shape))
        return pl.BlockSpec(block, lambda r, *_: tuple(r if d == dim else 0 for d in range(len(shape))))

    moved = sum(a.size * a.dtype.itemsize for a, _ in ins)
    moved += sum(int(np.prod(s)) * np.dtype(t).itemsize for s, t, _ in outs)
    return pl.pallas_call(
        kernel,
        out_shape=tuple(jax.ShapeDtypeStruct(s, t) for s, t, _ in outs),
        grid_spec=pltpu.PrefetchScalarGridSpec(
            num_scalar_prefetch=len(scalars),
            grid=(rows_n,),
            in_specs=[spec(a.shape, d) for a, d in ins],
            out_specs=[spec(s, d) for s, t, d in outs],
        ),
        compiler_params=pltpu.CompilerParams(vmem_limit_bytes=56 * 1024 * 1024),
        cost_estimate=pl.CostEstimate(flops=int(flops), bytes_accessed=int(moved), transcendentals=0),
    )(*scalars, *[a for a, _ in ins])


SEQ = ("sy", "sc")
HEAD = ("ha", "hb")


def here():
    return tuple(lax.axis_index(n) for n in ("sy", "sc", "ha", "hb"))


def remote(src, dst, ssem, rsem, k, device):
    return pltpu.make_async_remote_copy(
        src_ref=src,
        dst_ref=dst,
        send_sem=ssem.at[k],
        recv_sem=rsem.at[k],
        device_id=device,
        device_id_type=MESH_ID,
    )


def greet(devices):
    bar = pltpu.get_barrier_semaphore()
    for device in devices:
        pl.semaphore_signal(bar, 1, device_id=device, device_id_type=MESH_ID)
    pl.semaphore_wait(bar, len(devices))


def square():
    return tuple(lax.axis_size(n) for n in ("sy", "ha", "hb")) == (2, 4, 2)


def place(block, head, special):
    if special:
        ha = 2 * (block % 2) + block // 2
        return (head // 2 + ha % 2) % 2, head % 2, ha
    return head // 2, head % 2, block


def own_place():
    sy, sc, ha, _ = here()
    if square():
        return 2 * (ha % 2) + ha // 2, 2 * ((sy + ha) % 2) + sc
    return ha, sy * 2 + sc


def first_head(block):
    return block % 2 if square() else block


def home_of(head, special):
    if special:
        return 2 * (head % 2) + head // 2, 2 * ((head // 2 + head) % 2) + head % 2
    return head, head


def maybe_own(k, own, elsewhere, alone):
    if k:
        elsewhere()
    else:
        pl.when(jnp.logical_not(own))(elsewhere)
        pl.when(own)(alone)


def exchange_kernel(to_blocks, width, last_major, extra, src, *refs):
    n_in, n_out = {None: (0, 0), "gather": (2, 2), "scatter": (1, 2)}[extra]
    ins, dst, outs, sems = refs[:n_in], refs[n_in], refs[n_in + 1 : n_in + 1 + n_out], refs[n_in + 1 + n_out :]
    ssem, rsem, lsem = sems[:3]
    sy, sc, a, b = here()
    s = sy * 2 + sc
    block, head = own_place()
    special = square()
    size_a, size_b = lax.axis_size("ha"), lax.axis_size("hb")
    count = size_a * size_b
    bar = pltpu.get_barrier_semaphore()
    same = s == block

    def at(k):
        i, pb = k // size_b, lax.rem(b + k % size_b, size_b)
        if to_blocks:
            sender = (block // 2, block % 2, lax.rem(a + i, size_a), pb)
            to = lax.rem(a - place(s, 0, special)[2] + first_head(s) + i + size_a, size_a)
            piece = to * size_b + pb
            source = src.at[:, pl.ds(pl.multiple_of(piece * width, 128), width)]
            return sender, source, dst.at[a * size_b + b], place(s, to, special) + (pb,)
        sender = place(s, lax.rem(first_head(s) + i, size_a), special) + (pb,)
        to = lax.rem(head - first_head(block) + a + i + size_a, size_a)
        column = b * size_a + head if last_major else head * size_b + b
        far = dst.at[:, pl.ds(pl.multiple_of(column * width, 128), width)]
        return sender, src.at[to * size_b + pb], far, (block // 2, block % 2, to, pb)

    def copy(k):
        _, source, far, receiver = at(k)
        return remote(source, far, ssem, rsem, k, receiver)

    def local():
        return pltpu.make_async_copy(at(0)[1], at(0)[2], lsem.at[0])

    def signal(device):
        pl.semaphore_signal(bar, 1, device_id=device, device_id_type=MESH_ID)

    to_x, to_y, to_core = (sy, sc, a, 1 - b), (1 - sy, sc, a, b), (sy, 1 - sc, a, b)
    expected = count - same.astype(jnp.int32)
    for k in range(count):
        maybe_own(k, same, functools.partial(signal, at(k)[0]), lambda: None)
    if extra in ("gather", "scatter"):
        greeted = (to_x, to_y, to_core)[: 3 if extra == "gather" else 2]
        for device in greeted:
            signal(device)
        expected = expected + len(greeted)
    pl.semaphore_wait(bar, expected)
    for k in range(count):
        maybe_own(k, same, lambda: copy(k).start(), lambda: local().start())

    if extra == "gather":
        (more, own_w), (near, other_w) = ins, outs
        gsem, hsem = sems[3:]
        half = more.shape[0] // 2
        low, high = pl.ds(0, half), pl.ds(half, half)
        copies = [
            remote(more, near.at[0], gsem, hsem, 0, to_x),
            remote(more, near.at[1], gsem, hsem, 1, to_y),
            remote(own_w, other_w, gsem, hsem, 4, to_core),
        ]
        for c in copies:
            c.start()
        copies[0].wait_recv()
        copies.append(remote(near.at[0, high], near.at[2, high], gsem, hsem, 2, to_y))
        copies[3].start()
        copies[1].wait_recv()
        copies.append(remote(near.at[1, low], near.at[2, low], gsem, hsem, 3, to_x))
        copies[4].start()
        for c in copies[2:]:
            c.wait_recv()
        for c in copies:
            c.wait_send()
    if extra == "scatter":
        (parts,), (got, relay) = ins, outs
        gsem, hsem = sems[3:]
        half = parts.shape[1] // 2
        low, high = pl.ds(0, half), pl.ds(half, half)
        copies = [
            remote(parts.at[3, low], relay.at[0], gsem, hsem, 0, to_x),
            remote(parts.at[3, high], relay.at[1], gsem, hsem, 1, to_y),
            remote(parts.at[1], got.at[0], gsem, hsem, 2, to_x),
            remote(parts.at[2], got.at[1], gsem, hsem, 3, to_y),
        ]
        for c in copies:
            c.start()
        copies[0].wait_recv()
        copies.append(remote(relay.at[0], got.at[2, low], gsem, hsem, 4, to_y))
        copies[4].start()
        copies[1].wait_recv()
        copies.append(remote(relay.at[1], got.at[2, high], gsem, hsem, 5, to_x))
        copies[5].start()
        for c in copies[2:]:
            c.wait_recv()
        for c in copies:
            c.wait_send()
    for k in range(count):
        maybe_own(k, same, lambda: copy(k).wait(), lambda: local().wait())


def exchange(x, to_blocks, width, collective, extra=None, ins=(), outs=(), last_major=False):
    count = lax.axis_size("ha") * lax.axis_size("hb")
    tokens = x.shape[0] if to_blocks else x.shape[1]
    shape = (count, tokens, width) if to_blocks else (tokens, count * width)
    any_space = pl.BlockSpec(memory_space=pl.ANY)
    more = {None: 0, "gather": 5, "scatter": 6}[extra]
    return pl.pallas_call(
        functools.partial(exchange_kernel, to_blocks, width, last_major, extra),
        out_shape=[jax.ShapeDtypeStruct(s, x.dtype) for s in (shape, *outs)],
        in_specs=[any_space] * (1 + len(ins)),
        out_specs=[any_space] * (1 + len(outs)),
        scratch_shapes=[
            pltpu.SemaphoreType.DMA((count,)),
            pltpu.SemaphoreType.DMA((count,)),
            pltpu.SemaphoreType.DMA((1,)),
        ]
        + [pltpu.SemaphoreType.DMA((more,))] * (2 if more else 0),
        compiler_params=pltpu.CompilerParams(collective_id=collective, has_side_effects=True),
        cost_estimate=pl.CostEstimate(flops=0, bytes_accessed=x.size * 500, transcendentals=0),
    )(x, *ins)


def home_kernel(*refs):
    src, grads, windows, shards, dst, grads_got, windows_got, shards_got = refs[:8]
    ssem, rsem, lsem, gsem, hsem, usem, vsem = refs[8:]
    sy, sc, a, b = here()
    s = sy * 2 + sc
    block, head = own_place()
    special = square()
    size_a, size_b = lax.axis_size("ha"), lax.axis_size("hb")
    devices = src.shape[0]
    me = (s * size_a + a) * size_b + b
    homely = head == a
    block_h, seq_h = home_of(head, special)
    bar = pltpu.get_barrier_semaphore()

    def peer(k):
        i = lax.rem(me + k, devices)
        rest = i // (size_a * size_b)
        return i, (rest // 2, rest % 2, i // size_b % size_a, i % size_b)

    def copy(k):
        i, device = peer(k)
        return remote(src.at[i], dst.at[me], ssem, rsem, k, device)

    def grad_ends(k):
        e = lax.rem(block - block_h + seq_h + k + size_a, size_a)
        return grads.at[e], grads_got.at[block], (e // 2, e % 2, head, b)

    def grad_copy(k):
        source, far, device = grad_ends(k)
        return remote(source, far, gsem, hsem, k, device)

    def grad_local():
        return pltpu.make_async_copy(*grad_ends(0)[:2], lsem.at[1])

    def window_copy(k):
        e = lax.rem(s + k, size_a)
        return remote(windows.at[e], windows_got.at[s], gsem, hsem, size_a + k, (e // 2, e % 2, a, b))

    def shard_copy(k):
        pa, pb = lax.rem(a + k // size_b, size_a), lax.rem(b + k % size_b, size_b)
        far = shards_got.at[a * size_b + b]
        return remote(shards.at[pa * size_b + pb], far, usem, vsem, k, (sy, sc, pa, pb))

    @pl.loop(1, devices)
    def _(k):
        pl.semaphore_signal(bar, 1, device_id=peer(k)[1], device_id_type=MESH_ID)

    stay = [
        pltpu.make_async_copy(shards.at[a * size_b + b], shards_got.at[a * size_b + b], lsem.at[3]),
        pltpu.make_async_copy(src.at[me], dst.at[me], lsem.at[0]),
        pltpu.make_async_copy(windows.at[s], windows_got.at[s], lsem.at[2]),
    ]
    for c in stay:
        c.start()
    pl.semaphore_wait(bar, devices - 1)
    heads = size_a * size_b
    for k in range(size_a):
        maybe_own(k, homely, lambda: grad_copy(k).start(), lambda: grad_local().start())
        if k:
            window_copy(k).start()
    for k in range(1, heads):
        shard_copy(k).start()

    @pl.loop(1, devices)
    def _(k):
        copy(k).start()

    @pl.loop(1, devices)
    def _(k):
        copy(k).wait()

    for k in range(size_a):
        maybe_own(k, homely, lambda: grad_copy(k).wait(), lambda: grad_local().wait())
        if k:
            window_copy(k).wait()
    for k in range(1, heads):
        shard_copy(k).wait()
    for c in stay:
        c.wait()


def send_home(x, grads, windows, shards, collective):
    devices = 2 * lax.axis_size("sy") * lax.axis_size("ha") * lax.axis_size("hb")
    vectors, share = x.shape[0], x.shape[1] // devices
    x = jnp.transpose(x.reshape(vectors, devices, share), (1, 0, 2))
    x = jnp.pad(x, ((0, 0), (0, 8 - vectors), (0, 128 - share)))
    any_space = pl.BlockSpec(memory_space=pl.ANY)
    ins = [x, grads, windows, shards]
    size_a, heads = lax.axis_size("ha"), shards.shape[0]
    out = pl.pallas_call(
        home_kernel,
        out_shape=[jax.ShapeDtypeStruct(v.shape, v.dtype) for v in ins],
        in_specs=[any_space] * len(ins),
        out_specs=[any_space] * len(ins),
        scratch_shapes=[
            pltpu.SemaphoreType.DMA((devices,)),
            pltpu.SemaphoreType.DMA((devices,)),
            pltpu.SemaphoreType.DMA((4,)),
            pltpu.SemaphoreType.DMA((2 * size_a,)),
            pltpu.SemaphoreType.DMA((2 * size_a,)),
            pltpu.SemaphoreType.DMA((heads,)),
            pltpu.SemaphoreType.DMA((heads,)),
        ],
        compiler_params=pltpu.CompilerParams(collective_id=collective, has_side_effects=True),
        cost_estimate=pl.CostEstimate(flops=0, bytes_accessed=100000000, transcendentals=0),
    )(*ins)
    vectors = jnp.sum(out[0], axis=0)[:vectors, :share]
    return vectors, jnp.sum(out[1].astype(F32), axis=0), out[2], jnp.sum(out[3].astype(F32), axis=0)


def near_kernel(rows, src, weights, near, theirs, gsem, hsem):
    sy, sc, a, b = here()
    to_x, to_y, to_core = (sy, sc, a, 1 - b), (1 - sy, sc, a, b), (sy, 1 - sc, a, b)
    half = src.shape[0] // 2
    low, high = pl.ds(0, half), pl.ds(half, half)
    greet((to_x, to_y, to_core))
    copies = [
        remote(src, near.at[0], gsem, hsem, 0, to_x),
        remote(src, near.at[1], gsem, hsem, 1, to_y),
        remote(weights.at[:, pl.ds(0, rows)], theirs, gsem, hsem, 4, to_core),
    ]
    for copy in copies:
        copy.start()
    copies[0].wait_recv()
    copies.append(remote(near.at[0, high], near.at[2, high], gsem, hsem, 2, to_y))
    copies[3].start()
    copies[1].wait_recv()
    copies.append(remote(near.at[1, low], near.at[2, low], gsem, hsem, 3, to_x))
    copies[4].start()
    for copy in copies[2:]:
        copy.wait_recv()
    for copy in copies:
        copy.wait_send()


def gather_near(x, weights, rows, collective):
    if not square():
        return (lax.all_gather(x, QUAD, axis=0, tiled=True),), swap(weights[:, :rows], "sc")
    any_space = pl.BlockSpec(memory_space=pl.ANY)
    near, theirs = pl.pallas_call(
        functools.partial(near_kernel, rows),
        out_shape=[
            jax.ShapeDtypeStruct((3,) + x.shape, x.dtype),
            jax.ShapeDtypeStruct((weights.shape[0], rows, weights.shape[2]), weights.dtype),
        ],
        in_specs=[any_space] * 2,
        out_specs=[any_space] * 2,
        scratch_shapes=[pltpu.SemaphoreType.DMA((5,))] * 2,
        compiler_params=pltpu.CompilerParams(collective_id=collective, has_side_effects=True),
        cost_estimate=pl.CostEstimate(flops=0, bytes_accessed=x.size * 200, transcendentals=0),
    )(x, weights)
    return (x, near[0], near[1], near[2]), theirs


def start_kernel(parts, src, w_in, w_out, dst, w_in_home, w_out_all, ssem, rsem, lsem, wsem, vsem):
    sy, sc, a, b = here()
    block, head = own_place()
    size = lax.axis_size("ha")
    target = place(sy * 2 + sc, a, True) + (b,)
    source = (block // 2, block % 2, head, b)
    same = jnp.logical_and(sy * 2 + sc == block, a == head)
    apart = jnp.logical_not(same)
    to_x, to_y, to_core = (sy, sc, a, 1 - b), (1 - sy, sc, a, b), (sy, 1 - sc, a, b)
    to_up, to_down = (sy, sc, a + 1, b), (sy, sc, a - 1, b)
    has_up, has_down = a < size - 1, a > 0
    bar = pltpu.get_barrier_semaphore()

    def signal(device):
        pl.semaphore_signal(bar, 1, device_id=device, device_id_type=MESH_ID)

    for device in (to_x, to_y, to_core):
        signal(device)
    pl.when(apart)(lambda: signal(source))
    pl.when(has_up)(lambda: signal(to_up))
    pl.when(has_down)(lambda: signal(to_down))
    own_w = pltpu.make_async_copy(w_out, w_out_all.at[a * 2 + b], lsem.at[parts])
    own_w.start()
    pl.semaphore_wait(
        bar, 3 + apart.astype(jnp.int32) + has_up.astype(jnp.int32) + has_down.astype(jnp.int32)
    )

    step = src.shape[0] // parts
    count = 9
    half = src.shape[1] // 2

    def piece(z, x, r, lo=0, n=None):
        return dst.at[z * 2 + x, pl.ds(r * step, step), pl.ds(lo, src.shape[1] if n is None else n)]

    def make(k, r, ref, device):
        return remote(ref, ref, ssem, rsem, count * r + k, device)

    def home(r):
        return remote(src.at[pl.ds(r * step, step)], piece(a, b, r), ssem, rsem, count * r, target)

    def stay(r):
        return pltpu.make_async_copy(src.at[pl.ds(r * step, step)], piece(a, b, r), lsem.at[r])

    def w_home():
        return pltpu.make_async_remote_copy(
            src_ref=w_in,
            dst_ref=w_in_home,
            send_sem=wsem.at[0],
            recv_sem=wsem.at[1],
            device_id=target,
            device_id_type=MESH_ID,
        )

    def w_stay():
        return pltpu.make_async_copy(w_in, w_in_home, lsem.at[parts + 1])

    for r in range(parts):
        pl.when(apart)(lambda: home(r).start())
        pl.when(same)(lambda: stay(r).start())

    def send_w(k, pa, device):
        ref = w_out_all.at[pa * 2 + b]
        return remote(ref, ref, vsem.at[0], vsem.at[1], k, device)

    def spread(k, pa, up, down):
        if up:
            pl.when(has_up)(lambda: send_w(k, pa, to_up).start())
        if down:
            pl.when(has_down)(lambda: send_w(size + k, pa, to_down).start())
        send_w(2 * size + pa, pa, to_x).start()

    def w_step(k):
        @pl.when(a - k >= 0)
        def _():
            send_w(k - 1, a - k, to_x).wait_recv()
            spread(k, a - k, True, False)

        @pl.when(a + k < size)
        def _():
            send_w(size + k - 1, a + k, to_x).wait_recv()
            spread(k, a + k, False, True)

    across_y, across_c = (head + 2) % 4, head + 1 - 2 * (head % 2)
    across = (across_y + 1) - 2 * (across_y % 2)
    sent = []

    def go(copy):
        copy.start()
        sent.append(copy)

    def arrive(k, r, ref):
        make(k, r, ref, to_x).wait_recv()

    def stage_0(r):
        pl.when(apart)(lambda: arrive(0, r, piece(head, b, r)))
        pl.when(same)(lambda: stay(r).wait())
        for k, device in ((1, to_x), (2, to_y), (3, to_core)):
            go(make(k, r, piece(head, b, r), device))

    def stage_1(r):
        arrive(1, r, piece(head, 1 - b, r))
        go(make(4, r, piece(head, 1 - b, r, half, half), to_y))
        go(make(5, r, piece(head, 1 - b, r), to_core))
        arrive(2, r, piece(across_y, b, r))
        go(make(6, r, piece(across_y, b, r, 0, half), to_x))
        go(make(7, r, piece(across_y, b, r), to_core))

    def stage_2(r):
        arrive(4, r, piece(across_y, 1 - b, r, half, half))
        arrive(6, r, piece(across_y, 1 - b, r, 0, half))
        go(make(8, r, piece(across_y, 1 - b, r), to_core))

    def stage_3(r):
        arrive(3, r, piece(across_c, b, r))
        arrive(5, r, piece(across_c, 1 - b, r))
        arrive(7, r, piece(across, b, r))
        arrive(8, r, piece(across, 1 - b, r))

    stages = (stage_0, stage_1, stage_2, stage_3)
    for t in range(parts + 3):
        for i, stage in enumerate(stages):
            if 0 <= t - i < parts:
                stage(t - i)
        if t == 0:
            pl.when(apart)(lambda: w_home().start())
            pl.when(same)(lambda: w_stay().start())
            own_w.wait()
            spread(0, a, True, True)
        elif t < size:
            w_step(t)
    for k in range(parts + 3, size):
        w_step(k)
    pl.when(apart)(lambda: w_home().wait_recv())
    pl.when(same)(lambda: w_stay().wait())
    for k in range(size):
        ref = w_out_all.at[k * 2 + 1 - b]
        remote(ref, ref, vsem.at[0], vsem.at[1], 2 * size + k, to_x).wait_recv()
        send_w(2 * size + k, k, to_x).wait_send()
        pl.when(jnp.logical_and(has_up, a - k >= 0))(lambda: send_w(k, a - k, to_x).wait_send())
        pl.when(jnp.logical_and(has_down, a + k < size))(lambda: send_w(size + k, a + k, to_x).wait_send())
    for copy in sent:
        copy.wait_send()
    for r in range(parts):
        pl.when(apart)(lambda: home(r).wait_send())
    pl.when(apart)(lambda: w_home().wait_send())


def start(x, w_in, w_out, collective):
    if not square():
        size = lax.axis_size("ha")
        perm = [(s * size + z, z * size + s) for s in range(size) for z in range(size)]
        x, w_in = (lax.ppermute(v, ("sy", "sc", "ha"), perm) for v in (x, w_in))
        return lax.all_gather(x, ("sy", "sc", "hb"), axis=0), w_in, lax.all_gather(w_out, HEAD, axis=0)
    parts = x.shape[0]
    return pl.pallas_call(
        functools.partial(start_kernel, parts),
        out_shape=[
            jax.ShapeDtypeStruct((8,) + x.shape, x.dtype),
            jax.ShapeDtypeStruct(w_in.shape, w_in.dtype),
            jax.ShapeDtypeStruct((8,) + w_out.shape, w_out.dtype),
        ],
        in_specs=[pl.BlockSpec(memory_space=pl.ANY)] * 3,
        out_specs=[pl.BlockSpec(memory_space=pl.ANY)] * 3,
        scratch_shapes=[
            pltpu.SemaphoreType.DMA((9 * parts,)),
            pltpu.SemaphoreType.DMA((9 * parts,)),
            pltpu.SemaphoreType.DMA((parts + 2,)),
            pltpu.SemaphoreType.DMA((2,)),
            pltpu.SemaphoreType.DMA((2, 12)),
        ],
        compiler_params=pltpu.CompilerParams(collective_id=collective, has_side_effects=True),
        cost_estimate=pl.CostEstimate(flops=0, bytes_accessed=x.size * 400, transcendentals=0),
    )(x, w_in, w_out)


def swap(x, axis):
    return lax.ppermute(x, axis, [(0, 1), (1, 0)])


def seat(block, head, size, special):
    sy, sc, ha = place(block, head, special)
    return (sy * 2 + sc) * size + ha


def chain_pieces(x, backward):
    size, special = lax.axis_size("ha"), square()
    out = []
    for k in range(1, size):
        perm = []
        for i in range(size - k):
            ends = (i + k, i) if backward else (i, i + k)
            perm += [tuple(seat(e, h, size, special) for e in ends) for h in range(size)]
        out.append(lax.ppermute(x, SEQ + ("ha",), perm))
    return out


def tie(*values):
    return lax.optimization_barrier(values)


def my_columns(x, by_core):
    parts, place_of = lax.axis_size("sy") * 2, lax.axis_index("sy") * 2 + lax.axis_index("sc")
    if by_core:
        parts, place_of = 2, lax.axis_index("sc")
    size = x.shape[1] // parts
    return lax.dynamic_slice_in_dim(x, place_of * size, size, 1)


def by_halves(a, own, other):
    own, other = dot(a, own), dot(a, other)
    first = lax.axis_index("sc") == 0
    return jnp.concatenate([jnp.where(first, own, other), jnp.where(first, other, own)], axis=1)


def by_halves_back(a, own, other):
    size = own.shape[1]
    core = lax.axis_index("sc")
    ours, theirs = (lax.dynamic_slice_in_dim(a, i * size, size, 1) for i in (core, 1 - core))
    return dot(ours, own, NT) + dot(theirs, other, NT)


def unit_window(x, size):
    units = x.shape[0]
    window = -(-units // (size * 16)) * 16
    place = lax.axis_index("sy") * 2 + lax.axis_index("sc")
    start = jnp.minimum(place * window, units - window)
    part = lax.dynamic_slice_in_dim(x, start, window, 0)
    fresh = start + lax.broadcasted_iota(jnp.int32, part.shape, 0) >= place * window
    return jnp.where(fresh, part, jnp.zeros_like(part))


def windows_joined(parts, units):
    size, window = parts.shape[0], parts.shape[1]
    pieces = []
    for i in range(size):
        start = min(i * window, units - window)
        pieces.append(parts[i, max(i * window - start, 0) :])
    return jnp.concatenate(pieces, axis=0)


def ff_kernel(meta, n2, cot, mine, theirs, *rest):
    gg_out, gu_out, hid_out, n2_out, cot_out, part_out, acc = rest[-7:]
    shard = pl.program_id(0)

    def work(w, first):
        x, c = n2[...], cot[...]
        window, width = w.shape[1] // 3, w.shape[2]
        w_gate, w_up, w_down = (w[:, i * window : (i + 1) * window].reshape(-1, width) for i in range(3))
        gate, up, gh = dot(x, w_gate, NT), dot(x, w_up, NT), dot(c, w_down, NT)
        sig = jax.nn.sigmoid(gate)
        act = gate * sig
        hid_out[0, 0] = (act * up).astype(BF)
        gg = (gh * up * (sig + act * (1.0 - sig))).astype(BF)
        gu = (gh * act).astype(BF)
        gg_out[0, 0] = gg
        gu_out[0, 0] = gu
        back = dot(gg, w_gate) + dot(gu, w_up)
        if first:
            acc[...] = back
            n2_out[0] = x
            cot_out[0] = c
        else:
            part_out[...] = (acc[...] + back).astype(BF)

    @pl.when(shard == 0)
    def _():
        work(mine, True)

    @pl.when(shard == 1)
    def _():
        work(theirs, False)


def ff_chunk(n2, cot, mine, theirs, place, chunks, kept):
    tokens, width = n2.shape
    units = theirs.shape[0] * theirs.shape[1] // 3
    keep = jax.ShapeDtypeStruct((2, chunks, tokens, units), BF)
    held_shape = jax.ShapeDtypeStruct((chunks, tokens, width), BF)
    whole = pl.BlockSpec((tokens, width), lambda i, m: (0, 0))
    weights = pl.BlockSpec(theirs.shape, lambda i, m: (0, 0, 0), pipeline_mode=pl.Buffered(1))
    piece = pl.BlockSpec((1, 1, tokens, units), lambda i, m: (i, m[0], 0, 0))
    held = pl.BlockSpec((1, tokens, width), lambda i, m: (m[0], 0, 0))
    old = [] if kept is None else list(kept)
    return pl.pallas_call(
        ff_kernel,
        out_shape=(keep, keep, keep, held_shape, held_shape, jax.ShapeDtypeStruct((tokens, width), BF)),
        grid_spec=pltpu.PrefetchScalarGridSpec(
            num_scalar_prefetch=1,
            grid=(2,),
            in_specs=[whole, whole, weights, weights] + [pl.BlockSpec(memory_space=pl.ANY)] * len(old),
            out_specs=[piece, piece, piece, held, held, whole],
            scratch_shapes=[pltpu.VMEM((tokens, width), F32)],
        ),
        input_output_aliases={5 + i: i for i in range(len(old))},
        compiler_params=pltpu.CompilerParams(vmem_limit_bytes=58 * 1024 * 1024),
        cost_estimate=pl.CostEstimate(
            flops=tokens * width * units * 20,
            bytes_accessed=12 * units * width + 8 * tokens * width,
            transcendentals=0,
        ),
    )(place, n2, cot, mine, theirs, *old)


def branch_kernel(order, hidden, mine, theirs, out):
    width = out.shape[1]
    part = dot(hidden[0, 0], mine[...].reshape(-1, width)) + dot(hidden[1, 0], theirs[...].reshape(-1, width))
    out[...] = part.astype(BF)


def branch_product(hidden, mine, theirs):
    _, chunks, tokens, units = hidden.shape
    size, rows, width = theirs.shape
    weights = pl.BlockSpec((size, rows // 3, width), lambda i, m: (0, 2, 0), pipeline_mode=pl.Buffered(1))
    y, b = lax.axis_index("sy"), lax.axis_index("hb")
    turns = ((y, b), (y, 1 - b), (1 - y, b), (1 - y, 1 - b))[:chunks]
    order = jnp.stack([p * 2 + q if chunks > 1 else 0 * p for p, q in turns]).astype(jnp.int32)
    return pl.pallas_call(
        branch_kernel,
        out_shape=jax.ShapeDtypeStruct((chunks * tokens, width), BF),
        grid_spec=pltpu.PrefetchScalarGridSpec(
            num_scalar_prefetch=1,
            grid=(chunks,),
            in_specs=[pl.BlockSpec((2, 1, tokens, units), lambda i, m: (0, i, 0, 0)), weights, weights],
            out_specs=pl.BlockSpec((tokens, width), lambda i, m: (m[i], 0)),
        ),
        compiler_params=pltpu.CompilerParams(vmem_limit_bytes=40 * 1024 * 1024),
        cost_estimate=pl.CostEstimate(
            flops=chunks * tokens * units * width * 4, bytes_accessed=12 * units * width, transcendentals=0
        ),
    )(order, hidden, mine, theirs)


QUAD = ("sy", "hb")


def add_low(a, b):
    return (a.astype(F32) + b.astype(F32)).astype(BF)


def ring_sum(parts, meanwhile):
    own, to_x, to_y, across = parts
    half = own.shape[0] // 2
    via_x, via_y = swap(across[:half], "hb"), swap(across[half:], "sy")
    x_low, y_high = swap(to_x[:half], "hb"), swap(to_y[half:], "sy")
    work = meanwhile(0)
    via_x, via_y, *work = tie(via_x, via_y, *work)
    meanwhile(0, work)
    y_low = swap(add_low(to_y[:half], via_x), "sy")
    x_high = swap(add_low(to_x[half:], via_y), "hb")
    work = meanwhile(1)
    y_low, x_high, *work = tie(y_low, x_high, *work)
    meanwhile(1, work)
    low = own[:half].astype(F32) + x_low.astype(F32) + y_low.astype(F32)
    high = own[half:].astype(F32) + x_high.astype(F32) + y_high.astype(F32)
    return jnp.concatenate([low, high], axis=0)


def seq_sum(a, b):
    size_y, core, y = lax.axis_size("sy"), lax.axis_index("sc"), lax.axis_index("sy")
    size = b.shape[1] // (size_y * 2)

    def columns(x, i):
        return lax.dynamic_slice_in_dim(x, i * size, size, 1)

    def of_core(c):
        return jnp.concatenate([columns(b, i * 2 + c) for i in range(size_y)], axis=1)

    given = swap(dot(a, of_core(1 - core), TN).astype(BF), "sc")
    part = (dot(a, of_core(core), TN) + given.astype(F32)).astype(BF)
    if size_y != 2:
        return lax.psum_scatter(part, "sy", scatter_dimension=1, tiled=True)
    return add_low(columns(part, y), swap(columns(part, 1 - y), "sy"))


def quad_sum(parts, meanwhile):
    if len(parts) == 4:
        return ring_sum(parts, meanwhile)
    for stage in (0, 1):
        meanwhile(stage)
    return lax.psum_scatter(parts[0], QUAD, scatter_dimension=0, tiled=True).astype(F32)


def ff_group(chunks, cots, mine, theirs):
    kept, parts = None, []
    for i, (chunk, cot) in enumerate(zip(chunks, cots)):
        where = jnp.full((1,), i, jnp.int32)
        *kept, part = ff_chunk(chunk, cot, mine, theirs, where, len(cots), kept)
        parts.append(part)
    grads, branch = [], []
    flat = [k.reshape((2, -1, k.shape[-1]) if k.ndim == 4 else (-1, k.shape[-1])) for k in kept]
    pairs = [(flat[0], flat[3]), (flat[1], flat[3]), (flat[2], flat[4])]

    def meanwhile(stage, results=None):
        if results is not None:
            grads[:] = results[:3]
            branch[:] = results[3:]
            return None
        if stage == 0:
            grads.extend(swap(dot(a[1], b, TN).astype(BF), "sc") for a, b in pairs)
            return grads
        for i, (a, b) in enumerate(pairs):
            grads[i] = (dot(a[0], b, TN) + grads[i].astype(F32)).astype(BF)
        branch.append(branch_product(kept[2], mine, theirs))
        return grads + branch

    return quad_sum(parts, meanwhile), grads, branch[0]


def rms_scale(x):
    return lax.rsqrt(jnp.mean(x * x, axis=-1, keepdims=True) + EPS)


def on_device(
    inputs,
    attn_gain,
    w_query,
    w_key,
    w_value,
    w_out,
    out_bias,
    mlp_gain,
    gate_weight,
    up_weight,
    down_weight,
    cotangent,
    doc_lengths,
):
    every = ("sy", "sc", "ha", "hb")
    blocks = lax.axis_size("sy") * 2
    size_a, size_b = lax.axis_size("ha"), lax.axis_size("hb")
    count = size_a * size_b
    sub_len, rows_n, width = inputs.shape
    docs = doc_lengths.shape[1]
    nh = w_query.shape[1] // FEAT
    vd = w_value.shape[1] // nh
    vw = nh * vd
    xw = vw + 128
    length = sub_len * count
    tokens = rows_n * sub_len
    meta = own_place()[0].astype(jnp.int32).reshape(1)
    pa, pb, frows, align = feature_tables(nh)
    scalars = (doc_lengths, meta)

    x = jnp.transpose(inputs, (1, 0, 2)).astype(F32)
    cot = jnp.transpose(cotangent, (1, 0, 2))
    scale_one = rms_scale(x)
    normed_one = x * scale_one
    pad = jnp.zeros((128 - 2 * nh * FEAT, width), BF)
    w_in = jnp.concatenate([w_value.T, w_query.T, w_key.T, pad], axis=0)
    units = down_weight.shape[0]
    windows = [unit_window(w, blocks) for w in (gate_weight.T, up_weight.T, down_weight)]
    w_in_piece = my_columns(w_in, False)
    to_fetch = jnp.concatenate(windows, axis=0)
    normed_full, w_in_home, w_out_piece = start((normed_one * attn_gain).astype(BF), w_in, my_columns(w_out, True), 3)
    to_fetch, normed_full = tie(to_fetch, normed_full)
    fetched = lax.all_gather(to_fetch, "ha", axis=0)
    window = windows[0].shape[0]

    qkv = jnp.einsum("grtd,cd->grtc", normed_full, w_in_home, preferred_element_type=F32).astype(BF)
    pair = nh * rows_n * length * length
    (states,) = row_call(
        functools.partial(state_kernel, nh, vd, docs),
        rows_n,
        scalars,
        [(qkv, 1), (pa, None), (pb, None), (frows, None)],
        [((rows_n, nh, AUX, TILE), BF, 0)],
        nh * rows_n * length * 256 * 256 * 4,
    )
    earlier = chain_pieces(states, False)
    num, den = row_call(
        functools.partial(intra_kernel, nh, vd, docs),
        rows_n,
        scalars,
        [(qkv, 1), (align, None)],
        [((rows_n, length, vw), F32, 0), ((rows_n, length, 128), F32, 0)],
        pair * 256 * 4,
    )
    att, den, state_in = row_call(
        functools.partial(attend_kernel, nh, vd, docs, blocks),
        rows_n,
        scalars,
        [(qkv, 1), (num, 0), (den, 0), (pa, None), (pb, None), (frows, None)]
        + [(e, 0) for e in earlier],
        [
            ((count, rows_n, sub_len, vw), BF, 1),
            ((rows_n, length, 128), F32, 0),
            ((rows_n, nh, AUX, TILE), BF, 0),
        ],
        nh * rows_n * length * 256 * 256 * 6,
    )
    flat_cot, to_owners = cot.reshape(tokens, width), att.reshape(count, tokens, vw)
    if square():
        attended, near, w_out_other = exchange(
            to_owners, False, vw, 0, "gather", (flat_cot, w_out_piece), ((3, tokens, width), w_out_piece.shape)
        )
        cots = (flat_cot, near[0], near[1], near[2])
    else:
        (attended,) = exchange(to_owners, False, vw, 0)
        cots = (lax.all_gather(flat_cot, QUAD, axis=0, tiled=True),)
        w_out_other = swap(w_out_piece, "sc")
    w_out_halves = [w.reshape(count * vw, width // 2) for w in (w_out_piece, w_out_other)]
    attn_branch = by_halves(attended, *w_out_halves).reshape(rows_n, sub_len, width)
    middle = x + attn_branch + out_bias
    scale_two = rms_scale(middle)
    normed_two = middle * scale_two
    normed_two_low = (normed_two * mlp_gain).astype(BF)

    chunks, theirs = gather_near(normed_two_low.reshape(tokens, width), fetched, 3 * window, 4)
    w_in_piece, chunks = tie(w_in_piece, chunks)
    w_in_all = lax.all_gather(w_in_piece, ("sy", "sc", "hb", "ha"), axis=0)
    grad_two, ff_grads, branch = ff_group(chunks, cots, fetched, theirs)
    grad_two = grad_two.reshape(rows_n, sub_len, width)
    gain_two_part = jnp.sum(grad_two * normed_two, axis=(0, 1))
    scaled = grad_two * mlp_gain
    grad_middle = cot.astype(F32) + scale_two * (
        scaled - normed_two * jnp.mean(scaled * normed_two, axis=-1, keepdims=True)
    )
    bias_part = jnp.sum(grad_middle, axis=(0, 1))
    grad_branch = grad_middle.astype(BF)

    flat_branch = grad_branch.reshape(tokens, width)
    grad_att = by_halves_back(flat_branch, *w_out_halves).astype(BF)
    branch, w_in_all = tie(branch, w_in_all)
    branch = lax.psum_scatter(branch, QUAD, scatter_dimension=0, tiled=True)
    (grad_att,) = exchange(grad_att, True, vw, 1)
    ff_grads, branch, grad_att = tie(jnp.concatenate(ff_grads, axis=1), branch, grad_att)
    ff_grads = lax.psum_scatter(ff_grads, "ha", scatter_dimension=0, tiled=True)
    grad_att = grad_att.reshape(count, rows_n, sub_len, vw)
    output = (middle + branch.astype(F32).reshape(rows_n, sub_len, width)).astype(BF)
    grad_w_out = seq_sum(attended, flat_branch).reshape(count, vw, width // blocks)
    ff_grads = jnp.transpose(ff_grads.reshape(-1, 3, blocks, width // blocks), (2, 1, 0, 3))
    ff_grads = ff_grads.reshape(blocks, -1, width // blocks)
    gn, grad_states = row_call(
        functools.partial(back_state_kernel, nh, vd, docs),
        rows_n,
        scalars,
        [(qkv, 1), (grad_att, 1), (att, 1), (den, 0), (pa, None), (pb, None), (frows, None)],
        [((rows_n, length, nh * 256), BF, 0), ((rows_n, nh, AUX, TILE), BF, 0)],
        nh * rows_n * length * 256 * 256 * 4,
    )
    later = chain_pieces(grad_states, True)
    gqk, gv = row_call(
        functools.partial(back_intra_kernel, nh, vd, docs),
        rows_n,
        scalars,
        [(qkv, 1), (gn, 0), (state_in, 0), (pa, None), (pb, None), (frows, None), (align, None)],
        [((rows_n, length, 128), F32, 0), ((rows_n, length, vw), F32, 0)],
        pair * 256 * 8,
    )
    (gqkv,) = row_call(
        functools.partial(back_key_kernel, nh, vd, docs, blocks),
        rows_n,
        scalars,
        [(qkv, 1), (gqk, 0), (gv, 0), (pa, None), (pb, None), (frows, None)] + [(e, 0) for e in later],
        [((count, rows_n, sub_len, xw), BF, 1)],
        nh * rows_n * length * 256 * 256 * 6,
    )
    (grad_in,) = exchange(gqkv.reshape(count, tokens, xw), False, xw, 2, last_major=True)
    w_in_all = w_in_all.reshape(blocks, count * xw, width // blocks)
    grad_one = jnp.concatenate([dot(grad_in, w_in_all[i]) for i in range(blocks)], axis=1)
    grad_one = grad_one.reshape(rows_n, sub_len, width)
    gain_one_part = jnp.sum(grad_one * normed_one, axis=(0, 1))
    scaled = grad_one * attn_gain
    input_grad = (
        grad_middle
        + scale_one * (scaled - normed_one * jnp.mean(scaled * normed_one, axis=-1, keepdims=True))
    ).astype(BF)

    flat_tokens = count * tokens
    grad_w_in = dot(gqkv.reshape(flat_tokens, xw), normed_full.reshape(flat_tokens, width), TN)
    grad_w_in = jnp.transpose(grad_w_in.astype(BF).reshape(xw, blocks, width // blocks), (1, 0, 2))
    vectors = jnp.stack([gain_one_part, bias_part, gain_two_part])
    vectors, grad_w_in, ff_grads, grad_w_out = send_home(vectors, grad_w_in, ff_grads, grad_w_out, 5)
    ff_grads = ff_grads.astype(F32).reshape(blocks, 3, -1, width // blocks)
    grad_gate_w, grad_up_w, grad_down_w = (windows_joined(ff_grads[:, i], units) for i in range(3))
    qk_cut = vw + nh * FEAT
    return (
        jnp.transpose(output, (1, 0, 2)),
        jnp.transpose(input_grad, (1, 0, 2)),
        vectors[0],
        grad_w_in[vw:qk_cut].T,
        grad_w_in[qk_cut : qk_cut + nh * FEAT].T,
        grad_w_in[:vw].T,
        grad_w_out,
        vectors[1],
        vectors[2],
        grad_gate_w.T,
        grad_up_w.T,
        grad_down_w,
    )


def solution(mesh):
    seq, head = mesh.shape["seq"], mesh.shape["head"]
    inner = Mesh(mesh.devices.reshape(seq // 2, 2, seq, head // seq), ("sy", "sc", "ha", "hb"))
    every, heads = ("sy", "sc", "ha", "hb"), ("ha", "hb")
    placed = (
        P(every, None, None),
        P(),
        P(None, heads),
        P(None, heads),
        P(None, heads),
        P(heads, None),
        P(),
        P(),
        P(None, heads),
        P(None, heads),
        P(heads, None),
        P(every, None, None),
        P(),
    )
    return jax.shard_map(
        on_device,
        mesh=inner,
        in_specs=placed,
        out_specs=(
            P(every, None, None),
            P(every, None, None),
            P(every),
            P(SEQ, heads),
            P(SEQ, heads),
            P(SEQ, heads),
            P(heads, SEQ),
            P(every),
            P(every),
            P(SEQ, heads),
            P(SEQ, heads),
            P(heads, SEQ),
        ),
        check_vma=False,
    )
```

```python
import functools

import jax
import jax.numpy as jnp
import numpy as np
from jax import lax
from jax.experimental import pallas as pl
from jax.experimental.pallas import tpu as pltpu
from jax.sharding import Mesh
from jax.sharding import PartitionSpec as P

FEAT = 16
EPS = 1e-05
ROOT_HALF = 0.7071067811865476
TILE = 256
AUX = 136
BF = jnp.bfloat16
F32 = jnp.float32
MESH_ID = pl.DeviceIdType.MESH
NT = (((1,), (1,)), ((), ()))
TN = (((0,), (0,)), ((), ()))


def dot(a, b, dims=(((1,), (0,)), ((), ()))):
    return lax.dot_general(a, b, dims, preferred_element_type=F32)


def feature_tables(nh):
    cols = [(None, None)] + [(i, None) for i in range(FEAT)]
    cols += [(i, j) for i in range(FEAT) for j in range(i, FEAT)]
    pick_a = np.zeros((2 * nh, 128, TILE), np.float32)
    pick_b = np.zeros((2 * nh, 128, TILE), np.float32)
    rows = np.zeros((8, TILE), np.float32)
    for c, (i, j) in enumerate(cols):
        scale = 1.0 if i is None else 0.5 if j is None else 0.25 * ROOT_HALF
        rows[0, c] = 1.0 if i is None else 0.0
        rows[1, c] = 1.0 if j is None else 0.0
        rows[2, c] = scale * (2.0 if j is not None and i != j else 1.0)
        rows[3, c] = scale
        for n in range(2 * nh):
            if i is not None:
                pick_a[n, FEAT * n + i, c] = 1.0
            if j is not None:
                pick_b[n, FEAT * n + j, c] = 1.0
    align = np.zeros((4 * nh, 128, 128), np.float32)
    for h in range(nh):
        for f in range(FEAT):
            q, k = FEAT * h + f, FEAT * (nh + h) + f
            align[4 * h, q, f] = 0.25
            align[4 * h + 1, k, f] = 1.0
            align[4 * h + 2, k, q] = 0.25
            align[4 * h + 3, q, k] = 0.25
    to_low = lambda a: jnp.asarray(a, BF)
    return to_low(pick_a), to_low(pick_b), jnp.asarray(rows), to_low(align)


def begin_at(lens, row, docs, position, start_block):
    start = -start_block
    found = start + position * 0
    for j in range(docs):
        if j:
            start = start + lens[row, j - 1]
            found = jnp.where(start <= position, start, found)
    return found


def chain_weights(lens, row, docs, block, blocks, length, backward):
    out, alive = [], None
    for k in range(1, blocks):
        source = block + k if backward else block - k
        inside = (source < blocks) if backward else (source >= 0)
        here = inside if alive is None else jnp.logical_and(alive, inside)
        out.append(jnp.where(here, 1.0, 0.0).astype(F32))
        first = begin_at(lens, row, docs, length - 1, source * length)
        passes = first < 0
        alive = passes if alive is None else jnp.logical_and(alive, passes)
    return out


def lane_iota(shape):
    return lax.broadcasted_iota(jnp.int32, shape, len(shape) - 1)


def row_iota(shape):
    return lax.broadcasted_iota(jnp.int32, shape, len(shape) - 2)


def with_ones(v, lanes=(0, 1)):
    side = lane_iota(v.shape)
    ones = jnp.where((side >= lanes[0]) & (side <= lanes[1]), 1.0, 0.0).astype(BF)
    return jnp.concatenate([v, ones], axis=1)


def split_sum(state, total, third):
    rows = row_iota(state.shape)
    high = total.astype(BF).astype(F32)
    low = total - high
    out = jnp.where(rows < 128, state, 0.0)
    out = jnp.where(rows == 128, high, out)
    if third:
        out = jnp.where(rows == 129, high, out)
        out = jnp.where(rows == 130, low, out)
    else:
        out = jnp.where(rows == 129, low, out)
    return out.astype(BF)


def flat(ref):
    x = ref[...]
    return x.reshape(x.shape[0] * x.shape[2], x.shape[3])


def picks(qk, pa, pb, rows, n):
    a = dot(qk, pa[n]) + rows[0:1, :]
    b = dot(qk, pb[n]) + rows[1:2, :]
    return a, b


def state_kernel(nh, vd, docs, lens, meta, x_ref, pa, pb, rows, out):
    row = pl.program_id(0)
    x = flat(x_ref)
    length = x.shape[0]
    qk = x[:, nh * vd :]
    last = begin_at(lens, row, docs, length - 1, meta[0] * length)
    trail = row_iota((length, 2 * 128)) >= last
    for h in range(nh):
        a, b = picks(qk, pa, pb, rows, nh + h)
        kf = (a * b * rows[3:4, :]).astype(BF)
        va = jnp.where(trail, with_ones(x[:, h * vd : (h + 1) * vd]).astype(F32), 0.0).astype(BF)
        st = dot(va, kf, TN)[:AUX]
        out[0, h] = split_sum(st, st[128:129], False)


def intra_kernel(nh, vd, docs, lens, meta, x_ref, align, num_out, den_out):
    row = pl.program_id(0)
    x = flat(x_ref)
    length = x.shape[0]
    qk = x[:, nh * vd :]
    one16 = jnp.where(lane_iota((1, 128)) == FEAT, 1.0, 0.0)
    tile = min(TILE, length)
    dens = [jnp.zeros((tile, 128), F32) for _ in range(length // tile)]
    for h in range(nh):
        qa = (dot(qk, align[4 * h]) + one16).astype(BF)
        ka = (dot(qk, align[4 * h + 1]) + one16).astype(BF)
        va = with_ones(x[:, h * vd : (h + 1) * vd])
        for t in range(length // tile):
            lo, hi = t * tile, (t + 1) * tile
            s1 = dot(qa[lo:hi], ka[:hi], NT)
            w = 0.5 * (s1 * s1) + 0.5
            pos = lo + row_iota((tile, 1))
            beg = begin_at(lens, row, docs, pos, meta[0] * length)
            kpos = lane_iota(w.shape)
            w = jnp.where((kpos >= beg) & (kpos <= pos), w, 0.0).astype(BF)
            acc = dot(w, va[:hi])
            num_out[0, lo:hi, h * vd : (h + 1) * vd] = acc[:, :vd]
            lane = lane_iota((tile, 128))
            dens[t] = jnp.where(lane == h, acc[:, vd : vd + 1], dens[t])
    for t in range(length // tile):
        den_out[0, t * tile : (t + 1) * tile, :] = dens[t]


def gather_states(sts, weights, h):
    total = None
    for st, w in zip(sts, weights):
        part = st[0, h].astype(F32) * w
        total = part if total is None else total + part
    return total


def attend_kernel(nh, vd, docs, blocks, lens, meta, x_ref, num, den, pa, pb, rows, *rest):
    sts, (att_out, den_out, st_out) = rest[: blocks - 1], rest[blocks - 1 :]
    row = pl.program_id(0)
    x = flat(x_ref)
    length = x.shape[0]
    qk = x[:, nh * vd :]
    weights = chain_weights(lens, row, docs, meta[0], blocks, length, False)
    pos = row_iota((length, 1))
    carried = begin_at(lens, row, docs, pos, meta[0] * length) < 0
    lane = lane_iota((length, 128))
    dens = den[0]
    for h in range(nh):
        st = gather_states(sts, weights, h)
        st = split_sum(st, st[128:129] + st[129:130], True)
        st_out[0, h] = st
        a, b = picks(qk, pa, pb, rows, h)
        qf = (a * b * rows[2:3, :]).astype(BF)
        inter = dot(qf, st, NT)
        more = jnp.where(carried, inter[:, :vd], 0.0)
        more_den = jnp.where(carried, inter[:, 128:129] + inter[:, 130:131], 0.0)
        total = dens[:, h : h + 1] + more_den
        value = (num[0, :, h * vd : (h + 1) * vd] + more) / total
        att_out[:, 0, :, h * vd : (h + 1) * vd] = value.astype(BF).reshape(
            att_out.shape[0], att_out.shape[2], vd
        )
        dens = jnp.where(lane == h, total, dens)
    den_out[0] = dens


def back_state_kernel(nh, vd, docs, lens, meta, x_ref, ga_ref, att_ref, den, pa, pb, rows, gn_out, out):
    row = pl.program_id(0)
    x, ga, att = flat(x_ref), flat(ga_ref), flat(att_ref)
    length = x.shape[0]
    qk = x[:, nh * vd :]
    pos = row_iota((length, 1))
    carried = begin_at(lens, row, docs, pos, meta[0] * length) < 0
    side = lane_iota((length, 128))
    for h in range(nh):
        cut = slice(h * vd, (h + 1) * vd)
        inv = 1.0 / den[0, :, h : h + 1]
        gah = ga[:, cut].astype(F32) * inv
        gd = -jnp.sum(gah * att[:, cut].astype(F32), axis=1, keepdims=True)
        high = gd.astype(BF).astype(F32)
        aux = jnp.where((side == 0) | (side == 2), high, jnp.where(side == 1, gd - high, 0.0))
        gn = jnp.concatenate([gah, aux], axis=1)
        gn_out[0, :, h * 256 : (h + 1) * 256] = gn.astype(BF)
        a, b = picks(qk, pa, pb, rows, h)
        qf = (a * b * rows[2:3, :]).astype(BF)
        st = dot(jnp.where(carried, gn, 0.0).astype(BF), qf, TN)[:AUX]
        out[0, h] = split_sum(st, st[128:129] + st[129:130], False)


def back_intra_kernel(
    nh, vd, docs, lens, meta, x_ref, gn_ref, st_ref, pa, pb, rows, align, gqk_out, gv_out
):
    row = pl.program_id(0)
    x = flat(x_ref)
    length = x.shape[0]
    qk = x[:, nh * vd :]
    one16 = jnp.where(lane_iota((1, 128)) == FEAT, 1.0, 0.0)
    tile = min(TILE, length)
    pos = row_iota((length, 1))
    carried = begin_at(lens, row, docs, pos, meta[0] * length) < 0
    gqk = None
    for h in range(nh):
        qa = (dot(qk, align[4 * h]) + one16).astype(BF)
        ka = (dot(qk, align[4 * h + 1]) + one16).astype(BF)
        k_at_q = dot(qk, align[4 * h + 2]).astype(BF)
        q_at_k = dot(qk, align[4 * h + 3]).astype(BF)
        va = with_ones(x[:, h * vd : (h + 1) * vd])
        gn = gn_ref[0, :, h * 256 : (h + 1) * 256]
        st = st_ref[0, h]
        gqf = jnp.where(carried, dot(gn[:, :AUX], st), 0.0) * rows[2:3, :]
        a, b = picks(qk, pa, pb, rows, h)
        part = dot((gqf * b).astype(BF), pa[h], NT) + dot((gqf * a).astype(BF), pb[h], NT)
        gqk = part if gqk is None else gqk + part
        gk_parts = []
        gq_parts = [None] * (length // tile)
        for t in range(length // tile):
            lo, hi = t * tile, (t + 1) * tile
            s1 = dot(ka[lo:hi], qa[lo:], NT)
            w = 0.5 * (s1 * s1) + 0.5
            kpos = lo + row_iota((tile, 1))
            qpos = lo + lane_iota((1, length - lo))
            beg = begin_at(lens, row, docs, qpos, meta[0] * length)
            see = (kpos >= beg) & (kpos <= qpos)
            gw = dot(va[lo:hi], gn[lo:], NT)
            gs = jnp.where(see, gw * s1, 0.0).astype(BF)
            w = jnp.where(see, w, 0.0).astype(BF)
            gv_out[0, lo:hi, h * vd : (h + 1) * vd] = dot(w, gn[lo:, :vd])
            gk_parts.append(dot(gs, q_at_k[lo:]))
            gq = dot(gs, k_at_q[lo:hi], TN)
            for u in range(t, length // tile):
                piece = gq[(u - t) * tile : (u - t + 1) * tile]
                gq_parts[u] = piece if gq_parts[u] is None else gq_parts[u] + piece
        gqk = gqk + jnp.concatenate(gk_parts, axis=0) + jnp.concatenate(gq_parts, axis=0)
    gqk_out[0] = gqk


def back_key_kernel(nh, vd, docs, blocks, lens, meta, x_ref, gqk_ref, gv_ref, pa, pb, rows, *rest):
    sts, (out,) = rest[: blocks - 1], rest[blocks - 1 :]
    row = pl.program_id(0)
    x = flat(x_ref)
    length = x.shape[0]
    qk = x[:, nh * vd :]
    weights = chain_weights(lens, row, docs, meta[0], blocks, length, True)
    last = begin_at(lens, row, docs, length - 1, meta[0] * length)
    trail = row_iota((length, 1)) >= last
    gqk = gqk_ref[0]
    shape = (out.shape[0], out.shape[2])
    for h in range(nh):
        st = gather_states(sts, weights, h)
        st = split_sum(st, st[128:129] + st[129:130], False)
        va = with_ones(x[:, h * vd : (h + 1) * vd])
        gkf = jnp.where(trail, dot(va[:, :AUX], st), 0.0) * rows[3:4, :]
        a, b = picks(qk, pa, pb, rows, nh + h)
        gqk = gqk + dot((gkf * b).astype(BF), pa[nh + h], NT)
        gqk = gqk + dot((gkf * a).astype(BF), pb[nh + h], NT)
        kf = (a * b * rows[3:4, :]).astype(BF)
        more = jnp.where(trail, dot(kf, st[:vd], NT), 0.0)
        gv = gv_ref[0, :, h * vd : (h + 1) * vd] + more
        out[:, 0, :, h * vd : (h + 1) * vd] = gv.astype(BF).reshape(shape + (vd,))
    out[:, 0, :, nh * vd :] = gqk.astype(BF).reshape(shape + (128,))


def row_call(kernel, rows_n, scalars, ins, outs, flops):
    def spec(shape, dim):
        if dim is None:
            return pl.BlockSpec(shape, lambda r, *_: (0,) * len(shape))
        block = tuple(1 if d == dim else n for d, n in enumerate(shape))
        return pl.BlockSpec(block, lambda r, *_: tuple(r if d == dim else 0 for d in range(len(shape))))

    moved = sum(a.size * a.dtype.itemsize for a, _ in ins)
    moved += sum(int(np.prod(s)) * np.dtype(t).itemsize for s, t, _ in outs)
    return pl.pallas_call(
        kernel,
        out_shape=tuple(jax.ShapeDtypeStruct(s, t) for s, t, _ in outs),
        grid_spec=pltpu.PrefetchScalarGridSpec(
            num_scalar_prefetch=len(scalars),
            grid=(rows_n,),
            in_specs=[spec(a.shape, d) for a, d in ins],
            out_specs=[spec(s, d) for s, t, d in outs],
        ),
        compiler_params=pltpu.CompilerParams(vmem_limit_bytes=56 * 1024 * 1024),
        cost_estimate=pl.CostEstimate(flops=int(flops), bytes_accessed=int(moved), transcendentals=0),
    )(*scalars, *[a for a, _ in ins])


SEQ = ("sy", "sc")
HEAD = ("ha", "hb")


def here():
    return tuple(lax.axis_index(n) for n in ("sy", "sc", "ha", "hb"))


def remote(src, dst, ssem, rsem, k, device):
    return pltpu.make_async_remote_copy(
        src_ref=src,
        dst_ref=dst,
        send_sem=ssem.at[k],
        recv_sem=rsem.at[k],
        device_id=device,
        device_id_type=MESH_ID,
    )


def greet(devices):
    bar = pltpu.get_barrier_semaphore()
    for device in devices:
        pl.semaphore_signal(bar, 1, device_id=device, device_id_type=MESH_ID)
    pl.semaphore_wait(bar, len(devices))


def square():
    return tuple(lax.axis_size(n) for n in ("sy", "ha", "hb")) == (2, 4, 2)


def place(block, head, special):
    if special:
        ha = 2 * (block % 2) + block // 2
        return (head // 2 + ha % 2) % 2, head % 2, ha
    return head // 2, head % 2, block


def own_place():
    sy, sc, ha, _ = here()
    if square():
        return 2 * (ha % 2) + ha // 2, 2 * ((sy + ha) % 2) + sc
    return ha, sy * 2 + sc


def first_head(block):
    return block % 2 if square() else block


def home_of(head, special):
    if special:
        return 2 * (head % 2) + head // 2, 2 * ((head // 2 + head) % 2) + head % 2
    return head, head


def maybe_own(k, own, elsewhere, alone):
    if k:
        elsewhere()
    else:
        pl.when(jnp.logical_not(own))(elsewhere)
        pl.when(own)(alone)


def exchange_kernel(to_blocks, width, last_major, extra, src, *refs):
    n_in, n_out = {None: (0, 0), "gather": (2, 2), "scatter": (1, 2)}[extra]
    ins, dst, outs, sems = refs[:n_in], refs[n_in], refs[n_in + 1 : n_in + 1 + n_out], refs[n_in + 1 + n_out :]
    ssem, rsem, lsem = sems[:3]
    sy, sc, a, b = here()
    s = sy * 2 + sc
    block, head = own_place()
    special = square()
    size_a, size_b = lax.axis_size("ha"), lax.axis_size("hb")
    count = size_a * size_b
    bar = pltpu.get_barrier_semaphore()
    same = s == block

    def at(k):
        i, pb = k // size_b, lax.rem(b + k % size_b, size_b)
        if to_blocks:
            sender = (block // 2, block % 2, lax.rem(a + i, size_a), pb)
            to = lax.rem(a - place(s, 0, special)[2] + first_head(s) + i + size_a, size_a)
            piece = to * size_b + pb
            source = src.at[:, pl.ds(pl.multiple_of(piece * width, 128), width)]
            return sender, source, dst.at[a * size_b + b], place(s, to, special) + (pb,)
        sender = place(s, lax.rem(first_head(s) + i, size_a), special) + (pb,)
        to = lax.rem(head - first_head(block) + a + i + size_a, size_a)
        column = b * size_a + head if last_major else head * size_b + b
        far = dst.at[:, pl.ds(pl.multiple_of(column * width, 128), width)]
        return sender, src.at[to * size_b + pb], far, (block // 2, block % 2, to, pb)

    def copy(k):
        _, source, far, receiver = at(k)
        return remote(source, far, ssem, rsem, k, receiver)

    def local():
        return pltpu.make_async_copy(at(0)[1], at(0)[2], lsem.at[0])

    def signal(device):
        pl.semaphore_signal(bar, 1, device_id=device, device_id_type=MESH_ID)

    to_x, to_y, to_core = (sy, sc, a, 1 - b), (1 - sy, sc, a, b), (sy, 1 - sc, a, b)
    expected = count - same.astype(jnp.int32)
    for k in range(count):
        maybe_own(k, same, functools.partial(signal, at(k)[0]), lambda: None)
    if extra in ("gather", "scatter"):
        greeted = (to_x, to_y, to_core)[: 3 if extra == "gather" else 2]
        for device in greeted:
            signal(device)
        expected = expected + len(greeted)
    pl.semaphore_wait(bar, expected)
    for k in range(count):
        maybe_own(k, same, lambda: copy(k).start(), lambda: local().start())

    if extra == "gather":
        (more, own_w), (near, other_w) = ins, outs
        gsem, hsem = sems[3:]
        half = more.shape[0] // 2
        low, high = pl.ds(0, half), pl.ds(half, half)
        copies = [
            remote(more, near.at[1], gsem, hsem, 0, to_x),
            remote(more, near.at[2], gsem, hsem, 1, to_y),
            remote(own_w, other_w, gsem, hsem, 4, to_core),
        ]
        for c in copies:
            c.start()
        stay = pltpu.make_async_copy(more, near.at[0], lsem.at[1])
        stay.start()
        copies[0].wait_recv()
        copies.append(remote(near.at[1, high], near.at[3, high], gsem, hsem, 2, to_y))
        copies[3].start()
        copies[1].wait_recv()
        copies.append(remote(near.at[2, low], near.at[3, low], gsem, hsem, 3, to_x))
        copies[4].start()
        stay.wait()
        for c in copies[2:]:
            c.wait_recv()
        for c in copies:
            c.wait_send()
    if extra == "scatter":
        (parts,), (got, relay) = ins, outs
        gsem, hsem = sems[3:]
        half = parts.shape[1] // 2
        low, high = pl.ds(0, half), pl.ds(half, half)
        copies = [
            remote(parts.at[3, low], relay.at[0], gsem, hsem, 0, to_x),
            remote(parts.at[3, high], relay.at[1], gsem, hsem, 1, to_y),
            remote(parts.at[1], got.at[0], gsem, hsem, 2, to_x),
            remote(parts.at[2], got.at[1], gsem, hsem, 3, to_y),
        ]
        for c in copies:
            c.start()
        copies[0].wait_recv()
        copies.append(remote(relay.at[0], got.at[2, low], gsem, hsem, 4, to_y))
        copies[4].start()
        copies[1].wait_recv()
        copies.append(remote(relay.at[1], got.at[2, high], gsem, hsem, 5, to_x))
        copies[5].start()
        for c in copies[2:]:
            c.wait_recv()
        for c in copies:
            c.wait_send()
    for k in range(count):
        maybe_own(k, same, lambda: copy(k).wait(), lambda: local().wait())


def exchange(x, to_blocks, width, collective, extra=None, ins=(), outs=(), last_major=False):
    count = lax.axis_size("ha") * lax.axis_size("hb")
    tokens = x.shape[0] if to_blocks else x.shape[1]
    shape = (count, tokens, width) if to_blocks else (tokens, count * width)
    any_space = pl.BlockSpec(memory_space=pl.ANY)
    more = {None: 0, "gather": 5, "scatter": 6}[extra]
    return pl.pallas_call(
        functools.partial(exchange_kernel, to_blocks, width, last_major, extra),
        out_shape=[jax.ShapeDtypeStruct(s, x.dtype) for s in (shape, *outs)],
        in_specs=[any_space] * (1 + len(ins)),
        out_specs=[any_space] * (1 + len(outs)),
        scratch_shapes=[
            pltpu.SemaphoreType.DMA((count,)),
            pltpu.SemaphoreType.DMA((count,)),
            pltpu.SemaphoreType.DMA((2,)),
        ]
        + [pltpu.SemaphoreType.DMA((more,))] * (2 if more else 0),
        compiler_params=pltpu.CompilerParams(collective_id=collective, has_side_effects=True),
        cost_estimate=pl.CostEstimate(flops=0, bytes_accessed=x.size * 500, transcendentals=0),
    )(x, *ins)


def home_kernel(*refs):
    src, grads, windows, shards, dst, grads_got, windows_got, shards_got = refs[:8]
    ssem, rsem, lsem, gsem, hsem, usem, vsem = refs[8:]
    sy, sc, a, b = here()
    s = sy * 2 + sc
    block, head = own_place()
    special = square()
    size_a, size_b = lax.axis_size("ha"), lax.axis_size("hb")
    devices = src.shape[0]
    me = (s * size_a + a) * size_b + b
    homely = head == a
    block_h, seq_h = home_of(head, special)
    bar = pltpu.get_barrier_semaphore()

    def peer(k):
        i = lax.rem(me + k, devices)
        rest = i // (size_a * size_b)
        return i, (rest // 2, rest % 2, i // size_b % size_a, i % size_b)

    def copy(k):
        i, device = peer(k)
        return remote(src.at[i], dst.at[me], ssem, rsem, k, device)

    def grad_ends(k):
        e = lax.rem(block - block_h + seq_h + k + size_a, size_a)
        return grads.at[e], grads_got.at[block], (e // 2, e % 2, head, b)

    def grad_copy(k):
        source, far, device = grad_ends(k)
        return remote(source, far, gsem, hsem, k, device)

    def grad_local():
        return pltpu.make_async_copy(*grad_ends(0)[:2], lsem.at[1])

    def window_copy(k):
        e = lax.rem(s + k, size_a)
        return remote(windows.at[e], windows_got.at[s], gsem, hsem, size_a + k, (e // 2, e % 2, a, b))

    def shard_copy(k):
        pa = lax.rem(a + k, size_a)
        return remote(shards.at[pa], shards_got.at[a], usem, vsem, k, (sy, sc, pa, b))

    @pl.loop(1, devices)
    def _(k):
        pl.semaphore_signal(bar, 1, device_id=peer(k)[1], device_id_type=MESH_ID)

    stay = [
        pltpu.make_async_copy(shards.at[a], shards_got.at[a], lsem.at[3]),
        pltpu.make_async_copy(src.at[me], dst.at[me], lsem.at[0]),
        pltpu.make_async_copy(windows.at[s], windows_got.at[s], lsem.at[2]),
    ]
    for c in stay:
        c.start()
    pl.semaphore_wait(bar, devices - 1)
    for k in range(size_a):
        maybe_own(k, homely, lambda: grad_copy(k).start(), lambda: grad_local().start())
        if k:
            window_copy(k).start()
    for k in range(1, size_a):
        shard_copy(k).start()

    @pl.loop(1, devices)
    def _(k):
        copy(k).start()

    @pl.loop(1, devices)
    def _(k):
        copy(k).wait()

    for k in range(size_a):
        maybe_own(k, homely, lambda: grad_copy(k).wait(), lambda: grad_local().wait())
        if k:
            window_copy(k).wait()
    for k in range(1, size_a):
        shard_copy(k).wait()
    for c in stay:
        c.wait()


def send_home(x, grads, windows, shards, collective):
    devices = 2 * lax.axis_size("sy") * lax.axis_size("ha") * lax.axis_size("hb")
    vectors, share = x.shape[0], x.shape[1] // devices
    x = jnp.transpose(x.reshape(vectors, devices, share), (1, 0, 2))
    x = jnp.pad(x, ((0, 0), (0, 8 - vectors), (0, 128 - share)))
    any_space = pl.BlockSpec(memory_space=pl.ANY)
    ins = [x, grads, windows, shards]
    size_a, heads = lax.axis_size("ha"), shards.shape[0]
    out = pl.pallas_call(
        home_kernel,
        out_shape=[jax.ShapeDtypeStruct(v.shape, v.dtype) for v in ins],
        in_specs=[any_space] * len(ins),
        out_specs=[any_space] * len(ins),
        scratch_shapes=[
            pltpu.SemaphoreType.DMA((devices,)),
            pltpu.SemaphoreType.DMA((devices,)),
            pltpu.SemaphoreType.DMA((4,)),
            pltpu.SemaphoreType.DMA((2 * size_a,)),
            pltpu.SemaphoreType.DMA((2 * size_a,)),
            pltpu.SemaphoreType.DMA((heads,)),
            pltpu.SemaphoreType.DMA((heads,)),
        ],
        compiler_params=pltpu.CompilerParams(collective_id=collective, has_side_effects=True),
        cost_estimate=pl.CostEstimate(flops=0, bytes_accessed=100000000, transcendentals=0),
    )(*ins)
    vectors = jnp.sum(out[0], axis=0)[:vectors, :share]
    return vectors, jnp.sum(out[1].astype(F32), axis=0), out[2], jnp.sum(out[3].astype(F32), axis=0)


def near_kernel(rows, src, weights, near, theirs, gsem, hsem, lsem):
    sy, sc, a, b = here()
    to_x, to_y, to_core = (sy, sc, a, 1 - b), (1 - sy, sc, a, b), (sy, 1 - sc, a, b)
    half = src.shape[0] // 2
    low, high = pl.ds(0, half), pl.ds(half, half)
    greet((to_x, to_y, to_core))
    copies = [
        remote(src, near.at[1], gsem, hsem, 0, to_x),
        remote(src, near.at[2], gsem, hsem, 1, to_y),
        remote(weights.at[:, pl.ds(0, rows)], theirs, gsem, hsem, 4, to_core),
    ]
    for copy in copies:
        copy.start()
    stay = pltpu.make_async_copy(src, near.at[0], lsem)
    stay.start()
    copies[0].wait_recv()
    copies.append(remote(near.at[1, high], near.at[3, high], gsem, hsem, 2, to_y))
    copies[3].start()
    copies[1].wait_recv()
    copies.append(remote(near.at[2, low], near.at[3, low], gsem, hsem, 3, to_x))
    copies[4].start()
    stay.wait()
    for copy in copies[2:]:
        copy.wait_recv()
    for copy in copies:
        copy.wait_send()


def gather_near(x, weights, rows, collective):
    if not square():
        return lax.all_gather(x, QUAD, axis=0, tiled=True)[None], swap(weights[:, :rows], "sc")
    any_space = pl.BlockSpec(memory_space=pl.ANY)
    near, theirs = pl.pallas_call(
        functools.partial(near_kernel, rows),
        out_shape=[
            jax.ShapeDtypeStruct((4,) + x.shape, x.dtype),
            jax.ShapeDtypeStruct((weights.shape[0], rows, weights.shape[2]), weights.dtype),
        ],
        in_specs=[any_space] * 2,
        out_specs=[any_space] * 2,
        scratch_shapes=[pltpu.SemaphoreType.DMA((5,))] * 2 + [pltpu.SemaphoreType.DMA],
        compiler_params=pltpu.CompilerParams(collective_id=collective, has_side_effects=True),
        cost_estimate=pl.CostEstimate(flops=0, bytes_accessed=x.size * 200, transcendentals=0),
    )(x, weights)
    return near, theirs


def start_kernel(parts, src, w_in, w_out, dst, w_in_home, w_out_all, ssem, rsem, lsem, wsem, vsem):
    sy, sc, a, b = here()
    block, head = own_place()
    size = lax.axis_size("ha")
    target = place(sy * 2 + sc, a, True) + (b,)
    source = (block // 2, block % 2, head, b)
    same = jnp.logical_and(sy * 2 + sc == block, a == head)
    apart = jnp.logical_not(same)
    to_x, to_y, to_core = (sy, sc, a, 1 - b), (1 - sy, sc, a, b), (sy, 1 - sc, a, b)
    to_up, to_down = (sy, sc, a + 1, b), (sy, sc, a - 1, b)
    has_up, has_down = a < size - 1, a > 0
    bar = pltpu.get_barrier_semaphore()

    def signal(device):
        pl.semaphore_signal(bar, 1, device_id=device, device_id_type=MESH_ID)

    for device in (to_x, to_y, to_core):
        signal(device)
    pl.when(apart)(lambda: signal(source))
    pl.when(has_up)(lambda: signal(to_up))
    pl.when(has_down)(lambda: signal(to_down))
    own_w = pltpu.make_async_copy(w_out, w_out_all.at[a * 2 + b], lsem.at[parts])
    own_w.start()
    pl.semaphore_wait(
        bar, 3 + apart.astype(jnp.int32) + has_up.astype(jnp.int32) + has_down.astype(jnp.int32)
    )

    step = src.shape[0] // parts
    count = 9
    half = src.shape[1] // 2

    def piece(z, x, r, lo=0, n=None):
        return dst.at[z * 2 + x, pl.ds(r * step, step), pl.ds(lo, src.shape[1] if n is None else n)]

    def make(k, r, ref, device):
        return remote(ref, ref, ssem, rsem, count * r + k, device)

    def home(r):
        return remote(src.at[pl.ds(r * step, step)], piece(a, b, r), ssem, rsem, count * r, target)

    def stay(r):
        return pltpu.make_async_copy(src.at[pl.ds(r * step, step)], piece(a, b, r), lsem.at[r])

    def w_home():
        return pltpu.make_async_remote_copy(
            src_ref=w_in,
            dst_ref=w_in_home,
            send_sem=wsem.at[0],
            recv_sem=wsem.at[1],
            device_id=target,
            device_id_type=MESH_ID,
        )

    def w_stay():
        return pltpu.make_async_copy(w_in, w_in_home, lsem.at[parts + 1])

    for r in range(parts):
        pl.when(apart)(lambda: home(r).start())
        pl.when(same)(lambda: stay(r).start())

    def send_w(k, pa, device):
        ref = w_out_all.at[pa * 2 + b]
        return remote(ref, ref, vsem.at[0], vsem.at[1], k, device)

    def spread(k, pa, up, down):
        if up:
            pl.when(has_up)(lambda: send_w(k, pa, to_up).start())
        if down:
            pl.when(has_down)(lambda: send_w(size + k, pa, to_down).start())
        send_w(2 * size + pa, pa, to_x).start()

    def w_step(k):
        @pl.when(a - k >= 0)
        def _():
            send_w(k - 1, a - k, to_x).wait_recv()
            spread(k, a - k, True, False)

        @pl.when(a + k < size)
        def _():
            send_w(size + k - 1, a + k, to_x).wait_recv()
            spread(k, a + k, False, True)

    across_y, across_c = (head + 2) % 4, head + 1 - 2 * (head % 2)
    across = (across_y + 1) - 2 * (across_y % 2)
    sent = []

    def go(copy):
        copy.start()
        sent.append(copy)

    def arrive(k, r, ref):
        make(k, r, ref, to_x).wait_recv()

    def stage_0(r):
        pl.when(apart)(lambda: arrive(0, r, piece(head, b, r)))
        pl.when(same)(lambda: stay(r).wait())
        for k, device in ((1, to_x), (2, to_y), (3, to_core)):
            go(make(k, r, piece(head, b, r), device))

    def stage_1(r):
        arrive(1, r, piece(head, 1 - b, r))
        go(make(4, r, piece(head, 1 - b, r, half, half), to_y))
        go(make(5, r, piece(head, 1 - b, r), to_core))
        arrive(2, r, piece(across_y, b, r))
        go(make(6, r, piece(across_y, b, r, 0, half), to_x))
        go(make(7, r, piece(across_y, b, r), to_core))

    def stage_2(r):
        arrive(4, r, piece(across_y, 1 - b, r, half, half))
        arrive(6, r, piece(across_y, 1 - b, r, 0, half))
        go(make(8, r, piece(across_y, 1 - b, r), to_core))

    def stage_3(r):
        arrive(3, r, piece(across_c, b, r))
        arrive(5, r, piece(across_c, 1 - b, r))
        arrive(7, r, piece(across, b, r))
        arrive(8, r, piece(across, 1 - b, r))

    stages = (stage_0, stage_1, stage_2, stage_3)
    for t in range(parts + 3):
        for i, stage in enumerate(stages):
            if 0 <= t - i < parts:
                stage(t - i)
        if t == 0:
            pl.when(apart)(lambda: w_home().start())
            pl.when(same)(lambda: w_stay().start())
            own_w.wait()
            spread(0, a, True, True)
        elif t < size:
            w_step(t)
    for k in range(parts + 3, size):
        w_step(k)
    pl.when(apart)(lambda: w_home().wait_recv())
    pl.when(same)(lambda: w_stay().wait())
    for k in range(size):
        ref = w_out_all.at[k * 2 + 1 - b]
        remote(ref, ref, vsem.at[0], vsem.at[1], 2 * size + k, to_x).wait_recv()
        send_w(2 * size + k, k, to_x).wait_send()
        pl.when(jnp.logical_and(has_up, a - k >= 0))(lambda: send_w(k, a - k, to_x).wait_send())
        pl.when(jnp.logical_and(has_down, a + k < size))(lambda: send_w(size + k, a + k, to_x).wait_send())
    for copy in sent:
        copy.wait_send()
    for r in range(parts):
        pl.when(apart)(lambda: home(r).wait_send())
    pl.when(apart)(lambda: w_home().wait_send())


def start(x, w_in, w_out, collective):
    if not square():
        size = lax.axis_size("ha")
        perm = [(s * size + z, z * size + s) for s in range(size) for z in range(size)]
        x, w_in = (lax.ppermute(v, ("sy", "sc", "ha"), perm) for v in (x, w_in))
        return lax.all_gather(x, ("sy", "sc", "hb"), axis=0), w_in, lax.all_gather(w_out, HEAD, axis=0)
    parts = x.shape[0]
    return pl.pallas_call(
        functools.partial(start_kernel, parts),
        out_shape=[
            jax.ShapeDtypeStruct((8,) + x.shape, x.dtype),
            jax.ShapeDtypeStruct(w_in.shape, w_in.dtype),
            jax.ShapeDtypeStruct((8,) + w_out.shape, w_out.dtype),
        ],
        in_specs=[pl.BlockSpec(memory_space=pl.ANY)] * 3,
        out_specs=[pl.BlockSpec(memory_space=pl.ANY)] * 3,
        scratch_shapes=[
            pltpu.SemaphoreType.DMA((9 * parts,)),
            pltpu.SemaphoreType.DMA((9 * parts,)),
            pltpu.SemaphoreType.DMA((parts + 2,)),
            pltpu.SemaphoreType.DMA((2,)),
            pltpu.SemaphoreType.DMA((2, 12)),
        ],
        compiler_params=pltpu.CompilerParams(collective_id=collective, has_side_effects=True),
        cost_estimate=pl.CostEstimate(flops=0, bytes_accessed=x.size * 400, transcendentals=0),
    )(x, w_in, w_out)


def swap(x, axis):
    return lax.ppermute(x, axis, [(0, 1), (1, 0)])


def seat(block, head, size, special):
    sy, sc, ha = place(block, head, special)
    return (sy * 2 + sc) * size + ha


def chain_pieces(x, backward):
    size, special = lax.axis_size("ha"), square()
    out = []
    for k in range(1, size):
        perm = []
        for i in range(size - k):
            ends = (i + k, i) if backward else (i, i + k)
            perm += [tuple(seat(e, h, size, special) for e in ends) for h in range(size)]
        out.append(lax.ppermute(x, SEQ + ("ha",), perm))
    return out


def tie(*values):
    return lax.optimization_barrier(values)


def my_columns(x, by_core):
    parts, place_of = lax.axis_size("sy") * 2, lax.axis_index("sy") * 2 + lax.axis_index("sc")
    if by_core:
        parts, place_of = 2, lax.axis_index("sc")
    size = x.shape[1] // parts
    return lax.dynamic_slice_in_dim(x, place_of * size, size, 1)


def by_halves(a, own, other):
    own, other = dot(a, own), dot(a, other)
    first = lax.axis_index("sc") == 0
    return jnp.concatenate([jnp.where(first, own, other), jnp.where(first, other, own)], axis=1)


def by_halves_back(a, own, other):
    size = own.shape[1]
    core = lax.axis_index("sc")
    ours, theirs = (lax.dynamic_slice_in_dim(a, i * size, size, 1) for i in (core, 1 - core))
    return dot(ours, own, NT) + dot(theirs, other, NT)


def unit_window(x, size):
    units = x.shape[0]
    window = -(-units // (size * 16)) * 16
    place = lax.axis_index("sy") * 2 + lax.axis_index("sc")
    start = jnp.minimum(place * window, units - window)
    part = lax.dynamic_slice_in_dim(x, start, window, 0)
    fresh = start + lax.broadcasted_iota(jnp.int32, part.shape, 0) >= place * window
    return jnp.where(fresh, part, jnp.zeros_like(part))


def windows_joined(parts, units):
    size, window = parts.shape[0], parts.shape[1]
    pieces = []
    for i in range(size):
        start = min(i * window, units - window)
        pieces.append(parts[i, max(i * window - start, 0) :])
    return jnp.concatenate(pieces, axis=0)


def ff_kernel(n2, cot, mine, theirs, gg_out, gu_out, hid_out, part_out, acc):
    shard = pl.program_id(1)

    def work(w, first):
        x, c = n2[0], cot[0]
        window, width = w.shape[1] // 3, w.shape[2]
        w_gate, w_up, w_down = (w[:, i * window : (i + 1) * window].reshape(-1, width) for i in range(3))
        gate, up, gh = dot(x, w_gate, NT), dot(x, w_up, NT), dot(c, w_down, NT)
        sig = jax.nn.sigmoid(gate)
        act = gate * sig
        hid_out[0, 0] = (act * up).astype(BF)
        gg = (gh * up * (sig + act * (1.0 - sig))).astype(BF)
        gu = (gh * act).astype(BF)
        gg_out[0, 0] = gg
        gu_out[0, 0] = gu
        back = dot(gg, w_gate) + dot(gu, w_up)
        if first:
            acc[...] = back
        else:
            part_out[0] = (acc[...] + back).astype(BF)

    @pl.when(shard == 0)
    def _():
        work(mine, True)

    @pl.when(shard == 1)
    def _():
        work(theirs, False)


def ff_pass(n2, cots, mine, theirs):
    chunks, tokens, width = n2.shape
    units = theirs.shape[0] * theirs.shape[1] // 3
    keep = jax.ShapeDtypeStruct((2, chunks, tokens, units), BF)
    whole = pl.BlockSpec((1, tokens, width), lambda c, i: (c, 0, 0))
    weights = pl.BlockSpec(theirs.shape, lambda c, i: (0, 0, 0), pipeline_mode=pl.Buffered(1))
    piece = pl.BlockSpec((1, 1, tokens, units), lambda c, i: (i, c, 0, 0))
    return pl.pallas_call(
        ff_kernel,
        out_shape=(keep, keep, keep, jax.ShapeDtypeStruct((chunks, tokens, width), BF)),
        grid=(chunks, 2),
        in_specs=[whole, whole, weights, weights],
        out_specs=[piece, piece, piece, whole],
        scratch_shapes=[pltpu.VMEM((tokens, width), F32)],
        compiler_params=pltpu.CompilerParams(vmem_limit_bytes=60 * 1024 * 1024),
        cost_estimate=pl.CostEstimate(
            flops=chunks * tokens * width * units * 20,
            bytes_accessed=12 * units * width + 8 * chunks * tokens * width,
            transcendentals=0,
        ),
    )(n2, cots, mine, theirs)


def branch_kernel(order, hidden, mine, theirs, out):
    width = out.shape[1]
    part = dot(hidden[0, 0], mine[...].reshape(-1, width)) + dot(hidden[1, 0], theirs[...].reshape(-1, width))
    out[...] = part.astype(BF)


def branch_product(hidden, mine, theirs):
    _, chunks, tokens, units = hidden.shape
    size, rows, width = theirs.shape
    weights = pl.BlockSpec((size, rows // 3, width), lambda i, m: (0, 2, 0), pipeline_mode=pl.Buffered(1))
    y, b = lax.axis_index("sy"), lax.axis_index("hb")
    turns = ((y, b), (y, 1 - b), (1 - y, b), (1 - y, 1 - b))[:chunks]
    order = jnp.stack([p * 2 + q if chunks > 1 else 0 * p for p, q in turns]).astype(jnp.int32)
    return pl.pallas_call(
        branch_kernel,
        out_shape=jax.ShapeDtypeStruct((chunks * tokens, width), BF),
        grid_spec=pltpu.PrefetchScalarGridSpec(
            num_scalar_prefetch=1,
            grid=(chunks,),
            in_specs=[pl.BlockSpec((2, 1, tokens, units), lambda i, m: (0, i, 0, 0)), weights, weights],
            out_specs=pl.BlockSpec((tokens, width), lambda i, m: (m[i], 0)),
        ),
        compiler_params=pltpu.CompilerParams(vmem_limit_bytes=40 * 1024 * 1024),
        cost_estimate=pl.CostEstimate(
            flops=chunks * tokens * units * width * 4, bytes_accessed=12 * units * width, transcendentals=0
        ),
    )(order, hidden, mine, theirs)


QUAD = ("sy", "hb")


def add_low(a, b):
    return (a.astype(F32) + b.astype(F32)).astype(BF)


def ring_sum(parts, meanwhile):
    own, to_x, to_y, across = parts
    half = own.shape[0] // 2
    via_x, via_y = swap(across[:half], "hb"), swap(across[half:], "sy")
    x_low, y_high = swap(to_x[:half], "hb"), swap(to_y[half:], "sy")
    work = meanwhile(0)
    via_x, via_y, *work = tie(via_x, via_y, *work)
    meanwhile(0, work)
    y_low = swap(add_low(to_y[:half], via_x), "sy")
    x_high = swap(add_low(to_x[half:], via_y), "hb")
    work = meanwhile(1)
    y_low, x_high, *work = tie(y_low, x_high, *work)
    meanwhile(1, work)
    low = own[:half].astype(F32) + x_low.astype(F32) + y_low.astype(F32)
    high = own[half:].astype(F32) + x_high.astype(F32) + y_high.astype(F32)
    return jnp.concatenate([low, high], axis=0)


def core_sum(a, b):
    size_y, core = lax.axis_size("sy"), lax.axis_index("sc")
    size = b.shape[1] // (size_y * 2)

    def of_core(c):
        columns = [lax.dynamic_slice_in_dim(b, (i * 2 + c) * size, size, 1) for i in range(size_y)]
        return jnp.concatenate(columns, axis=1)

    given = swap(dot(a, of_core(1 - core), TN).astype(BF), "sc")
    part = (dot(a, of_core(core), TN) + given.astype(F32)).astype(BF)
    return jnp.stack([part[:, i * size : (i + 1) * size] for i in range(size_y)])


def quad_sum(parts, meanwhile):
    if len(parts) == 4:
        return ring_sum(parts, meanwhile)
    for stage in (0, 1):
        meanwhile(stage)
    return lax.psum_scatter(parts[0], QUAD, scatter_dimension=0, tiled=True).astype(F32)


def ff_group(chunks, cots, mine, theirs):
    *kept, part = ff_pass(chunks, cots, mine, theirs)
    grads, branch = [], []
    width = chunks.shape[-1]
    flat = [k.reshape(2, -1, k.shape[-1]) for k in kept] + [chunks.reshape(-1, width), cots.reshape(-1, width)]
    pairs = [(flat[0], flat[3]), (flat[1], flat[3]), (flat[2], flat[4])]

    def meanwhile(stage, results=None):
        if results is not None:
            grads[:] = results[:3]
            branch[:] = results[3:]
            return None
        if stage == 0:
            grads.extend(swap(dot(a[1], b, TN).astype(BF), "sc") for a, b in pairs)
            return grads
        for i, (a, b) in enumerate(pairs):
            grads[i] = (dot(a[0], b, TN) + grads[i].astype(F32)).astype(BF)
        branch.append(branch_product(kept[2], mine, theirs))
        return grads + branch

    return quad_sum([part[i] for i in range(part.shape[0])], meanwhile), grads, branch[0]


def rms_scale(x):
    return lax.rsqrt(jnp.mean(x * x, axis=-1, keepdims=True) + EPS)


def on_device(
    inputs,
    attn_gain,
    w_query,
    w_key,
    w_value,
    w_out,
    out_bias,
    mlp_gain,
    gate_weight,
    up_weight,
    down_weight,
    cotangent,
    doc_lengths,
):
    every = ("sy", "sc", "ha", "hb")
    blocks = lax.axis_size("sy") * 2
    size_a, size_b = lax.axis_size("ha"), lax.axis_size("hb")
    count = size_a * size_b
    sub_len, rows_n, width = inputs.shape
    docs = doc_lengths.shape[1]
    nh = w_query.shape[1] // FEAT
    vd = w_value.shape[1] // nh
    vw = nh * vd
    xw = vw + 128
    length = sub_len * count
    tokens = rows_n * sub_len
    meta = own_place()[0].astype(jnp.int32).reshape(1)
    pa, pb, frows, align = feature_tables(nh)
    scalars = (doc_lengths, meta)

    x = jnp.transpose(inputs, (1, 0, 2)).astype(F32)
    cot = jnp.transpose(cotangent, (1, 0, 2))
    scale_one = rms_scale(x)
    normed_one = x * scale_one
    pad = jnp.zeros((128 - 2 * nh * FEAT, width), BF)
    w_in = jnp.concatenate([w_value.T, w_query.T, w_key.T, pad], axis=0)
    units = down_weight.shape[0]
    windows = [unit_window(w, blocks) for w in (gate_weight.T, up_weight.T, down_weight)]
    w_in_piece = my_columns(w_in, False)
    to_fetch = jnp.concatenate(windows, axis=0)
    normed_full, w_in_home, w_out_piece = start((normed_one * attn_gain).astype(BF), w_in, my_columns(w_out, True), 3)
    to_fetch, normed_full = tie(to_fetch, normed_full)
    fetched = lax.all_gather(to_fetch, "ha", axis=0)
    window = windows[0].shape[0]

    qkv = jnp.einsum("grtd,cd->grtc", normed_full, w_in_home, preferred_element_type=F32).astype(BF)
    pair = nh * rows_n * length * length
    (states,) = row_call(
        functools.partial(state_kernel, nh, vd, docs),
        rows_n,
        scalars,
        [(qkv, 1), (pa, None), (pb, None), (frows, None)],
        [((rows_n, nh, AUX, TILE), BF, 0)],
        nh * rows_n * length * 256 * 256 * 4,
    )
    earlier = chain_pieces(states, False)
    num, den = row_call(
        functools.partial(intra_kernel, nh, vd, docs),
        rows_n,
        scalars,
        [(qkv, 1), (align, None)],
        [((rows_n, length, vw), F32, 0), ((rows_n, length, 128), F32, 0)],
        pair * 256 * 4,
    )
    att, den, state_in = row_call(
        functools.partial(attend_kernel, nh, vd, docs, blocks),
        rows_n,
        scalars,
        [(qkv, 1), (num, 0), (den, 0), (pa, None), (pb, None), (frows, None)]
        + [(e, 0) for e in earlier],
        [
            ((count, rows_n, sub_len, vw), BF, 1),
            ((rows_n, length, 128), F32, 0),
            ((rows_n, nh, AUX, TILE), BF, 0),
        ],
        nh * rows_n * length * 256 * 256 * 6,
    )
    flat_cot, to_owners = cot.reshape(tokens, width), att.reshape(count, tokens, vw)
    if square():
        attended, cots, w_out_other = exchange(
            to_owners, False, vw, 0, "gather", (flat_cot, w_out_piece), ((4, tokens, width), w_out_piece.shape)
        )
    else:
        (attended,) = exchange(to_owners, False, vw, 0)
        cots = lax.all_gather(flat_cot, QUAD, axis=0, tiled=True)[None]
        w_out_other = swap(w_out_piece, "sc")
    w_out_halves = [w.reshape(count * vw, width // 2) for w in (w_out_piece, w_out_other)]
    attn_branch = by_halves(attended, *w_out_halves).reshape(rows_n, sub_len, width)
    middle = x + attn_branch + out_bias
    scale_two = rms_scale(middle)
    normed_two = middle * scale_two
    normed_two_low = (normed_two * mlp_gain).astype(BF)

    chunks, theirs = gather_near(normed_two_low.reshape(tokens, width), fetched, 3 * window, 4)
    w_in_piece, chunks = tie(w_in_piece, chunks)
    w_in_all = lax.all_gather(w_in_piece, ("sy", "sc", "hb", "ha"), axis=0)
    grad_two, ff_grads, branch = ff_group(chunks, cots, fetched, theirs)
    grad_two = grad_two.reshape(rows_n, sub_len, width)
    gain_two_part = jnp.sum(grad_two * normed_two, axis=(0, 1))
    scaled = grad_two * mlp_gain
    grad_middle = cot.astype(F32) + scale_two * (
        scaled - normed_two * jnp.mean(scaled * normed_two, axis=-1, keepdims=True)
    )
    bias_part = jnp.sum(grad_middle, axis=(0, 1))
    grad_branch = grad_middle.astype(BF)

    flat_branch = grad_branch.reshape(tokens, width)
    grad_att = by_halves_back(flat_branch, *w_out_halves).astype(BF)
    branch, w_in_all = tie(branch, w_in_all)
    branch = lax.psum_scatter(branch, QUAD, scatter_dimension=0, tiled=True)
    (grad_att,) = exchange(grad_att, True, vw, 1)
    ff_grads, branch, grad_att = tie(jnp.concatenate(ff_grads, axis=1), branch, grad_att)
    ff_grads = lax.psum_scatter(ff_grads, "ha", scatter_dimension=0, tiled=True)
    grad_att = grad_att.reshape(count, rows_n, sub_len, vw)
    output = (middle + branch.astype(F32).reshape(rows_n, sub_len, width)).astype(BF)
    part = core_sum(attended, flat_branch).reshape(-1, size_a, size_b, vw, width // blocks)
    part = jnp.transpose(part, (0, 2, 1, 3, 4)).reshape(-1, size_a * vw, width // blocks)
    ff_grads = jnp.transpose(ff_grads.reshape(-1, 3, blocks, width // blocks), (2, 1, 0, 3))
    ff_grads = ff_grads.reshape(blocks, -1, width // blocks)
    gn, grad_states = row_call(
        functools.partial(back_state_kernel, nh, vd, docs),
        rows_n,
        scalars,
        [(qkv, 1), (grad_att, 1), (att, 1), (den, 0), (pa, None), (pb, None), (frows, None)],
        [((rows_n, length, nh * 256), BF, 0), ((rows_n, nh, AUX, TILE), BF, 0)],
        nh * rows_n * length * 256 * 256 * 4,
    )
    later = chain_pieces(grad_states, True)
    gqk, gv = row_call(
        functools.partial(back_intra_kernel, nh, vd, docs),
        rows_n,
        scalars,
        [(qkv, 1), (gn, 0), (state_in, 0), (pa, None), (pb, None), (frows, None), (align, None)],
        [((rows_n, length, 128), F32, 0), ((rows_n, length, vw), F32, 0)],
        pair * 256 * 8,
    )
    (gqkv,) = row_call(
        functools.partial(back_key_kernel, nh, vd, docs, blocks),
        rows_n,
        scalars,
        [(qkv, 1), (gqk, 0), (gv, 0), (pa, None), (pb, None), (frows, None)] + [(e, 0) for e in later],
        [((count, rows_n, sub_len, xw), BF, 1)],
        nh * rows_n * length * 256 * 256 * 6,
    )
    to_owners = gqkv.reshape(count, tokens, xw)
    if square():
        y, b = lax.axis_index("sy"), lax.axis_index("hb")
        turns = (y * 2 + b, y * 2 + 1 - b, (1 - y) * 2 + b, (1 - y) * 2 + 1 - b)
        part = jnp.stack([lax.dynamic_index_in_dim(part, i, 0, False) for i in turns])
        shape = part.shape[1:]
        relay = (2, shape[0] // 2, shape[1])
        grad_in, got, _ = exchange(
            to_owners, False, xw, 2, "scatter", (part,), ((3,) + shape, relay), last_major=True
        )
        grad_w_out = sum((got[i].astype(F32) for i in range(3)), part[0].astype(F32)).astype(BF)
    else:
        (grad_in,) = exchange(to_owners, False, xw, 2, last_major=True)
        grad_w_out = lax.psum_scatter(part, QUAD, scatter_dimension=0, tiled=True)
    grad_w_out = grad_w_out.reshape(size_a, vw, width // blocks)
    w_in_all = w_in_all.reshape(blocks, count * xw, width // blocks)
    grad_one = jnp.concatenate([dot(grad_in, w_in_all[i]) for i in range(blocks)], axis=1)
    grad_one = grad_one.reshape(rows_n, sub_len, width)
    gain_one_part = jnp.sum(grad_one * normed_one, axis=(0, 1))
    scaled = grad_one * attn_gain
    input_grad = (
        grad_middle
        + scale_one * (scaled - normed_one * jnp.mean(scaled * normed_one, axis=-1, keepdims=True))
    ).astype(BF)

    flat_tokens = count * tokens
    grad_w_in = dot(gqkv.reshape(flat_tokens, xw), normed_full.reshape(flat_tokens, width), TN)
    grad_w_in = jnp.transpose(grad_w_in.astype(BF).reshape(xw, blocks, width // blocks), (1, 0, 2))
    vectors = jnp.stack([gain_one_part, bias_part, gain_two_part])
    vectors, grad_w_in, ff_grads, grad_w_out = send_home(vectors, grad_w_in, ff_grads, grad_w_out, 5)
    ff_grads = ff_grads.astype(F32).reshape(blocks, 3, -1, width // blocks)
    grad_gate_w, grad_up_w, grad_down_w = (windows_joined(ff_grads[:, i], units) for i in range(3))
    qk_cut = vw + nh * FEAT
    return (
        jnp.transpose(output, (1, 0, 2)),
        jnp.transpose(input_grad, (1, 0, 2)),
        vectors[0],
        grad_w_in[vw:qk_cut].T,
        grad_w_in[qk_cut : qk_cut + nh * FEAT].T,
        grad_w_in[:vw].T,
        grad_w_out,
        vectors[1],
        vectors[2],
        grad_gate_w.T,
        grad_up_w.T,
        grad_down_w,
    )


def solution(mesh):
    seq, head = mesh.shape["seq"], mesh.shape["head"]
    inner = Mesh(mesh.devices.reshape(seq // 2, 2, seq, head // seq), ("sy", "sc", "ha", "hb"))
    every, heads = ("sy", "sc", "ha", "hb"), ("ha", "hb")
    placed = (
        P(every, None, None),
        P(),
        P(None, heads),
        P(None, heads),
        P(None, heads),
        P(heads, None),
        P(),
        P(),
        P(None, heads),
        P(None, heads),
        P(heads, None),
        P(every, None, None),
        P(),
    )
    return jax.shard_map(
        on_device,
        mesh=inner,
        in_specs=placed,
        out_specs=(
            P(every, None, None),
            P(every, None, None),
            P(every),
            P(SEQ, heads),
            P(SEQ, heads),
            P(SEQ, heads),
            P(heads, SEQ),
            P(every),
            P(every),
            P(SEQ, heads),
            P(SEQ, heads),
            P(heads, SEQ),
        ),
        check_vma=False,
    )
```

```python
import functools

import jax
import jax.numpy as jnp
import numpy as np
from jax import lax
from jax.experimental import pallas as pl
from jax.experimental.pallas import tpu as pltpu
from jax.sharding import Mesh
from jax.sharding import PartitionSpec as P

FEAT = 16
EPS = 1e-05
ROOT_HALF = 0.7071067811865476
TILE = 256
AUX = 136
BF = jnp.bfloat16
F32 = jnp.float32
MESH_ID = pl.DeviceIdType.MESH
NT = (((1,), (1,)), ((), ()))
TN = (((0,), (0,)), ((), ()))


def dot(a, b, dims=(((1,), (0,)), ((), ()))):
    return lax.dot_general(a, b, dims, preferred_element_type=F32)


def feature_tables(nh):
    cols = [(None, None)] + [(i, None) for i in range(FEAT)]
    cols += [(i, j) for i in range(FEAT) for j in range(i, FEAT)]
    pick_a = np.zeros((2 * nh, 128, TILE), np.float32)
    pick_b = np.zeros((2 * nh, 128, TILE), np.float32)
    rows = np.zeros((8, TILE), np.float32)
    for c, (i, j) in enumerate(cols):
        scale = 1.0 if i is None else 0.5 if j is None else 0.25 * ROOT_HALF
        rows[0, c] = 1.0 if i is None else 0.0
        rows[1, c] = 1.0 if j is None else 0.0
        rows[2, c] = scale * (2.0 if j is not None and i != j else 1.0)
        rows[3, c] = scale
        for n in range(2 * nh):
            if i is not None:
                pick_a[n, FEAT * n + i, c] = 1.0
            if j is not None:
                pick_b[n, FEAT * n + j, c] = 1.0
    align = np.zeros((4 * nh, 128, 128), np.float32)
    for h in range(nh):
        for f in range(FEAT):
            q, k = FEAT * h + f, FEAT * (nh + h) + f
            align[4 * h, q, f] = 0.25
            align[4 * h + 1, k, f] = 1.0
            align[4 * h + 2, k, q] = 0.25
            align[4 * h + 3, q, k] = 0.25
    to_low = lambda a: jnp.asarray(a, BF)
    return to_low(pick_a), to_low(pick_b), jnp.asarray(rows), to_low(align)


def begin_at(lens, row, docs, position, start_block):
    start = -start_block
    found = start + position * 0
    for j in range(docs):
        if j:
            start = start + lens[row, j - 1]
            found = jnp.where(start <= position, start, found)
    return found


def chain_weights(lens, row, docs, block, blocks, length, backward):
    out, alive = [], None
    for k in range(1, blocks):
        source = block + k if backward else block - k
        inside = (source < blocks) if backward else (source >= 0)
        here = inside if alive is None else jnp.logical_and(alive, inside)
        out.append(jnp.where(here, 1.0, 0.0).astype(F32))
        first = begin_at(lens, row, docs, length - 1, source * length)
        passes = first < 0
        alive = passes if alive is None else jnp.logical_and(alive, passes)
    return out


def lane_iota(shape):
    return lax.broadcasted_iota(jnp.int32, shape, len(shape) - 1)


def row_iota(shape):
    return lax.broadcasted_iota(jnp.int32, shape, len(shape) - 2)


def with_ones(v, lanes=(0, 1)):
    side = lane_iota(v.shape)
    ones = jnp.where((side >= lanes[0]) & (side <= lanes[1]), 1.0, 0.0).astype(BF)
    return jnp.concatenate([v, ones], axis=1)


def split_sum(state, total, third):
    rows = row_iota(state.shape)
    high = total.astype(BF).astype(F32)
    low = total - high
    out = jnp.where(rows < 128, state, 0.0)
    out = jnp.where(rows == 128, high, out)
    if third:
        out = jnp.where(rows == 129, high, out)
        out = jnp.where(rows == 130, low, out)
    else:
        out = jnp.where(rows == 129, low, out)
    return out.astype(BF)


def flat(ref):
    x = ref[...]
    return x.reshape(x.shape[0] * x.shape[2], x.shape[3])


def picks(qk, pa, pb, rows, n):
    a = dot(qk, pa[n]) + rows[0:1, :]
    b = dot(qk, pb[n]) + rows[1:2, :]
    return a, b


def state_kernel(nh, vd, docs, lens, meta, x_ref, pa, pb, rows, out):
    row = pl.program_id(0)
    x = flat(x_ref)
    length = x.shape[0]
    qk = x[:, nh * vd :]
    last = begin_at(lens, row, docs, length - 1, meta[0] * length)
    trail = row_iota((length, 2 * 128)) >= last
    for h in range(nh):
        a, b = picks(qk, pa, pb, rows, nh + h)
        kf = (a * b * rows[3:4, :]).astype(BF)
        va = jnp.where(trail, with_ones(x[:, h * vd : (h + 1) * vd]).astype(F32), 0.0).astype(BF)
        st = dot(va, kf, TN)[:AUX]
        out[0, h] = split_sum(st, st[128:129], False)


def intra_kernel(nh, vd, docs, lens, meta, x_ref, align, num_out, den_out):
    row = pl.program_id(0)
    x = flat(x_ref)
    length = x.shape[0]
    qk = x[:, nh * vd :]
    one16 = jnp.where(lane_iota((1, 128)) == FEAT, 1.0, 0.0)
    tile = min(TILE, length)
    dens = [jnp.zeros((tile, 128), F32) for _ in range(length // tile)]
    for h in range(nh):
        qa = (dot(qk, align[4 * h]) + one16).astype(BF)
        ka = (dot(qk, align[4 * h + 1]) + one16).astype(BF)
        va = with_ones(x[:, h * vd : (h + 1) * vd])
        for t in range(length // tile):
            lo, hi = t * tile, (t + 1) * tile
            s1 = dot(qa[lo:hi], ka[:hi], NT)
            w = 0.5 * (s1 * s1) + 0.5
            pos = lo + row_iota((tile, 1))
            beg = begin_at(lens, row, docs, pos, meta[0] * length)
            kpos = lane_iota(w.shape)
            w = jnp.where((kpos >= beg) & (kpos <= pos), w, 0.0).astype(BF)
            acc = dot(w, va[:hi])
            num_out[0, lo:hi, h * vd : (h + 1) * vd] = acc[:, :vd]
            lane = lane_iota((tile, 128))
            dens[t] = jnp.where(lane == h, acc[:, vd : vd + 1], dens[t])
    for t in range(length // tile):
        den_out[0, t * tile : (t + 1) * tile, :] = dens[t]


def gather_states(sts, weights, h):
    total = None
    for st, w in zip(sts, weights):
        part = st[0, h].astype(F32) * w
        total = part if total is None else total + part
    return total


def attend_kernel(nh, vd, docs, blocks, lens, meta, x_ref, num, den, pa, pb, rows, *rest):
    sts, (att_out, den_out, st_out) = rest[: blocks - 1], rest[blocks - 1 :]
    row = pl.program_id(0)
    x = flat(x_ref)
    length = x.shape[0]
    qk = x[:, nh * vd :]
    weights = chain_weights(lens, row, docs, meta[0], blocks, length, False)
    pos = row_iota((length, 1))
    carried = begin_at(lens, row, docs, pos, meta[0] * length) < 0
    lane = lane_iota((length, 128))
    dens = den[0]
    for h in range(nh):
        st = gather_states(sts, weights, h)
        st = split_sum(st, st[128:129] + st[129:130], True)
        st_out[0, h] = st
        a, b = picks(qk, pa, pb, rows, h)
        qf = (a * b * rows[2:3, :]).astype(BF)
        inter = dot(qf, st, NT)
        more = jnp.where(carried, inter[:, :vd], 0.0)
        more_den = jnp.where(carried, inter[:, 128:129] + inter[:, 130:131], 0.0)
        total = dens[:, h : h + 1] + more_den
        value = (num[0, :, h * vd : (h + 1) * vd] + more) / total
        att_out[:, 0, :, h * vd : (h + 1) * vd] = value.astype(BF).reshape(
            att_out.shape[0], att_out.shape[2], vd
        )
        dens = jnp.where(lane == h, total, dens)
    den_out[0] = dens


def back_state_kernel(nh, vd, docs, lens, meta, x_ref, ga_ref, att_ref, den, pa, pb, rows, gn_out, out):
    row = pl.program_id(0)
    x, ga, att = flat(x_ref), flat(ga_ref), flat(att_ref)
    length = x.shape[0]
    qk = x[:, nh * vd :]
    pos = row_iota((length, 1))
    carried = begin_at(lens, row, docs, pos, meta[0] * length) < 0
    side = lane_iota((length, 128))
    for h in range(nh):
        cut = slice(h * vd, (h + 1) * vd)
        inv = 1.0 / den[0, :, h : h + 1]
        gah = ga[:, cut].astype(F32) * inv
        gd = -jnp.sum(gah * att[:, cut].astype(F32), axis=1, keepdims=True)
        high = gd.astype(BF).astype(F32)
        aux = jnp.where((side == 0) | (side == 2), high, jnp.where(side == 1, gd - high, 0.0))
        gn = jnp.concatenate([gah, aux], axis=1)
        gn_out[0, :, h * 256 : (h + 1) * 256] = gn.astype(BF)
        a, b = picks(qk, pa, pb, rows, h)
        qf = (a * b * rows[2:3, :]).astype(BF)
        st = dot(jnp.where(carried, gn, 0.0).astype(BF), qf, TN)[:AUX]
        out[0, h] = split_sum(st, st[128:129] + st[129:130], False)


def back_intra_kernel(
    nh, vd, docs, lens, meta, x_ref, gn_ref, st_ref, pa, pb, rows, align, gqk_out, gv_out
):
    row = pl.program_id(0)
    x = flat(x_ref)
    length = x.shape[0]
    qk = x[:, nh * vd :]
    one16 = jnp.where(lane_iota((1, 128)) == FEAT, 1.0, 0.0)
    tile = min(TILE, length)
    pos = row_iota((length, 1))
    carried = begin_at(lens, row, docs, pos, meta[0] * length) < 0
    gqk = None
    for h in range(nh):
        qa = (dot(qk, align[4 * h]) + one16).astype(BF)
        ka = (dot(qk, align[4 * h + 1]) + one16).astype(BF)
        k_at_q = dot(qk, align[4 * h + 2]).astype(BF)
        q_at_k = dot(qk, align[4 * h + 3]).astype(BF)
        va = with_ones(x[:, h * vd : (h + 1) * vd])
        gn = gn_ref[0, :, h * 256 : (h + 1) * 256]
        st = st_ref[0, h]
        gqf = jnp.where(carried, dot(gn[:, :AUX], st), 0.0) * rows[2:3, :]
        a, b = picks(qk, pa, pb, rows, h)
        part = dot((gqf * b).astype(BF), pa[h], NT) + dot((gqf * a).astype(BF), pb[h], NT)
        gqk = part if gqk is None else gqk + part
        gk_parts = []
        gq_parts = [None] * (length // tile)
        for t in range(length // tile):
            lo, hi = t * tile, (t + 1) * tile
            s1 = dot(ka[lo:hi], qa[lo:], NT)
            w = 0.5 * (s1 * s1) + 0.5
            kpos = lo + row_iota((tile, 1))
            qpos = lo + lane_iota((1, length - lo))
            beg = begin_at(lens, row, docs, qpos, meta[0] * length)
            see = (kpos >= beg) & (kpos <= qpos)
            gw = dot(va[lo:hi], gn[lo:], NT)
            gs = jnp.where(see, gw * s1, 0.0).astype(BF)
            w = jnp.where(see, w, 0.0).astype(BF)
            gv_out[0, lo:hi, h * vd : (h + 1) * vd] = dot(w, gn[lo:, :vd])
            gk_parts.append(dot(gs, q_at_k[lo:]))
            gq = dot(gs, k_at_q[lo:hi], TN)
            for u in range(t, length // tile):
                piece = gq[(u - t) * tile : (u - t + 1) * tile]
                gq_parts[u] = piece if gq_parts[u] is None else gq_parts[u] + piece
        gqk = gqk + jnp.concatenate(gk_parts, axis=0) + jnp.concatenate(gq_parts, axis=0)
    gqk_out[0] = gqk


def back_key_kernel(nh, vd, docs, blocks, lens, meta, x_ref, gqk_ref, gv_ref, pa, pb, rows, *rest):
    sts, (out,) = rest[: blocks - 1], rest[blocks - 1 :]
    row = pl.program_id(0)
    x = flat(x_ref)
    length = x.shape[0]
    qk = x[:, nh * vd :]
    weights = chain_weights(lens, row, docs, meta[0], blocks, length, True)
    last = begin_at(lens, row, docs, length - 1, meta[0] * length)
    trail = row_iota((length, 1)) >= last
    gqk = gqk_ref[0]
    shape = (out.shape[0], out.shape[2])
    for h in range(nh):
        st = gather_states(sts, weights, h)
        st = split_sum(st, st[128:129] + st[129:130], False)
        va = with_ones(x[:, h * vd : (h + 1) * vd])
        gkf = jnp.where(trail, dot(va[:, :AUX], st), 0.0) * rows[3:4, :]
        a, b = picks(qk, pa, pb, rows, nh + h)
        gqk = gqk + dot((gkf * b).astype(BF), pa[nh + h], NT)
        gqk = gqk + dot((gkf * a).astype(BF), pb[nh + h], NT)
        kf = (a * b * rows[3:4, :]).astype(BF)
        more = jnp.where(trail, dot(kf, st[:vd], NT), 0.0)
        gv = gv_ref[0, :, h * vd : (h + 1) * vd] + more
        out[:, 0, :, h * vd : (h + 1) * vd] = gv.astype(BF).reshape(shape + (vd,))
    out[:, 0, :, nh * vd :] = gqk.astype(BF).reshape(shape + (128,))


def row_call(kernel, rows_n, scalars, ins, outs, flops):
    def spec(shape, dim):
        if dim is None:
            return pl.BlockSpec(shape, lambda r, *_: (0,) * len(shape))
        block = tuple(1 if d == dim else n for d, n in enumerate(shape))
        return pl.BlockSpec(block, lambda r, *_: tuple(r if d == dim else 0 for d in range(len(shape))))

    moved = sum(a.size * a.dtype.itemsize for a, _ in ins)
    moved += sum(int(np.prod(s)) * np.dtype(t).itemsize for s, t, _ in outs)
    return pl.pallas_call(
        kernel,
        out_shape=tuple(jax.ShapeDtypeStruct(s, t) for s, t, _ in outs),
        grid_spec=pltpu.PrefetchScalarGridSpec(
            num_scalar_prefetch=len(scalars),
            grid=(rows_n,),
            in_specs=[spec(a.shape, d) for a, d in ins],
            out_specs=[spec(s, d) for s, t, d in outs],
        ),
        compiler_params=pltpu.CompilerParams(vmem_limit_bytes=56 * 1024 * 1024),
        cost_estimate=pl.CostEstimate(flops=int(flops), bytes_accessed=int(moved), transcendentals=0),
    )(*scalars, *[a for a, _ in ins])


SEQ = ("sy", "sc")
HEAD = ("ha", "hb")


def here():
    return tuple(lax.axis_index(n) for n in ("sy", "sc", "ha", "hb"))


def remote(src, dst, ssem, rsem, k, device):
    return pltpu.make_async_remote_copy(
        src_ref=src,
        dst_ref=dst,
        send_sem=ssem.at[k],
        recv_sem=rsem.at[k],
        device_id=device,
        device_id_type=MESH_ID,
    )


def greet(devices):
    bar = pltpu.get_barrier_semaphore()
    for device in devices:
        pl.semaphore_signal(bar, 1, device_id=device, device_id_type=MESH_ID)
    pl.semaphore_wait(bar, len(devices))


def square():
    return tuple(lax.axis_size(n) for n in ("sy", "ha", "hb")) == (2, 4, 2)


def place(block, head, special):
    if special:
        ha = 2 * (block % 2) + block // 2
        return (head // 2 + ha % 2) % 2, head % 2, ha
    return head // 2, head % 2, block


def own_place():
    sy, sc, ha, _ = here()
    if square():
        return 2 * (ha % 2) + ha // 2, 2 * ((sy + ha) % 2) + sc
    return ha, sy * 2 + sc


def first_head(block):
    return block % 2 if square() else block


def home_of(head, special):
    if special:
        return 2 * (head % 2) + head // 2, 2 * ((head // 2 + head) % 2) + head % 2
    return head, head


def maybe_own(k, own, elsewhere, alone):
    if k:
        elsewhere()
    else:
        pl.when(jnp.logical_not(own))(elsewhere)
        pl.when(own)(alone)


def exchange_kernel(to_blocks, width, last_major, extra, src, *refs):
    n_in, n_out = {None: (0, 0), "gather": (2, 2), "scatter": (1, 2)}[extra]
    ins, dst, outs, sems = refs[:n_in], refs[n_in], refs[n_in + 1 : n_in + 1 + n_out], refs[n_in + 1 + n_out :]
    ssem, rsem, lsem = sems[:3]
    sy, sc, a, b = here()
    s = sy * 2 + sc
    block, head = own_place()
    special = square()
    size_a, size_b = lax.axis_size("ha"), lax.axis_size("hb")
    count = size_a * size_b
    bar = pltpu.get_barrier_semaphore()
    same = s == block

    def at(k):
        i, pb = k // size_b, lax.rem(b + k % size_b, size_b)
        if to_blocks:
            sender = (block // 2, block % 2, lax.rem(a + i, size_a), pb)
            to = lax.rem(a - place(s, 0, special)[2] + first_head(s) + i + size_a, size_a)
            piece = to * size_b + pb
            source = src.at[:, pl.ds(pl.multiple_of(piece * width, 128), width)]
            return sender, source, dst.at[a * size_b + b], place(s, to, special) + (pb,)
        sender = place(s, lax.rem(first_head(s) + i, size_a), special) + (pb,)
        to = lax.rem(head - first_head(block) + a + i + size_a, size_a)
        column = b * size_a + head if last_major else head * size_b + b
        far = dst.at[:, pl.ds(pl.multiple_of(column * width, 128), width)]
        return sender, src.at[to * size_b + pb], far, (block // 2, block % 2, to, pb)

    def copy(k):
        _, source, far, receiver = at(k)
        return remote(source, far, ssem, rsem, k, receiver)

    def local():
        return pltpu.make_async_copy(at(0)[1], at(0)[2], lsem.at[0])

    def signal(device):
        pl.semaphore_signal(bar, 1, device_id=device, device_id_type=MESH_ID)

    to_x, to_y, to_core = (sy, sc, a, 1 - b), (1 - sy, sc, a, b), (sy, 1 - sc, a, b)
    expected = count - same.astype(jnp.int32)
    for k in range(count):
        maybe_own(k, same, functools.partial(signal, at(k)[0]), lambda: None)
    if extra in ("gather", "scatter"):
        greeted = (to_x, to_y, to_core)[: 3 if extra == "gather" else 2]
        for device in greeted:
            signal(device)
        expected = expected + len(greeted)
    pl.semaphore_wait(bar, expected)
    for k in range(count):
        maybe_own(k, same, lambda: copy(k).start(), lambda: local().start())

    if extra == "gather":
        (more, own_w), (near, other_w) = ins, outs
        gsem, hsem = sems[3:]
        half = more.shape[0] // 2
        low, high = pl.ds(0, half), pl.ds(half, half)
        copies = [
            remote(more, near.at[1], gsem, hsem, 0, to_x),
            remote(more, near.at[2], gsem, hsem, 1, to_y),
            remote(own_w, other_w, gsem, hsem, 4, to_core),
        ]
        for c in copies:
            c.start()
        stay = pltpu.make_async_copy(more, near.at[0], lsem.at[1])
        stay.start()
        copies[0].wait_recv()
        copies.append(remote(near.at[1, high], near.at[3, high], gsem, hsem, 2, to_y))
        copies[3].start()
        copies[1].wait_recv()
        copies.append(remote(near.at[2, low], near.at[3, low], gsem, hsem, 3, to_x))
        copies[4].start()
        stay.wait()
        for c in copies[2:]:
            c.wait_recv()
        for c in copies:
            c.wait_send()
    if extra == "scatter":
        (parts,), (got, relay) = ins, outs
        gsem, hsem = sems[3:]
        half = parts.shape[1] // 2
        low, high = pl.ds(0, half), pl.ds(half, half)
        copies = [
            remote(parts.at[3, low], relay.at[0], gsem, hsem, 0, to_x),
            remote(parts.at[3, high], relay.at[1], gsem, hsem, 1, to_y),
            remote(parts.at[1], got.at[0], gsem, hsem, 2, to_x),
            remote(parts.at[2], got.at[1], gsem, hsem, 3, to_y),
        ]
        for c in copies:
            c.start()
        copies[0].wait_recv()
        copies.append(remote(relay.at[0], got.at[2, low], gsem, hsem, 4, to_y))
        copies[4].start()
        copies[1].wait_recv()
        copies.append(remote(relay.at[1], got.at[2, high], gsem, hsem, 5, to_x))
        copies[5].start()
        for c in copies[2:]:
            c.wait_recv()
        for c in copies:
            c.wait_send()
    for k in range(count):
        maybe_own(k, same, lambda: copy(k).wait(), lambda: local().wait())


def exchange(x, to_blocks, width, collective, extra=None, ins=(), outs=(), last_major=False):
    count = lax.axis_size("ha") * lax.axis_size("hb")
    tokens = x.shape[0] if to_blocks else x.shape[1]
    shape = (count, tokens, width) if to_blocks else (tokens, count * width)
    any_space = pl.BlockSpec(memory_space=pl.ANY)
    more = {None: 0, "gather": 5, "scatter": 6}[extra]
    return pl.pallas_call(
        functools.partial(exchange_kernel, to_blocks, width, last_major, extra),
        out_shape=[jax.ShapeDtypeStruct(s, x.dtype) for s in (shape, *outs)],
        in_specs=[any_space] * (1 + len(ins)),
        out_specs=[any_space] * (1 + len(outs)),
        scratch_shapes=[
            pltpu.SemaphoreType.DMA((count,)),
            pltpu.SemaphoreType.DMA((count,)),
            pltpu.SemaphoreType.DMA((2,)),
        ]
        + [pltpu.SemaphoreType.DMA((more,))] * (2 if more else 0),
        compiler_params=pltpu.CompilerParams(collective_id=collective, has_side_effects=True),
        cost_estimate=pl.CostEstimate(flops=0, bytes_accessed=x.size * 500, transcendentals=0),
    )(x, *ins)


def home_kernel(*refs):
    src, grads, windows, shards, dst, grads_got, windows_got, shards_got = refs[:8]
    ssem, rsem, lsem, gsem, hsem, usem, vsem = refs[8:]
    sy, sc, a, b = here()
    s = sy * 2 + sc
    block, head = own_place()
    special = square()
    size_a, size_b = lax.axis_size("ha"), lax.axis_size("hb")
    devices = src.shape[0]
    me = (s * size_a + a) * size_b + b
    homely = head == a
    block_h, seq_h = home_of(head, special)
    bar = pltpu.get_barrier_semaphore()

    def peer(k):
        i = lax.rem(me + k, devices)
        rest = i // (size_a * size_b)
        return i, (rest // 2, rest % 2, i // size_b % size_a, i % size_b)

    def copy(k):
        i, device = peer(k)
        return remote(src.at[i], dst.at[me], ssem, rsem, k, device)

    def grad_ends(k):
        e = lax.rem(block - block_h + seq_h + k + size_a, size_a)
        return grads.at[e], grads_got.at[block], (e // 2, e % 2, head, b)

    def grad_copy(k):
        source, far, device = grad_ends(k)
        return remote(source, far, gsem, hsem, k, device)

    def grad_local():
        return pltpu.make_async_copy(*grad_ends(0)[:2], lsem.at[1])

    def window_copy(k):
        e = lax.rem(s + k, size_a)
        return remote(windows.at[e], windows_got.at[s], gsem, hsem, size_a + k, (e // 2, e % 2, a, b))

    def shard_copy(k):
        pa = lax.rem(a + k, size_a)
        return remote(shards.at[pa], shards_got.at[a], usem, vsem, k, (sy, sc, pa, b))

    @pl.loop(1, devices)
    def _(k):
        pl.semaphore_signal(bar, 1, device_id=peer(k)[1], device_id_type=MESH_ID)

    stay = [
        pltpu.make_async_copy(shards.at[a], shards_got.at[a], lsem.at[3]),
        pltpu.make_async_copy(src.at[me], dst.at[me], lsem.at[0]),
        pltpu.make_async_copy(windows.at[s], windows_got.at[s], lsem.at[2]),
    ]
    for c in stay:
        c.start()
    pl.semaphore_wait(bar, devices - 1)
    for k in range(size_a):
        maybe_own(k, homely, lambda: grad_copy(k).start(), lambda: grad_local().start())
        if k:
            window_copy(k).start()
    for k in range(1, size_a):
        shard_copy(k).start()

    @pl.loop(1, devices)
    def _(k):
        copy(k).start()

    @pl.loop(1, devices)
    def _(k):
        copy(k).wait()

    for k in range(size_a):
        maybe_own(k, homely, lambda: grad_copy(k).wait(), lambda: grad_local().wait())
        if k:
            window_copy(k).wait()
    for k in range(1, size_a):
        shard_copy(k).wait()
    for c in stay:
        c.wait()


def send_home(x, grads, windows, shards, collective):
    devices = 2 * lax.axis_size("sy") * lax.axis_size("ha") * lax.axis_size("hb")
    vectors, share = x.shape[0], x.shape[1] // devices
    x = jnp.transpose(x.reshape(vectors, devices, share), (1, 0, 2))
    x = jnp.pad(x, ((0, 0), (0, 8 - vectors), (0, 128 - share)))
    any_space = pl.BlockSpec(memory_space=pl.ANY)
    ins = [x, grads, windows, shards]
    size_a, heads = lax.axis_size("ha"), shards.shape[0]
    out = pl.pallas_call(
        home_kernel,
        out_shape=[jax.ShapeDtypeStruct(v.shape, v.dtype) for v in ins],
        in_specs=[any_space] * len(ins),
        out_specs=[any_space] * len(ins),
        scratch_shapes=[
            pltpu.SemaphoreType.DMA((devices,)),
            pltpu.SemaphoreType.DMA((devices,)),
            pltpu.SemaphoreType.DMA((4,)),
            pltpu.SemaphoreType.DMA((2 * size_a,)),
            pltpu.SemaphoreType.DMA((2 * size_a,)),
            pltpu.SemaphoreType.DMA((heads,)),
            pltpu.SemaphoreType.DMA((heads,)),
        ],
        compiler_params=pltpu.CompilerParams(collective_id=collective, has_side_effects=True),
        cost_estimate=pl.CostEstimate(flops=0, bytes_accessed=100000000, transcendentals=0),
    )(*ins)
    vectors = jnp.sum(out[0], axis=0)[:vectors, :share]
    return vectors, jnp.sum(out[1].astype(F32), axis=0), out[2], jnp.sum(out[3].astype(F32), axis=0)


def near_kernel(rows, src, weights, near, theirs, gsem, hsem, lsem):
    sy, sc, a, b = here()
    to_x, to_y, to_core = (sy, sc, a, 1 - b), (1 - sy, sc, a, b), (sy, 1 - sc, a, b)
    half = src.shape[0] // 2
    low, high = pl.ds(0, half), pl.ds(half, half)
    greet((to_x, to_y, to_core))
    copies = [
        remote(src, near.at[1], gsem, hsem, 0, to_x),
        remote(src, near.at[2], gsem, hsem, 1, to_y),
        remote(weights.at[:, pl.ds(0, rows)], theirs, gsem, hsem, 4, to_core),
    ]
    for copy in copies:
        copy.start()
    stay = pltpu.make_async_copy(src, near.at[0], lsem)
    stay.start()
    copies[0].wait_recv()
    copies.append(remote(near.at[1, high], near.at[3, high], gsem, hsem, 2, to_y))
    copies[3].start()
    copies[1].wait_recv()
    copies.append(remote(near.at[2, low], near.at[3, low], gsem, hsem, 3, to_x))
    copies[4].start()
    stay.wait()
    for copy in copies[2:]:
        copy.wait_recv()
    for copy in copies:
        copy.wait_send()


def gather_near(x, weights, rows, collective):
    if not square():
        return lax.all_gather(x, QUAD, axis=0, tiled=True)[None], swap(weights[:, :rows], "sc")
    any_space = pl.BlockSpec(memory_space=pl.ANY)
    near, theirs = pl.pallas_call(
        functools.partial(near_kernel, rows),
        out_shape=[
            jax.ShapeDtypeStruct((4,) + x.shape, x.dtype),
            jax.ShapeDtypeStruct((weights.shape[0], rows, weights.shape[2]), weights.dtype),
        ],
        in_specs=[any_space] * 2,
        out_specs=[any_space] * 2,
        scratch_shapes=[pltpu.SemaphoreType.DMA((5,))] * 2 + [pltpu.SemaphoreType.DMA],
        compiler_params=pltpu.CompilerParams(collective_id=collective, has_side_effects=True),
        cost_estimate=pl.CostEstimate(flops=0, bytes_accessed=x.size * 200, transcendentals=0),
    )(x, weights)
    return near, theirs


def start_kernel(parts, live, src, w_in, w_out, dst, w_in_home, w_out_all, ssem, rsem, lsem, wsem, vsem):
    sy, sc, a, b = here()
    block, head = own_place()
    size = lax.axis_size("ha")
    target = place(sy * 2 + sc, a, True) + (b,)
    source = (block // 2, block % 2, head, b)
    same = jnp.logical_and(sy * 2 + sc == block, a == head)
    apart = jnp.logical_not(same)
    to_x, to_y, to_core = (sy, sc, a, 1 - b), (1 - sy, sc, a, b), (sy, 1 - sc, a, b)
    to_up, to_down = (sy, sc, a + 1, b), (sy, sc, a - 1, b)
    has_up, has_down = a < size - 1, a > 0
    bar = pltpu.get_barrier_semaphore()

    def signal(device):
        pl.semaphore_signal(bar, 1, device_id=device, device_id_type=MESH_ID)

    for device in (to_x, to_y, to_core):
        signal(device)
    pl.when(apart)(lambda: signal(source))
    pl.when(has_up)(lambda: signal(to_up))
    pl.when(has_down)(lambda: signal(to_down))
    own_w = pltpu.make_async_copy(w_out, w_out_all.at[a * 2 + b], lsem.at[parts])
    own_w.start()
    pad = pl.ds(live, w_in.shape[0] - live)
    own_pad = pltpu.make_async_copy(w_in.at[pad], w_in_home.at[pad], lsem.at[parts + 2])
    own_pad.start()
    pl.semaphore_wait(
        bar, 3 + apart.astype(jnp.int32) + has_up.astype(jnp.int32) + has_down.astype(jnp.int32)
    )

    step = src.shape[0] // parts
    count = 9
    half = src.shape[1] // 2

    def piece(z, x, r, lo=0, n=None):
        return dst.at[z * 2 + x, pl.ds(r * step, step), pl.ds(lo, src.shape[1] if n is None else n)]

    def make(k, r, ref, device):
        return remote(ref, ref, ssem, rsem, count * r + k, device)

    def home(r):
        return remote(src.at[pl.ds(r * step, step)], piece(a, b, r), ssem, rsem, count * r, target)

    def stay(r):
        return pltpu.make_async_copy(src.at[pl.ds(r * step, step)], piece(a, b, r), lsem.at[r])

    def w_home():
        return pltpu.make_async_remote_copy(
            src_ref=w_in.at[pl.ds(0, live)],
            dst_ref=w_in_home.at[pl.ds(0, live)],
            send_sem=wsem.at[0],
            recv_sem=wsem.at[1],
            device_id=target,
            device_id_type=MESH_ID,
        )

    def w_stay():
        return pltpu.make_async_copy(w_in.at[pl.ds(0, live)], w_in_home.at[pl.ds(0, live)], lsem.at[parts + 1])

    for r in range(parts):
        pl.when(apart)(lambda: home(r).start())
        pl.when(same)(lambda: stay(r).start())

    def send_w(k, pa, device):
        ref = w_out_all.at[pa * 2 + b]
        return remote(ref, ref, vsem.at[0], vsem.at[1], k, device)

    def spread(k, pa, up, down):
        if up:
            pl.when(has_up)(lambda: send_w(k, pa, to_up).start())
        if down:
            pl.when(has_down)(lambda: send_w(size + k, pa, to_down).start())
        send_w(2 * size + pa, pa, to_x).start()

    def w_step(k):
        @pl.when(a - k >= 0)
        def _():
            send_w(k - 1, a - k, to_x).wait_recv()
            spread(k, a - k, True, False)

        @pl.when(a + k < size)
        def _():
            send_w(size + k - 1, a + k, to_x).wait_recv()
            spread(k, a + k, False, True)

    across_y, across_c = (head + 2) % 4, head + 1 - 2 * (head % 2)
    across = (across_y + 1) - 2 * (across_y % 2)
    sent = []

    def go(copy):
        copy.start()
        sent.append(copy)

    def arrive(k, r, ref):
        make(k, r, ref, to_x).wait_recv()

    def stage_0(r):
        pl.when(apart)(lambda: arrive(0, r, piece(head, b, r)))
        pl.when(same)(lambda: stay(r).wait())
        for k, device in ((1, to_x), (2, to_y), (3, to_core)):
            go(make(k, r, piece(head, b, r), device))

    def stage_1(r):
        arrive(1, r, piece(head, 1 - b, r))
        go(make(4, r, piece(head, 1 - b, r, half, half), to_y))
        go(make(5, r, piece(head, 1 - b, r), to_core))
        arrive(2, r, piece(across_y, b, r))
        go(make(6, r, piece(across_y, b, r, 0, half), to_x))
        go(make(7, r, piece(across_y, b, r), to_core))

    def stage_2(r):
        arrive(4, r, piece(across_y, 1 - b, r, half, half))
        arrive(6, r, piece(across_y, 1 - b, r, 0, half))
        go(make(8, r, piece(across_y, 1 - b, r), to_core))

    def stage_3(r):
        arrive(3, r, piece(across_c, b, r))
        arrive(5, r, piece(across_c, 1 - b, r))
        arrive(7, r, piece(across, b, r))
        arrive(8, r, piece(across, 1 - b, r))

    stages = (stage_0, stage_1, stage_2, stage_3)
    for t in range(parts + 3):
        for i, stage in enumerate(stages):
            if 0 <= t - i < parts:
                stage(t - i)
        if t == 0:
            pl.when(apart)(lambda: w_home().start())
            pl.when(same)(lambda: w_stay().start())
            own_w.wait()
            spread(0, a, True, True)
        elif t < size:
            w_step(t)
    for k in range(parts + 3, size):
        w_step(k)
    pl.when(apart)(lambda: w_home().wait_recv())
    pl.when(same)(lambda: w_stay().wait())
    own_pad.wait()
    for k in range(size):
        ref = w_out_all.at[k * 2 + 1 - b]
        remote(ref, ref, vsem.at[0], vsem.at[1], 2 * size + k, to_x).wait_recv()
        send_w(2 * size + k, k, to_x).wait_send()
        pl.when(jnp.logical_and(has_up, a - k >= 0))(lambda: send_w(k, a - k, to_x).wait_send())
        pl.when(jnp.logical_and(has_down, a + k < size))(lambda: send_w(size + k, a + k, to_x).wait_send())
    for copy in sent:
        copy.wait_send()
    for r in range(parts):
        pl.when(apart)(lambda: home(r).wait_send())
    pl.when(apart)(lambda: w_home().wait_send())


def start(x, w_in, live, w_out, collective):
    if not square():
        size = lax.axis_size("ha")
        perm = [(s * size + z, z * size + s) for s in range(size) for z in range(size)]
        x, w_in = (lax.ppermute(v, ("sy", "sc", "ha"), perm) for v in (x, w_in))
        return lax.all_gather(x, ("sy", "sc", "hb"), axis=0), w_in, lax.all_gather(w_out, HEAD, axis=0)
    parts = x.shape[0]
    return pl.pallas_call(
        functools.partial(start_kernel, parts, live),
        out_shape=[
            jax.ShapeDtypeStruct((8,) + x.shape, x.dtype),
            jax.ShapeDtypeStruct(w_in.shape, w_in.dtype),
            jax.ShapeDtypeStruct((8,) + w_out.shape, w_out.dtype),
        ],
        in_specs=[pl.BlockSpec(memory_space=pl.ANY)] * 3,
        out_specs=[pl.BlockSpec(memory_space=pl.ANY)] * 3,
        scratch_shapes=[
            pltpu.SemaphoreType.DMA((9 * parts,)),
            pltpu.SemaphoreType.DMA((9 * parts,)),
            pltpu.SemaphoreType.DMA((parts + 3,)),
            pltpu.SemaphoreType.DMA((2,)),
            pltpu.SemaphoreType.DMA((2, 12)),
        ],
        compiler_params=pltpu.CompilerParams(collective_id=collective, has_side_effects=True),
        cost_estimate=pl.CostEstimate(flops=0, bytes_accessed=x.size * 400, transcendentals=0),
    )(x, w_in, w_out)


def swap(x, axis):
    return lax.ppermute(x, axis, [(0, 1), (1, 0)])


def seat(block, head, size, special):
    sy, sc, ha = place(block, head, special)
    return (sy * 2 + sc) * size + ha


def chain_pieces(x, backward):
    size, special = lax.axis_size("ha"), square()
    out = []
    for k in range(1, size):
        perm = []
        for i in range(size - k):
            ends = (i + k, i) if backward else (i, i + k)
            perm += [tuple(seat(e, h, size, special) for e in ends) for h in range(size)]
        out.append(lax.ppermute(x, SEQ + ("ha",), perm))
    return out


def tie(*values):
    return lax.optimization_barrier(values)


def my_columns(x, by_core):
    parts, place_of = lax.axis_size("sy") * 2, lax.axis_index("sy") * 2 + lax.axis_index("sc")
    if by_core:
        parts, place_of = 2, lax.axis_index("sc")
    size = x.shape[1] // parts
    return lax.dynamic_slice_in_dim(x, place_of * size, size, 1)


def by_halves(a, own, other):
    own, other = dot(a, own), dot(a, other)
    first = lax.axis_index("sc") == 0
    return jnp.concatenate([jnp.where(first, own, other), jnp.where(first, other, own)], axis=1)


def by_halves_back(a, own, other):
    size = own.shape[1]
    core = lax.axis_index("sc")
    ours, theirs = (lax.dynamic_slice_in_dim(a, i * size, size, 1) for i in (core, 1 - core))
    return dot(ours, own, NT) + dot(theirs, other, NT)


def unit_window(x, size):
    units = x.shape[0]
    window = -(-units // (size * 16)) * 16
    place = lax.axis_index("sy") * 2 + lax.axis_index("sc")
    start = jnp.minimum(place * window, units - window)
    part = lax.dynamic_slice_in_dim(x, start, window, 0)
    fresh = start + lax.broadcasted_iota(jnp.int32, part.shape, 0) >= place * window
    return jnp.where(fresh, part, jnp.zeros_like(part))


def windows_joined(parts, units):
    size, window = parts.shape[0], parts.shape[1]
    pieces = []
    for i in range(size):
        start = min(i * window, units - window)
        pieces.append(parts[i, max(i * window - start, 0) :])
    return jnp.concatenate(pieces, axis=0)


def ff_kernel(n2, cot, mine, theirs, gg_out, gu_out, hid_out, part_out, acc):
    shard = pl.program_id(1)

    def work(w, first):
        x, c = n2[0], cot[0]
        window, width = w.shape[1] // 3, w.shape[2]
        w_gate, w_up, w_down = (w[:, i * window : (i + 1) * window].reshape(-1, width) for i in range(3))
        gate, up, gh = dot(x, w_gate, NT), dot(x, w_up, NT), dot(c, w_down, NT)
        sig = jax.nn.sigmoid(gate)
        act = gate * sig
        hid_out[0, 0] = (act * up).astype(BF)
        gg = (gh * up * (sig + act * (1.0 - sig))).astype(BF)
        gu = (gh * act).astype(BF)
        gg_out[0, 0] = gg
        gu_out[0, 0] = gu
        back = dot(gg, w_gate) + dot(gu, w_up)
        if first:
            acc[...] = back
        else:
            part_out[0] = (acc[...] + back).astype(BF)

    @pl.when(shard == 0)
    def _():
        work(mine, True)

    @pl.when(shard == 1)
    def _():
        work(theirs, False)


def ff_pass(n2, cots, mine, theirs):
    chunks, tokens, width = n2.shape
    units = theirs.shape[0] * theirs.shape[1] // 3
    keep = jax.ShapeDtypeStruct((2, chunks, tokens, units), BF)
    whole = pl.BlockSpec((1, tokens, width), lambda c, i: (c, 0, 0))
    weights = pl.BlockSpec(theirs.shape, lambda c, i: (0, 0, 0), pipeline_mode=pl.Buffered(1))
    piece = pl.BlockSpec((1, 1, tokens, units), lambda c, i: (i, c, 0, 0))
    return pl.pallas_call(
        ff_kernel,
        out_shape=(keep, keep, keep, jax.ShapeDtypeStruct((chunks, tokens, width), BF)),
        grid=(chunks, 2),
        in_specs=[whole, whole, weights, weights],
        out_specs=[piece, piece, piece, whole],
        scratch_shapes=[pltpu.VMEM((tokens, width), F32)],
        compiler_params=pltpu.CompilerParams(vmem_limit_bytes=60 * 1024 * 1024),
        cost_estimate=pl.CostEstimate(
            flops=chunks * tokens * width * units * 20,
            bytes_accessed=12 * units * width + 8 * chunks * tokens * width,
            transcendentals=0,
        ),
    )(n2, cots, mine, theirs)


def branch_kernel(order, hidden, mine, theirs, out):
    width = out.shape[1]
    part = dot(hidden[0, 0], mine[...].reshape(-1, width)) + dot(hidden[1, 0], theirs[...].reshape(-1, width))
    out[...] = part.astype(BF)


def branch_product(hidden, mine, theirs):
    _, chunks, tokens, units = hidden.shape
    size, rows, width = theirs.shape
    weights = pl.BlockSpec((size, rows // 3, width), lambda i, m: (0, 2, 0), pipeline_mode=pl.Buffered(1))
    y, b = lax.axis_index("sy"), lax.axis_index("hb")
    turns = ((y, b), (y, 1 - b), (1 - y, b), (1 - y, 1 - b))[:chunks]
    order = jnp.stack([p * 2 + q if chunks > 1 else 0 * p for p, q in turns]).astype(jnp.int32)
    return pl.pallas_call(
        branch_kernel,
        out_shape=jax.ShapeDtypeStruct((chunks * tokens, width), BF),
        grid_spec=pltpu.PrefetchScalarGridSpec(
            num_scalar_prefetch=1,
            grid=(chunks,),
            in_specs=[pl.BlockSpec((2, 1, tokens, units), lambda i, m: (0, i, 0, 0)), weights, weights],
            out_specs=pl.BlockSpec((tokens, width), lambda i, m: (m[i], 0)),
        ),
        compiler_params=pltpu.CompilerParams(vmem_limit_bytes=40 * 1024 * 1024),
        cost_estimate=pl.CostEstimate(
            flops=chunks * tokens * units * width * 4, bytes_accessed=12 * units * width, transcendentals=0
        ),
    )(order, hidden, mine, theirs)


QUAD = ("sy", "hb")


def add_low(a, b):
    return (a.astype(F32) + b.astype(F32)).astype(BF)


def ring_sum(parts, meanwhile):
    own, to_x, to_y, across = parts
    half = own.shape[0] // 2
    via_x, via_y = swap(across[:half], "hb"), swap(across[half:], "sy")
    x_low, y_high = swap(to_x[:half], "hb"), swap(to_y[half:], "sy")
    work = meanwhile(0)
    via_x, via_y, *work = tie(via_x, via_y, *work)
    meanwhile(0, work)
    y_low = swap(add_low(to_y[:half], via_x), "sy")
    x_high = swap(add_low(to_x[half:], via_y), "hb")
    work = meanwhile(1)
    y_low, x_high, *work = tie(y_low, x_high, *work)
    meanwhile(1, work)
    low = own[:half].astype(F32) + x_low.astype(F32) + y_low.astype(F32)
    high = own[half:].astype(F32) + x_high.astype(F32) + y_high.astype(F32)
    return jnp.concatenate([low, high], axis=0)


def core_sum(a, b):
    size_y, core = lax.axis_size("sy"), lax.axis_index("sc")
    size = b.shape[1] // (size_y * 2)

    def of_core(c):
        columns = [lax.dynamic_slice_in_dim(b, (i * 2 + c) * size, size, 1) for i in range(size_y)]
        return jnp.concatenate(columns, axis=1)

    given = swap(dot(a, of_core(1 - core), TN).astype(BF), "sc")
    part = (dot(a, of_core(core), TN) + given.astype(F32)).astype(BF)
    return jnp.stack([part[:, i * size : (i + 1) * size] for i in range(size_y)])


def quad_sum(parts, meanwhile):
    if len(parts) == 4:
        return ring_sum(parts, meanwhile)
    for stage in (0, 1):
        meanwhile(stage)
    return lax.psum_scatter(parts[0], QUAD, scatter_dimension=0, tiled=True).astype(F32)


def ff_group(chunks, cots, mine, theirs):
    *kept, part = ff_pass(chunks, cots, mine, theirs)
    grads, branch = [], []
    width = chunks.shape[-1]
    flat = [k.reshape(2, -1, k.shape[-1]) for k in kept] + [chunks.reshape(-1, width), cots.reshape(-1, width)]
    pairs = [(flat[0], flat[3]), (flat[1], flat[3]), (flat[2], flat[4])]

    def meanwhile(stage, results=None):
        if results is not None:
            grads[:] = results[:3]
            branch[:] = results[3:]
            return None
        if stage == 0:
            grads.extend(swap(dot(a[1], b, TN).astype(BF), "sc") for a, b in pairs)
            return grads
        for i, (a, b) in enumerate(pairs):
            grads[i] = (dot(a[0], b, TN) + grads[i].astype(F32)).astype(BF)
        branch.append(branch_product(kept[2], mine, theirs))
        return grads + branch

    return quad_sum([part[i] for i in range(part.shape[0])], meanwhile), grads, branch[0]


def rms_scale(x):
    return lax.rsqrt(jnp.mean(x * x, axis=-1, keepdims=True) + EPS)


def on_device(
    inputs,
    attn_gain,
    w_query,
    w_key,
    w_value,
    w_out,
    out_bias,
    mlp_gain,
    gate_weight,
    up_weight,
    down_weight,
    cotangent,
    doc_lengths,
):
    every = ("sy", "sc", "ha", "hb")
    blocks = lax.axis_size("sy") * 2
    size_a, size_b = lax.axis_size("ha"), lax.axis_size("hb")
    count = size_a * size_b
    sub_len, rows_n, width = inputs.shape
    docs = doc_lengths.shape[1]
    nh = w_query.shape[1] // FEAT
    vd = w_value.shape[1] // nh
    vw = nh * vd
    xw = vw + 128
    length = sub_len * count
    tokens = rows_n * sub_len
    meta = own_place()[0].astype(jnp.int32).reshape(1)
    pa, pb, frows, align = feature_tables(nh)
    scalars = (doc_lengths, meta)

    x = jnp.transpose(inputs, (1, 0, 2)).astype(F32)
    cot = jnp.transpose(cotangent, (1, 0, 2))
    scale_one = rms_scale(x)
    normed_one = x * scale_one
    pad = jnp.zeros((128 - 2 * nh * FEAT, width), BF)
    w_in = jnp.concatenate([w_value.T, w_query.T, w_key.T, pad], axis=0)
    units = down_weight.shape[0]
    windows = [unit_window(w, blocks) for w in (gate_weight.T, up_weight.T, down_weight)]
    w_in_piece = my_columns(w_in, False)
    to_fetch = jnp.concatenate(windows, axis=0)
    normed_full, w_in_home, w_out_piece = start((normed_one * attn_gain).astype(BF), w_in, vw + 2 * nh * FEAT, my_columns(w_out, True), 3)
    to_fetch, normed_full = tie(to_fetch, normed_full)
    fetched = lax.all_gather(to_fetch, "ha", axis=0)
    window = windows[0].shape[0]

    qkv = jnp.einsum("grtd,cd->grtc", normed_full, w_in_home, preferred_element_type=F32).astype(BF)
    pair = nh * rows_n * length * length
    (states,) = row_call(
        functools.partial(state_kernel, nh, vd, docs),
        rows_n,
        scalars,
        [(qkv, 1), (pa, None), (pb, None), (frows, None)],
        [((rows_n, nh, AUX, TILE), BF, 0)],
        nh * rows_n * length * 256 * 256 * 4,
    )
    earlier = chain_pieces(states, False)
    num, den = row_call(
        functools.partial(intra_kernel, nh, vd, docs),
        rows_n,
        scalars,
        [(qkv, 1), (align, None)],
        [((rows_n, length, vw), F32, 0), ((rows_n, length, 128), F32, 0)],
        pair * 256 * 4,
    )
    att, den, state_in = row_call(
        functools.partial(attend_kernel, nh, vd, docs, blocks),
        rows_n,
        scalars,
        [(qkv, 1), (num, 0), (den, 0), (pa, None), (pb, None), (frows, None)]
        + [(e, 0) for e in earlier],
        [
            ((count, rows_n, sub_len, vw), BF, 1),
            ((rows_n, length, 128), F32, 0),
            ((rows_n, nh, AUX, TILE), BF, 0),
        ],
        nh * rows_n * length * 256 * 256 * 6,
    )
    flat_cot, to_owners = cot.reshape(tokens, width), att.reshape(count, tokens, vw)
    if square():
        attended, cots, w_out_other = exchange(
            to_owners, False, vw, 0, "gather", (flat_cot, w_out_piece), ((4, tokens, width), w_out_piece.shape)
        )
    else:
        (attended,) = exchange(to_owners, False, vw, 0)
        cots = lax.all_gather(flat_cot, QUAD, axis=0, tiled=True)[None]
        w_out_other = swap(w_out_piece, "sc")
    w_out_halves = [w.reshape(count * vw, width // 2) for w in (w_out_piece, w_out_other)]
    attn_branch = by_halves(attended, *w_out_halves).reshape(rows_n, sub_len, width)
    middle = x + attn_branch + out_bias
    scale_two = rms_scale(middle)
    normed_two = middle * scale_two
    normed_two_low = (normed_two * mlp_gain).astype(BF)

    chunks, theirs = gather_near(normed_two_low.reshape(tokens, width), fetched, 3 * window, 4)
    w_in_piece, chunks = tie(w_in_piece, chunks)
    w_in_all = lax.all_gather(w_in_piece, ("sy", "sc", "hb", "ha"), axis=0)
    grad_two, ff_grads, branch = ff_group(chunks, cots, fetched, theirs)
    grad_two = grad_two.reshape(rows_n, sub_len, width)
    gain_two_part = jnp.sum(grad_two * normed_two, axis=(0, 1))
    scaled = grad_two * mlp_gain
    grad_middle = cot.astype(F32) + scale_two * (
        scaled - normed_two * jnp.mean(scaled * normed_two, axis=-1, keepdims=True)
    )
    bias_part = jnp.sum(grad_middle, axis=(0, 1))
    grad_branch = grad_middle.astype(BF)

    flat_branch = grad_branch.reshape(tokens, width)
    grad_att = by_halves_back(flat_branch, *w_out_halves).astype(BF)
    branch, w_in_all = tie(branch, w_in_all)
    branch = lax.psum_scatter(branch, QUAD, scatter_dimension=0, tiled=True)
    grad_att, ff_grads = tie(grad_att, jnp.concatenate(ff_grads, axis=1))
    (grad_att,) = exchange(grad_att, True, vw, 1)
    ff_grads, branch, grad_att = tie(ff_grads, branch, grad_att)
    ff_grads = lax.psum_scatter(ff_grads, "ha", scatter_dimension=0, tiled=True)
    grad_att = grad_att.reshape(count, rows_n, sub_len, vw)
    output = (middle + branch.astype(F32).reshape(rows_n, sub_len, width)).astype(BF)
    part = core_sum(attended, flat_branch).reshape(-1, size_a, size_b, vw, width // blocks)
    part = jnp.transpose(part, (0, 2, 1, 3, 4)).reshape(-1, size_a * vw, width // blocks)
    ff_grads = jnp.transpose(ff_grads.reshape(-1, 3, blocks, width // blocks), (2, 1, 0, 3))
    ff_grads = ff_grads.reshape(blocks, -1, width // blocks)
    gn, grad_states = row_call(
        functools.partial(back_state_kernel, nh, vd, docs),
        rows_n,
        scalars,
        [(qkv, 1), (grad_att, 1), (att, 1), (den, 0), (pa, None), (pb, None), (frows, None)],
        [((rows_n, length, nh * 256), BF, 0), ((rows_n, nh, AUX, TILE), BF, 0)],
        nh * rows_n * length * 256 * 256 * 4,
    )
    later = chain_pieces(grad_states, True)
    gqk, gv = row_call(
        functools.partial(back_intra_kernel, nh, vd, docs),
        rows_n,
        scalars,
        [(qkv, 1), (gn, 0), (state_in, 0), (pa, None), (pb, None), (frows, None), (align, None)],
        [((rows_n, length, 128), F32, 0), ((rows_n, length, vw), F32, 0)],
        pair * 256 * 8,
    )
    (gqkv,) = row_call(
        functools.partial(back_key_kernel, nh, vd, docs, blocks),
        rows_n,
        scalars,
        [(qkv, 1), (gqk, 0), (gv, 0), (pa, None), (pb, None), (frows, None)] + [(e, 0) for e in later],
        [((count, rows_n, sub_len, xw), BF, 1)],
        nh * rows_n * length * 256 * 256 * 6,
    )
    to_owners = gqkv.reshape(count, tokens, xw)
    if square():
        y, b = lax.axis_index("sy"), lax.axis_index("hb")
        turns = (y * 2 + b, y * 2 + 1 - b, (1 - y) * 2 + b, (1 - y) * 2 + 1 - b)
        part = jnp.stack([lax.dynamic_index_in_dim(part, i, 0, False) for i in turns])
        shape = part.shape[1:]
        relay = (2, shape[0] // 2, shape[1])
        grad_in, got, _ = exchange(
            to_owners, False, xw, 2, "scatter", (part,), ((3,) + shape, relay), last_major=True
        )
        grad_w_out = sum((got[i].astype(F32) for i in range(3)), part[0].astype(F32)).astype(BF)
    else:
        (grad_in,) = exchange(to_owners, False, xw, 2, last_major=True)
        grad_w_out = lax.psum_scatter(part, QUAD, scatter_dimension=0, tiled=True)
    grad_w_out = grad_w_out.reshape(size_a, vw, width // blocks)
    w_in_all = w_in_all.reshape(blocks, count * xw, width // blocks)
    grad_one = jnp.concatenate([dot(grad_in, w_in_all[i]) for i in range(blocks)], axis=1)
    grad_one = grad_one.reshape(rows_n, sub_len, width)
    gain_one_part = jnp.sum(grad_one * normed_one, axis=(0, 1))
    scaled = grad_one * attn_gain
    input_grad = (
        grad_middle
        + scale_one * (scaled - normed_one * jnp.mean(scaled * normed_one, axis=-1, keepdims=True))
    ).astype(BF)

    flat_tokens = count * tokens
    grad_w_in = dot(gqkv.reshape(flat_tokens, xw), normed_full.reshape(flat_tokens, width), TN)
    live = vw + 2 * nh * FEAT
    grad_w_in = grad_w_in.astype(BF)[:live].reshape(live, blocks, width // blocks)
    grad_w_in = jnp.transpose(grad_w_in, (1, 0, 2))
    vectors = jnp.stack([gain_one_part, bias_part, gain_two_part])
    vectors, grad_w_in, ff_grads, grad_w_out = send_home(vectors, grad_w_in, ff_grads, grad_w_out, 5)
    ff_grads = ff_grads.astype(F32).reshape(blocks, 3, -1, width // blocks)
    grad_gate_w, grad_up_w, grad_down_w = (windows_joined(ff_grads[:, i], units) for i in range(3))
    qk_cut = vw + nh * FEAT
    return (
        jnp.transpose(output, (1, 0, 2)),
        jnp.transpose(input_grad, (1, 0, 2)),
        vectors[0],
        grad_w_in[vw:qk_cut].T,
        grad_w_in[qk_cut : qk_cut + nh * FEAT].T,
        grad_w_in[:vw].T,
        grad_w_out,
        vectors[1],
        vectors[2],
        grad_gate_w.T,
        grad_up_w.T,
        grad_down_w,
    )


def solution(mesh):
    seq, head = mesh.shape["seq"], mesh.shape["head"]
    inner = Mesh(mesh.devices.reshape(seq // 2, 2, seq, head // seq), ("sy", "sc", "ha", "hb"))
    every, heads = ("sy", "sc", "ha", "hb"), ("ha", "hb")
    placed = (
        P(every, None, None),
        P(),
        P(None, heads),
        P(None, heads),
        P(None, heads),
        P(heads, None),
        P(),
        P(),
        P(None, heads),
        P(None, heads),
        P(heads, None),
        P(every, None, None),
        P(),
    )
    return jax.shard_map(
        on_device,
        mesh=inner,
        in_specs=placed,
        out_specs=(
            P(every, None, None),
            P(every, None, None),
            P(every),
            P(SEQ, heads),
            P(SEQ, heads),
            P(SEQ, heads),
            P(heads, SEQ),
            P(every),
            P(every),
            P(SEQ, heads),
            P(SEQ, heads),
            P(heads, SEQ),
        ),
        check_vma=False,
    )
```

```python
import functools

import jax
import jax.numpy as jnp
import numpy as np
from jax import lax
from jax.experimental import pallas as pl
from jax.experimental.pallas import tpu as pltpu
from jax.sharding import Mesh
from jax.sharding import PartitionSpec as P

FEAT = 16
EPS = 1e-05
ROOT_HALF = 0.7071067811865476
TILE = 256
AUX = 136
MOST = 1536
BF = jnp.bfloat16
F32 = jnp.float32
MESH_ID = pl.DeviceIdType.MESH
NT = (((1,), (1,)), ((), ()))
TN = (((0,), (0,)), ((), ()))


def dot(a, b, dims=(((1,), (0,)), ((), ()))):
    return lax.dot_general(a, b, dims, preferred_element_type=F32)


def feature_tables(nh):
    cols = [(None, None)] + [(i, None) for i in range(FEAT)]
    cols += [(i, j) for i in range(FEAT) for j in range(i, FEAT)]
    pick_a = np.zeros((2 * nh, 128, TILE), np.float32)
    pick_b = np.zeros((2 * nh, 128, TILE), np.float32)
    rows = np.zeros((8, TILE), np.float32)
    for c, (i, j) in enumerate(cols):
        scale = 1.0 if i is None else 0.5 if j is None else 0.25 * ROOT_HALF
        rows[0, c] = 1.0 if i is None else 0.0
        rows[1, c] = 1.0 if j is None else 0.0
        rows[2, c] = scale * (2.0 if j is not None and i != j else 1.0)
        rows[3, c] = scale
        for n in range(2 * nh):
            if i is not None:
                pick_a[n, FEAT * n + i, c] = 1.0
            if j is not None:
                pick_b[n, FEAT * n + j, c] = 1.0
    align = np.zeros((4 * nh, 128, 128), np.float32)
    for h in range(nh):
        for f in range(FEAT):
            q, k = FEAT * h + f, FEAT * (nh + h) + f
            align[4 * h, q, f] = 0.25
            align[4 * h + 1, k, f] = 1.0
            align[4 * h + 2, k, q] = 0.25
            align[4 * h + 3, q, k] = 0.25
    to_low = lambda a: jnp.asarray(a, BF)
    return to_low(pick_a), to_low(pick_b), jnp.asarray(rows), to_low(align)


def begin_at(lens, row, docs, position, start_block):
    start = -start_block
    found = start + position * 0
    for j in range(docs):
        if j:
            start = start + lens[row, j - 1]
            found = jnp.where(start <= position, start, found)
    return found


def chain_reach(blocks, length):
    return min(blocks - 1, (MOST - 2) // length + 1)


def chain_weights(lens, row, docs, block, blocks, length, backward):
    out, alive = [], None
    for k in range(1, chain_reach(blocks, length) + 1):
        source = block + k if backward else block - k
        inside = (source < blocks) if backward else (source >= 0)
        here = inside if alive is None else jnp.logical_and(alive, inside)
        out.append(jnp.where(here, 1.0, 0.0).astype(F32))
        first = begin_at(lens, row, docs, length - 1, source * length)
        passes = first < 0
        alive = passes if alive is None else jnp.logical_and(alive, passes)
    return out


def lane_iota(shape):
    return lax.broadcasted_iota(jnp.int32, shape, len(shape) - 1)


def row_iota(shape):
    return lax.broadcasted_iota(jnp.int32, shape, len(shape) - 2)


def with_ones(v, lanes=(0, 1)):
    side = lane_iota(v.shape)
    ones = jnp.where((side >= lanes[0]) & (side <= lanes[1]), 1.0, 0.0).astype(BF)
    return jnp.concatenate([v, ones], axis=1)


def split_sum(state, total, third):
    rows = row_iota(state.shape)
    high = total.astype(BF).astype(F32)
    low = total - high
    out = jnp.where(rows < 128, state, 0.0)
    out = jnp.where(rows == 128, high, out)
    if third:
        out = jnp.where(rows == 129, high, out)
        out = jnp.where(rows == 130, low, out)
    else:
        out = jnp.where(rows == 129, low, out)
    return out.astype(BF)


def flat(ref):
    x = ref[...]
    return x.reshape(x.shape[0] * x.shape[2], x.shape[3])


def picks(qk, pa, pb, rows, n):
    a = dot(qk, pa[n]) + rows[0:1, :]
    b = dot(qk, pb[n]) + rows[1:2, :]
    return a, b


def state_kernel(nh, vd, docs, lens, meta, x_ref, pa, pb, rows, out):
    row = pl.program_id(0)
    x = flat(x_ref)
    length = x.shape[0]
    qk = x[:, nh * vd :]
    last = begin_at(lens, row, docs, length - 1, meta[0] * length)
    trail = row_iota((length, 2 * 128)) >= last
    for h in range(nh):
        a, b = picks(qk, pa, pb, rows, nh + h)
        kf = (a * b * rows[3:4, :]).astype(BF)
        va = jnp.where(trail, with_ones(x[:, h * vd : (h + 1) * vd]).astype(F32), 0.0).astype(BF)
        st = dot(va, kf, TN)[:AUX]
        out[0, h] = split_sum(st, st[128:129], False)


def intra_kernel(nh, vd, docs, lens, meta, x_ref, align, num_out, den_out):
    row = pl.program_id(0)
    x = flat(x_ref)
    length = x.shape[0]
    qk = x[:, nh * vd :]
    one16 = jnp.where(lane_iota((1, 128)) == FEAT, 1.0, 0.0)
    tile = min(TILE, length)
    dens = [jnp.zeros((tile, 128), F32) for _ in range(length // tile)]
    for h in range(nh):
        qa = (dot(qk, align[4 * h]) + one16).astype(BF)
        ka = (dot(qk, align[4 * h + 1]) + one16).astype(BF)
        va = with_ones(x[:, h * vd : (h + 1) * vd])
        for t in range(length // tile):
            lo, hi = t * tile, (t + 1) * tile
            s1 = dot(qa[lo:hi], ka[:hi], NT)
            w = 0.5 * (s1 * s1) + 0.5
            pos = lo + row_iota((tile, 1))
            beg = begin_at(lens, row, docs, pos, meta[0] * length)
            kpos = lane_iota(w.shape)
            w = jnp.where((kpos >= beg) & (kpos <= pos), w, 0.0).astype(BF)
            acc = dot(w, va[:hi])
            num_out[0, lo:hi, h * vd : (h + 1) * vd] = acc[:, :vd]
            lane = lane_iota((tile, 128))
            dens[t] = jnp.where(lane == h, acc[:, vd : vd + 1], dens[t])
    for t in range(length // tile):
        den_out[0, t * tile : (t + 1) * tile, :] = dens[t]


def gather_states(sts, weights, h):
    total = None
    for st, w in zip(sts, weights):
        part = st[0, h].astype(F32) * w
        total = part if total is None else total + part
    return total


def attend_kernel(nh, vd, docs, blocks, lens, meta, x_ref, num, den, pa, pb, rows, *rest):
    sts, (att_out, den_out, st_out) = rest[:-3], rest[-3:]
    row = pl.program_id(0)
    x = flat(x_ref)
    length = x.shape[0]
    qk = x[:, nh * vd :]
    weights = chain_weights(lens, row, docs, meta[0], blocks, length, False)
    pos = row_iota((length, 1))
    carried = begin_at(lens, row, docs, pos, meta[0] * length) < 0
    lane = lane_iota((length, 128))
    dens = den[0]
    for h in range(nh):
        st = gather_states(sts, weights, h)
        st = split_sum(st, st[128:129] + st[129:130], True)
        st_out[0, h] = st
        a, b = picks(qk, pa, pb, rows, h)
        qf = (a * b * rows[2:3, :]).astype(BF)
        inter = dot(qf, st, NT)
        more = jnp.where(carried, inter[:, :vd], 0.0)
        more_den = jnp.where(carried, inter[:, 128:129] + inter[:, 130:131], 0.0)
        total = dens[:, h : h + 1] + more_den
        value = (num[0, :, h * vd : (h + 1) * vd] + more) / total
        att_out[:, 0, :, h * vd : (h + 1) * vd] = value.astype(BF).reshape(
            att_out.shape[0], att_out.shape[2], vd
        )
        dens = jnp.where(lane == h, total, dens)
    den_out[0] = dens


def back_state_kernel(nh, vd, docs, lens, meta, x_ref, ga_ref, att_ref, den, pa, pb, rows, gn_out, out):
    row = pl.program_id(0)
    x, ga, att = flat(x_ref), flat(ga_ref), flat(att_ref)
    length = x.shape[0]
    qk = x[:, nh * vd :]
    pos = row_iota((length, 1))
    carried = begin_at(lens, row, docs, pos, meta[0] * length) < 0
    side = lane_iota((length, 128))
    for h in range(nh):
        cut = slice(h * vd, (h + 1) * vd)
        inv = 1.0 / den[0, :, h : h + 1]
        gah = ga[:, cut].astype(F32) * inv
        gd = -jnp.sum(gah * att[:, cut].astype(F32), axis=1, keepdims=True)
        high = gd.astype(BF).astype(F32)
        aux = jnp.where((side == 0) | (side == 2), high, jnp.where(side == 1, gd - high, 0.0))
        gn = jnp.concatenate([gah, aux], axis=1)
        gn_out[0, :, h * 256 : (h + 1) * 256] = gn.astype(BF)
        a, b = picks(qk, pa, pb, rows, h)
        qf = (a * b * rows[2:3, :]).astype(BF)
        st = dot(jnp.where(carried, gn, 0.0).astype(BF), qf, TN)[:AUX]
        out[0, h] = split_sum(st, st[128:129] + st[129:130], False)


def back_intra_kernel(
    nh, vd, docs, lens, meta, x_ref, gn_ref, st_ref, pa, pb, rows, align, gqk_out, gv_out
):
    row = pl.program_id(0)
    x = flat(x_ref)
    length = x.shape[0]
    qk = x[:, nh * vd :]
    one16 = jnp.where(lane_iota((1, 128)) == FEAT, 1.0, 0.0)
    tile = min(TILE, length)
    pos = row_iota((length, 1))
    carried = begin_at(lens, row, docs, pos, meta[0] * length) < 0
    gqk = None
    for h in range(nh):
        qa = (dot(qk, align[4 * h]) + one16).astype(BF)
        ka = (dot(qk, align[4 * h + 1]) + one16).astype(BF)
        k_at_q = dot(qk, align[4 * h + 2]).astype(BF)
        q_at_k = dot(qk, align[4 * h + 3]).astype(BF)
        va = with_ones(x[:, h * vd : (h + 1) * vd])
        gn = gn_ref[0, :, h * 256 : (h + 1) * 256]
        st = st_ref[0, h]
        gqf = jnp.where(carried, dot(gn[:, :AUX], st), 0.0) * rows[2:3, :]
        a, b = picks(qk, pa, pb, rows, h)
        part = dot((gqf * b).astype(BF), pa[h], NT) + dot((gqf * a).astype(BF), pb[h], NT)
        gqk = part if gqk is None else gqk + part
        gk_parts = []
        gq_parts = [None] * (length // tile)
        for t in range(length // tile):
            lo, hi = t * tile, (t + 1) * tile
            s1 = dot(ka[lo:hi], qa[lo:], NT)
            w = 0.5 * (s1 * s1) + 0.5
            kpos = lo + row_iota((tile, 1))
            qpos = lo + lane_iota((1, length - lo))
            beg = begin_at(lens, row, docs, qpos, meta[0] * length)
            see = (kpos >= beg) & (kpos <= qpos)
            gw = dot(va[lo:hi], gn[lo:], NT)
            gs = jnp.where(see, gw * s1, 0.0).astype(BF)
            w = jnp.where(see, w, 0.0).astype(BF)
            gv_out[0, lo:hi, h * vd : (h + 1) * vd] = dot(w, gn[lo:, :vd])
            gk_parts.append(dot(gs, q_at_k[lo:]))
            gq = dot(gs, k_at_q[lo:hi], TN)
            for u in range(t, length // tile):
                piece = gq[(u - t) * tile : (u - t + 1) * tile]
                gq_parts[u] = piece if gq_parts[u] is None else gq_parts[u] + piece
        gqk = gqk + jnp.concatenate(gk_parts, axis=0) + jnp.concatenate(gq_parts, axis=0)
    gqk_out[0] = gqk


def back_key_kernel(nh, vd, docs, blocks, lens, meta, x_ref, gqk_ref, gv_ref, pa, pb, rows, *rest):
    sts, out = rest[:-1], rest[-1]
    row = pl.program_id(0)
    x = flat(x_ref)
    length = x.shape[0]
    qk = x[:, nh * vd :]
    weights = chain_weights(lens, row, docs, meta[0], blocks, length, True)
    last = begin_at(lens, row, docs, length - 1, meta[0] * length)
    trail = row_iota((length, 1)) >= last
    gqk = gqk_ref[0]
    shape = (out.shape[0], out.shape[2])
    for h in range(nh):
        st = gather_states(sts, weights, h)
        st = split_sum(st, st[128:129] + st[129:130], False)
        va = with_ones(x[:, h * vd : (h + 1) * vd])
        gkf = jnp.where(trail, dot(va[:, :AUX], st), 0.0) * rows[3:4, :]
        a, b = picks(qk, pa, pb, rows, nh + h)
        gqk = gqk + dot((gkf * b).astype(BF), pa[nh + h], NT)
        gqk = gqk + dot((gkf * a).astype(BF), pb[nh + h], NT)
        kf = (a * b * rows[3:4, :]).astype(BF)
        more = jnp.where(trail, dot(kf, st[:vd], NT), 0.0)
        gv = gv_ref[0, :, h * vd : (h + 1) * vd] + more
        out[:, 0, :, h * vd : (h + 1) * vd] = gv.astype(BF).reshape(shape + (vd,))
    out[:, 0, :, nh * vd :] = gqk.astype(BF).reshape(shape + (128,))


def row_call(kernel, rows_n, scalars, ins, outs, flops):
    def spec(shape, dim):
        if dim is None:
            return pl.BlockSpec(shape, lambda r, *_: (0,) * len(shape))
        block = tuple(1 if d == dim else n for d, n in enumerate(shape))
        return pl.BlockSpec(block, lambda r, *_: tuple(r if d == dim else 0 for d in range(len(shape))))

    moved = sum(a.size * a.dtype.itemsize for a, _ in ins)
    moved += sum(int(np.prod(s)) * np.dtype(t).itemsize for s, t, _ in outs)
    return pl.pallas_call(
        kernel,
        out_shape=tuple(jax.ShapeDtypeStruct(s, t) for s, t, _ in outs),
        grid_spec=pltpu.PrefetchScalarGridSpec(
            num_scalar_prefetch=len(scalars),
            grid=(rows_n,),
            in_specs=[spec(a.shape, d) for a, d in ins],
            out_specs=[spec(s, d) for s, t, d in outs],
        ),
        compiler_params=pltpu.CompilerParams(vmem_limit_bytes=56 * 1024 * 1024),
        cost_estimate=pl.CostEstimate(flops=int(flops), bytes_accessed=int(moved), transcendentals=0),
    )(*scalars, *[a for a, _ in ins])


SEQ = ("sy", "sc")
HEAD = ("ha", "hb")


def here():
    return tuple(lax.axis_index(n) for n in ("sy", "sc", "ha", "hb"))


def remote(src, dst, ssem, rsem, k, device):
    return pltpu.make_async_remote_copy(
        src_ref=src,
        dst_ref=dst,
        send_sem=ssem.at[k],
        recv_sem=rsem.at[k],
        device_id=device,
        device_id_type=MESH_ID,
    )


def greet(devices):
    bar = pltpu.get_barrier_semaphore()
    for device in devices:
        pl.semaphore_signal(bar, 1, device_id=device, device_id_type=MESH_ID)
    pl.semaphore_wait(bar, len(devices))


def square():
    return tuple(lax.axis_size(n) for n in ("sy", "ha", "hb")) == (2, 4, 2)


def place(block, head, special):
    if special:
        ha = 2 * (block % 2) + block // 2
        return (head // 2 + ha % 2) % 2, head % 2, ha
    return head // 2, head % 2, block


def own_place():
    sy, sc, ha, _ = here()
    if square():
        return 2 * (ha % 2) + ha // 2, 2 * ((sy + ha) % 2) + sc
    return ha, sy * 2 + sc


def first_head(block):
    return block % 2 if square() else block


def home_of(head, special):
    if special:
        return 2 * (head % 2) + head // 2, 2 * ((head // 2 + head) % 2) + head % 2
    return head, head


def maybe_own(k, own, elsewhere, alone):
    if k:
        elsewhere()
    else:
        pl.when(jnp.logical_not(own))(elsewhere)
        pl.when(own)(alone)


def exchange_kernel(to_blocks, width, last_major, extra, src, *refs):
    n_in, n_out = {None: (0, 0), "gather": (2, 2), "scatter": (1, 2)}[extra]
    ins, dst, outs, sems = refs[:n_in], refs[n_in], refs[n_in + 1 : n_in + 1 + n_out], refs[n_in + 1 + n_out :]
    ssem, rsem, lsem = sems[:3]
    sy, sc, a, b = here()
    s = sy * 2 + sc
    block, head = own_place()
    special = square()
    size_a, size_b = lax.axis_size("ha"), lax.axis_size("hb")
    count = size_a * size_b
    bar = pltpu.get_barrier_semaphore()
    same = s == block

    def at(k):
        i, pb = k // size_b, lax.rem(b + k % size_b, size_b)
        if to_blocks:
            sender = (block // 2, block % 2, lax.rem(a + i, size_a), pb)
            to = lax.rem(a - place(s, 0, special)[2] + first_head(s) + i + size_a, size_a)
            piece = to * size_b + pb
            source = src.at[:, pl.ds(pl.multiple_of(piece * width, 128), width)]
            return sender, source, dst.at[a * size_b + b], place(s, to, special) + (pb,)
        sender = place(s, lax.rem(first_head(s) + i, size_a), special) + (pb,)
        to = lax.rem(head - first_head(block) + a + i + size_a, size_a)
        column = b * size_a + head if last_major else head * size_b + b
        far = dst.at[:, pl.ds(pl.multiple_of(column * width, 128), width)]
        return sender, src.at[to * size_b + pb], far, (block // 2, block % 2, to, pb)

    def copy(k):
        _, source, far, receiver = at(k)
        return remote(source, far, ssem, rsem, k, receiver)

    def local():
        return pltpu.make_async_copy(at(0)[1], at(0)[2], lsem.at[0])

    def signal(device):
        pl.semaphore_signal(bar, 1, device_id=device, device_id_type=MESH_ID)

    to_x, to_y, to_core = (sy, sc, a, 1 - b), (1 - sy, sc, a, b), (sy, 1 - sc, a, b)
    expected = count - same.astype(jnp.int32)
    for k in range(count):
        maybe_own(k, same, functools.partial(signal, at(k)[0]), lambda: None)
    if extra in ("gather", "scatter"):
        greeted = (to_x, to_y, to_core)[: 3 if extra == "gather" else 2]
        for device in greeted:
            signal(device)
        expected = expected + len(greeted)
    pl.semaphore_wait(bar, expected)
    for k in range(count):
        maybe_own(k, same, lambda: copy(k).start(), lambda: local().start())

    if extra == "gather":
        (more, own_w), (near, other_w) = ins, outs
        gsem, hsem = sems[3:]
        half = more.shape[0] // 2
        low, high = pl.ds(0, half), pl.ds(half, half)
        copies = [
            remote(more, near.at[1], gsem, hsem, 0, to_x),
            remote(more, near.at[2], gsem, hsem, 1, to_y),
            remote(own_w, other_w, gsem, hsem, 4, to_core),
        ]
        for c in copies:
            c.start()
        stay = pltpu.make_async_copy(more, near.at[0], lsem.at[1])
        stay.start()
        copies[0].wait_recv()
        copies.append(remote(near.at[1, high], near.at[3, high], gsem, hsem, 2, to_y))
        copies[3].start()
        copies[1].wait_recv()
        copies.append(remote(near.at[2, low], near.at[3, low], gsem, hsem, 3, to_x))
        copies[4].start()
        stay.wait()
        for c in copies[2:]:
            c.wait_recv()
        for c in copies:
            c.wait_send()
    if extra == "scatter":
        (parts,), (got, relay) = ins, outs
        gsem, hsem = sems[3:]
        half = parts.shape[1] // 2
        low, high = pl.ds(0, half), pl.ds(half, half)
        copies = [
            remote(parts.at[3, low], relay.at[0], gsem, hsem, 0, to_x),
            remote(parts.at[3, high], relay.at[1], gsem, hsem, 1, to_y),
            remote(parts.at[1], got.at[0], gsem, hsem, 2, to_x),
            remote(parts.at[2], got.at[1], gsem, hsem, 3, to_y),
        ]
        for c in copies:
            c.start()
        copies[0].wait_recv()
        copies.append(remote(relay.at[0], got.at[2, low], gsem, hsem, 4, to_y))
        copies[4].start()
        copies[1].wait_recv()
        copies.append(remote(relay.at[1], got.at[2, high], gsem, hsem, 5, to_x))
        copies[5].start()
        for c in copies[2:]:
            c.wait_recv()
        for c in copies:
            c.wait_send()
    for k in range(count):
        maybe_own(k, same, lambda: copy(k).wait(), lambda: local().wait())


def exchange(x, to_blocks, width, collective, extra=None, ins=(), outs=(), last_major=False):
    count = lax.axis_size("ha") * lax.axis_size("hb")
    tokens = x.shape[0] if to_blocks else x.shape[1]
    shape = (count, tokens, width) if to_blocks else (tokens, count * width)
    any_space = pl.BlockSpec(memory_space=pl.ANY)
    more = {None: 0, "gather": 5, "scatter": 6}[extra]
    return pl.pallas_call(
        functools.partial(exchange_kernel, to_blocks, width, last_major, extra),
        out_shape=[jax.ShapeDtypeStruct(s, x.dtype) for s in (shape, *outs)],
        in_specs=[any_space] * (1 + len(ins)),
        out_specs=[any_space] * (1 + len(outs)),
        scratch_shapes=[
            pltpu.SemaphoreType.DMA((count,)),
            pltpu.SemaphoreType.DMA((count,)),
            pltpu.SemaphoreType.DMA((2,)),
        ]
        + [pltpu.SemaphoreType.DMA((more,))] * (2 if more else 0),
        compiler_params=pltpu.CompilerParams(collective_id=collective, has_side_effects=True),
        cost_estimate=pl.CostEstimate(flops=0, bytes_accessed=x.size * 500, transcendentals=0),
    )(x, *ins)


def home_kernel(*refs):
    src, grads, windows, shards, dst, grads_got, windows_got, shards_got = refs[:8]
    ssem, rsem, lsem, gsem, hsem, usem, vsem = refs[8:]
    sy, sc, a, b = here()
    s = sy * 2 + sc
    block, head = own_place()
    special = square()
    size_a, size_b = lax.axis_size("ha"), lax.axis_size("hb")
    devices = src.shape[0]
    me = (s * size_a + a) * size_b + b
    homely = head == a
    block_h, seq_h = home_of(head, special)
    bar = pltpu.get_barrier_semaphore()

    def peer(k):
        i = lax.rem(me + k, devices)
        rest = i // (size_a * size_b)
        return i, (rest // 2, rest % 2, i // size_b % size_a, i % size_b)

    def copy(k):
        i, device = peer(k)
        return remote(src.at[i], dst.at[me], ssem, rsem, k, device)

    def grad_ends(k):
        e = lax.rem(block - block_h + seq_h + k + size_a, size_a)
        return grads.at[e], grads_got.at[block], (e // 2, e % 2, head, b)

    def grad_copy(k):
        source, far, device = grad_ends(k)
        return remote(source, far, gsem, hsem, k, device)

    def grad_local():
        return pltpu.make_async_copy(*grad_ends(0)[:2], lsem.at[1])

    def window_copy(k):
        e = lax.rem(s + k, size_a)
        return remote(windows.at[e], windows_got.at[s], gsem, hsem, size_a + k, (e // 2, e % 2, a, b))

    def shard_copy(k):
        pa = lax.rem(a + k, size_a)
        return remote(shards.at[pa], shards_got.at[a], usem, vsem, k, (sy, sc, pa, b))

    @pl.loop(1, devices)
    def _(k):
        pl.semaphore_signal(bar, 1, device_id=peer(k)[1], device_id_type=MESH_ID)

    stay = [
        pltpu.make_async_copy(shards.at[a], shards_got.at[a], lsem.at[3]),
        pltpu.make_async_copy(src.at[me], dst.at[me], lsem.at[0]),
        pltpu.make_async_copy(windows.at[s], windows_got.at[s], lsem.at[2]),
    ]
    for c in stay:
        c.start()
    pl.semaphore_wait(bar, devices - 1)
    for k in range(size_a):
        maybe_own(k, homely, lambda: grad_copy(k).start(), lambda: grad_local().start())
        if k:
            window_copy(k).start()
    for k in range(1, size_a):
        shard_copy(k).start()

    @pl.loop(1, devices)
    def _(k):
        copy(k).start()

    @pl.loop(1, devices)
    def _(k):
        copy(k).wait()

    for k in range(size_a):
        maybe_own(k, homely, lambda: grad_copy(k).wait(), lambda: grad_local().wait())
        if k:
            window_copy(k).wait()
    for k in range(1, size_a):
        shard_copy(k).wait()
    for c in stay:
        c.wait()


def send_home(x, grads, windows, shards, collective):
    devices = 2 * lax.axis_size("sy") * lax.axis_size("ha") * lax.axis_size("hb")
    vectors, share = x.shape[0], x.shape[1] // devices
    x = jnp.transpose(x.reshape(vectors, devices, share), (1, 0, 2))
    x = jnp.pad(x, ((0, 0), (0, 8 - vectors), (0, 128 - share)))
    any_space = pl.BlockSpec(memory_space=pl.ANY)
    ins = [x, grads, windows, shards]
    size_a, heads = lax.axis_size("ha"), shards.shape[0]
    out = pl.pallas_call(
        home_kernel,
        out_shape=[jax.ShapeDtypeStruct(v.shape, v.dtype) for v in ins],
        in_specs=[any_space] * len(ins),
        out_specs=[any_space] * len(ins),
        scratch_shapes=[
            pltpu.SemaphoreType.DMA((devices,)),
            pltpu.SemaphoreType.DMA((devices,)),
            pltpu.SemaphoreType.DMA((4,)),
            pltpu.SemaphoreType.DMA((2 * size_a,)),
            pltpu.SemaphoreType.DMA((2 * size_a,)),
            pltpu.SemaphoreType.DMA((heads,)),
            pltpu.SemaphoreType.DMA((heads,)),
        ],
        compiler_params=pltpu.CompilerParams(collective_id=collective, has_side_effects=True),
        cost_estimate=pl.CostEstimate(flops=0, bytes_accessed=100000000, transcendentals=0),
    )(*ins)
    vectors = jnp.sum(out[0], axis=0)[:vectors, :share]
    return vectors, jnp.sum(out[1].astype(F32), axis=0), out[2], jnp.sum(out[3].astype(F32), axis=0)


def near_kernel(rows, src, weights, near, theirs, gsem, hsem, lsem):
    sy, sc, a, b = here()
    to_x, to_y, to_core = (sy, sc, a, 1 - b), (1 - sy, sc, a, b), (sy, 1 - sc, a, b)
    half = src.shape[0] // 2
    low, high = pl.ds(0, half), pl.ds(half, half)
    greet((to_x, to_y, to_core))
    copies = [
        remote(src, near.at[1], gsem, hsem, 0, to_x),
        remote(src, near.at[2], gsem, hsem, 1, to_y),
        remote(weights.at[:, pl.ds(0, rows)], theirs, gsem, hsem, 4, to_core),
    ]
    for copy in copies:
        copy.start()
    stay = pltpu.make_async_copy(src, near.at[0], lsem)
    stay.start()
    copies[0].wait_recv()
    copies.append(remote(near.at[1, high], near.at[3, high], gsem, hsem, 2, to_y))
    copies[3].start()
    copies[1].wait_recv()
    copies.append(remote(near.at[2, low], near.at[3, low], gsem, hsem, 3, to_x))
    copies[4].start()
    stay.wait()
    for copy in copies[2:]:
        copy.wait_recv()
    for copy in copies:
        copy.wait_send()


def gather_near(x, weights, rows, collective):
    if not square():
        return lax.all_gather(x, QUAD, axis=0, tiled=True)[None], swap(weights[:, :rows], "sc")
    any_space = pl.BlockSpec(memory_space=pl.ANY)
    near, theirs = pl.pallas_call(
        functools.partial(near_kernel, rows),
        out_shape=[
            jax.ShapeDtypeStruct((4,) + x.shape, x.dtype),
            jax.ShapeDtypeStruct((weights.shape[0], rows, weights.shape[2]), weights.dtype),
        ],
        in_specs=[any_space] * 2,
        out_specs=[any_space] * 2,
        scratch_shapes=[pltpu.SemaphoreType.DMA((5,))] * 2 + [pltpu.SemaphoreType.DMA],
        compiler_params=pltpu.CompilerParams(collective_id=collective, has_side_effects=True),
        cost_estimate=pl.CostEstimate(flops=0, bytes_accessed=x.size * 200, transcendentals=0),
    )(x, weights)
    return near, theirs


def start_kernel(parts, live, src, w_in, w_out, dst, w_in_home, w_out_all, ssem, rsem, lsem, wsem, vsem):
    sy, sc, a, b = here()
    block, head = own_place()
    size = lax.axis_size("ha")
    target = place(sy * 2 + sc, a, True) + (b,)
    source = (block // 2, block % 2, head, b)
    same = jnp.logical_and(sy * 2 + sc == block, a == head)
    apart = jnp.logical_not(same)
    to_x, to_y, to_core = (sy, sc, a, 1 - b), (1 - sy, sc, a, b), (sy, 1 - sc, a, b)
    to_up, to_down = (sy, sc, a + 1, b), (sy, sc, a - 1, b)
    has_up, has_down = a < size - 1, a > 0
    bar = pltpu.get_barrier_semaphore()

    def signal(device):
        pl.semaphore_signal(bar, 1, device_id=device, device_id_type=MESH_ID)

    for device in (to_x, to_y, to_core):
        signal(device)
    pl.when(apart)(lambda: signal(source))
    pl.when(has_up)(lambda: signal(to_up))
    pl.when(has_down)(lambda: signal(to_down))
    own_w = pltpu.make_async_copy(w_out, w_out_all.at[a * 2 + b], lsem.at[parts])
    own_w.start()
    pad = pl.ds(live, w_in.shape[0] - live)
    own_pad = pltpu.make_async_copy(w_in.at[pad], w_in_home.at[pad], lsem.at[parts + 2])
    own_pad.start()
    pl.semaphore_wait(
        bar, 3 + apart.astype(jnp.int32) + has_up.astype(jnp.int32) + has_down.astype(jnp.int32)
    )

    step = src.shape[0] // parts
    count = 9
    half = src.shape[1] // 2

    def piece(z, x, r, lo=0, n=None):
        return dst.at[z * 2 + x, pl.ds(r * step, step), pl.ds(lo, src.shape[1] if n is None else n)]

    def make(k, r, ref, device):
        return remote(ref, ref, ssem, rsem, count * r + k, device)

    def home(r):
        return remote(src.at[pl.ds(r * step, step)], piece(a, b, r), ssem, rsem, count * r, target)

    def stay(r):
        return pltpu.make_async_copy(src.at[pl.ds(r * step, step)], piece(a, b, r), lsem.at[r])

    def w_home():
        return pltpu.make_async_remote_copy(
            src_ref=w_in.at[pl.ds(0, live)],
            dst_ref=w_in_home.at[pl.ds(0, live)],
            send_sem=wsem.at[0],
            recv_sem=wsem.at[1],
            device_id=target,
            device_id_type=MESH_ID,
        )

    def w_stay():
        return pltpu.make_async_copy(w_in.at[pl.ds(0, live)], w_in_home.at[pl.ds(0, live)], lsem.at[parts + 1])

    for r in range(parts):
        pl.when(apart)(lambda: home(r).start())
        pl.when(same)(lambda: stay(r).start())

    def send_w(k, pa, device):
        ref = w_out_all.at[pa * 2 + b]
        return remote(ref, ref, vsem.at[0], vsem.at[1], k, device)

    def spread(k, pa, up, down):
        if up:
            pl.when(has_up)(lambda: send_w(k, pa, to_up).start())
        if down:
            pl.when(has_down)(lambda: send_w(size + k, pa, to_down).start())
        send_w(2 * size + pa, pa, to_x).start()

    def w_step(k):
        @pl.when(a - k >= 0)
        def _():
            send_w(k - 1, a - k, to_x).wait_recv()
            spread(k, a - k, True, False)

        @pl.when(a + k < size)
        def _():
            send_w(size + k - 1, a + k, to_x).wait_recv()
            spread(k, a + k, False, True)

    across_y, across_c = (head + 2) % 4, head + 1 - 2 * (head % 2)
    across = (across_y + 1) - 2 * (across_y % 2)
    sent = []

    def go(copy):
        copy.start()
        sent.append(copy)

    def arrive(k, r, ref):
        make(k, r, ref, to_x).wait_recv()

    def stage_0(r):
        pl.when(apart)(lambda: arrive(0, r, piece(head, b, r)))
        pl.when(same)(lambda: stay(r).wait())
        for k, device in ((1, to_x), (2, to_y), (3, to_core)):
            go(make(k, r, piece(head, b, r), device))

    def stage_1(r):
        arrive(1, r, piece(head, 1 - b, r))
        go(make(4, r, piece(head, 1 - b, r, half, half), to_y))
        go(make(5, r, piece(head, 1 - b, r), to_core))
        arrive(2, r, piece(across_y, b, r))
        go(make(6, r, piece(across_y, b, r, 0, half), to_x))
        go(make(7, r, piece(across_y, b, r), to_core))

    def stage_2(r):
        arrive(4, r, piece(across_y, 1 - b, r, half, half))
        arrive(6, r, piece(across_y, 1 - b, r, 0, half))
        go(make(8, r, piece(across_y, 1 - b, r), to_core))

    def stage_3(r):
        arrive(3, r, piece(across_c, b, r))
        arrive(5, r, piece(across_c, 1 - b, r))
        arrive(7, r, piece(across, b, r))
        arrive(8, r, piece(across, 1 - b, r))

    stages = (stage_0, stage_1, stage_2, stage_3)
    for t in range(parts + 3):
        for i, stage in enumerate(stages):
            if 0 <= t - i < parts:
                stage(t - i)
        if t == 0:
            pl.when(apart)(lambda: w_home().start())
            pl.when(same)(lambda: w_stay().start())
            own_w.wait()
            spread(0, a, True, True)
        elif t < size:
            w_step(t)
    for k in range(parts + 3, size):
        w_step(k)
    pl.when(apart)(lambda: w_home().wait_recv())
    pl.when(same)(lambda: w_stay().wait())
    own_pad.wait()
    for k in range(size):
        ref = w_out_all.at[k * 2 + 1 - b]
        remote(ref, ref, vsem.at[0], vsem.at[1], 2 * size + k, to_x).wait_recv()
        send_w(2 * size + k, k, to_x).wait_send()
        pl.when(jnp.logical_and(has_up, a - k >= 0))(lambda: send_w(k, a - k, to_x).wait_send())
        pl.when(jnp.logical_and(has_down, a + k < size))(lambda: send_w(size + k, a + k, to_x).wait_send())
    for copy in sent:
        copy.wait_send()
    for r in range(parts):
        pl.when(apart)(lambda: home(r).wait_send())
    pl.when(apart)(lambda: w_home().wait_send())


def start(x, w_in, live, w_out, collective):
    if not square():
        size = lax.axis_size("ha")
        perm = [(s * size + z, z * size + s) for s in range(size) for z in range(size)]
        x, w_in = (lax.ppermute(v, ("sy", "sc", "ha"), perm) for v in (x, w_in))
        return lax.all_gather(x, ("sy", "sc", "hb"), axis=0), w_in, lax.all_gather(w_out, HEAD, axis=0)
    parts = x.shape[0]
    return pl.pallas_call(
        functools.partial(start_kernel, parts, live),
        out_shape=[
            jax.ShapeDtypeStruct((8,) + x.shape, x.dtype),
            jax.ShapeDtypeStruct(w_in.shape, w_in.dtype),
            jax.ShapeDtypeStruct((8,) + w_out.shape, w_out.dtype),
        ],
        in_specs=[pl.BlockSpec(memory_space=pl.ANY)] * 3,
        out_specs=[pl.BlockSpec(memory_space=pl.ANY)] * 3,
        scratch_shapes=[
            pltpu.SemaphoreType.DMA((9 * parts,)),
            pltpu.SemaphoreType.DMA((9 * parts,)),
            pltpu.SemaphoreType.DMA((parts + 3,)),
            pltpu.SemaphoreType.DMA((2,)),
            pltpu.SemaphoreType.DMA((2, 12)),
        ],
        compiler_params=pltpu.CompilerParams(collective_id=collective, has_side_effects=True),
        cost_estimate=pl.CostEstimate(flops=0, bytes_accessed=x.size * 400, transcendentals=0),
    )(x, w_in, w_out)


def swap(x, axis):
    return lax.ppermute(x, axis, [(0, 1), (1, 0)])


def seat(block, head, size, special):
    sy, sc, ha = place(block, head, special)
    return (sy * 2 + sc) * size + ha


def chain_pieces(x, reach, backward):
    size, special = lax.axis_size("ha"), square()
    out = []
    for k in range(1, reach + 1):
        perm = []
        for i in range(size - k):
            ends = (i + k, i) if backward else (i, i + k)
            perm += [tuple(seat(e, h, size, special) for e in ends) for h in range(size)]
        out.append(lax.ppermute(x, SEQ + ("ha",), perm))
    return out


def tie(*values):
    return lax.optimization_barrier(values)


def my_columns(x, by_core):
    parts, place_of = lax.axis_size("sy") * 2, lax.axis_index("sy") * 2 + lax.axis_index("sc")
    if by_core:
        parts, place_of = 2, lax.axis_index("sc")
    size = x.shape[1] // parts
    return lax.dynamic_slice_in_dim(x, place_of * size, size, 1)


def by_halves(a, own, other):
    own, other = dot(a, own), dot(a, other)
    first = lax.axis_index("sc") == 0
    return jnp.concatenate([jnp.where(first, own, other), jnp.where(first, other, own)], axis=1)


def by_halves_back(a, own, other):
    size = own.shape[1]
    core = lax.axis_index("sc")
    ours, theirs = (lax.dynamic_slice_in_dim(a, i * size, size, 1) for i in (core, 1 - core))
    return dot(ours, own, NT) + dot(theirs, other, NT)


def unit_window(x, size):
    units = x.shape[0]
    window = -(-units // (size * 16)) * 16
    place = lax.axis_index("sy") * 2 + lax.axis_index("sc")
    start = jnp.minimum(place * window, units - window)
    part = lax.dynamic_slice_in_dim(x, start, window, 0)
    fresh = start + lax.broadcasted_iota(jnp.int32, part.shape, 0) >= place * window
    return jnp.where(fresh, part, jnp.zeros_like(part))


def windows_joined(parts, units):
    size, window = parts.shape[0], parts.shape[1]
    pieces = []
    for i in range(size):
        start = min(i * window, units - window)
        pieces.append(parts[i, max(i * window - start, 0) :])
    return jnp.concatenate(pieces, axis=0)


def ff_kernel(n2, cot, mine, theirs, gg_out, gu_out, hid_out, part_out, acc):
    shard = pl.program_id(1)

    def work(w, first):
        x, c = n2[0], cot[0]
        window, width = w.shape[1] // 3, w.shape[2]
        w_gate, w_up, w_down = (w[:, i * window : (i + 1) * window].reshape(-1, width) for i in range(3))
        gate, up, gh = dot(x, w_gate, NT), dot(x, w_up, NT), dot(c, w_down, NT)
        sig = jax.nn.sigmoid(gate)
        act = gate * sig
        hid_out[0, 0] = (act * up).astype(BF)
        gg = (gh * up * (sig + act * (1.0 - sig))).astype(BF)
        gu = (gh * act).astype(BF)
        gg_out[0, 0] = gg
        gu_out[0, 0] = gu
        back = dot(gg, w_gate) + dot(gu, w_up)
        if first:
            acc[...] = back
        else:
            part_out[0] = (acc[...] + back).astype(BF)

    @pl.when(shard == 0)
    def _():
        work(mine, True)

    @pl.when(shard == 1)
    def _():
        work(theirs, False)


def ff_pass(n2, cots, mine, theirs):
    chunks, tokens, width = n2.shape
    units = theirs.shape[0] * theirs.shape[1] // 3
    keep = jax.ShapeDtypeStruct((2, chunks, tokens, units), BF)
    whole = pl.BlockSpec((1, tokens, width), lambda c, i: (c, 0, 0))
    weights = pl.BlockSpec(theirs.shape, lambda c, i: (0, 0, 0), pipeline_mode=pl.Buffered(1))
    piece = pl.BlockSpec((1, 1, tokens, units), lambda c, i: (i, c, 0, 0))
    return pl.pallas_call(
        ff_kernel,
        out_shape=(keep, keep, keep, jax.ShapeDtypeStruct((chunks, tokens, width), BF)),
        grid=(chunks, 2),
        in_specs=[whole, whole, weights, weights],
        out_specs=[piece, piece, piece, whole],
        scratch_shapes=[pltpu.VMEM((tokens, width), F32)],
        compiler_params=pltpu.CompilerParams(vmem_limit_bytes=60 * 1024 * 1024),
        cost_estimate=pl.CostEstimate(
            flops=chunks * tokens * width * units * 20,
            bytes_accessed=12 * units * width + 8 * chunks * tokens * width,
            transcendentals=0,
        ),
    )(n2, cots, mine, theirs)


def branch_kernel(order, hidden, mine, theirs, out):
    width = out.shape[1]
    part = dot(hidden[0, 0], mine[...].reshape(-1, width)) + dot(hidden[1, 0], theirs[...].reshape(-1, width))
    out[...] = part.astype(BF)


def branch_product(hidden, mine, theirs):
    _, chunks, tokens, units = hidden.shape
    size, rows, width = theirs.shape
    weights = pl.BlockSpec((size, rows // 3, width), lambda i, m: (0, 2, 0), pipeline_mode=pl.Buffered(1))
    y, b = lax.axis_index("sy"), lax.axis_index("hb")
    turns = ((y, b), (y, 1 - b), (1 - y, b), (1 - y, 1 - b))[:chunks]
    order = jnp.stack([p * 2 + q if chunks > 1 else 0 * p for p, q in turns]).astype(jnp.int32)
    return pl.pallas_call(
        branch_kernel,
        out_shape=jax.ShapeDtypeStruct((chunks * tokens, width), BF),
        grid_spec=pltpu.PrefetchScalarGridSpec(
            num_scalar_prefetch=1,
            grid=(chunks,),
            in_specs=[pl.BlockSpec((2, 1, tokens, units), lambda i, m: (0, i, 0, 0)), weights, weights],
            out_specs=pl.BlockSpec((tokens, width), lambda i, m: (m[i], 0)),
        ),
        compiler_params=pltpu.CompilerParams(vmem_limit_bytes=40 * 1024 * 1024),
        cost_estimate=pl.CostEstimate(
            flops=chunks * tokens * units * width * 4, bytes_accessed=12 * units * width, transcendentals=0
        ),
    )(order, hidden, mine, theirs)


QUAD = ("sy", "hb")


def add_low(a, b):
    return (a.astype(F32) + b.astype(F32)).astype(BF)


def ring_sum(parts, meanwhile):
    own, to_x, to_y, across = parts
    half = own.shape[0] // 2
    via_x, via_y = swap(across[:half], "hb"), swap(across[half:], "sy")
    x_low, y_high = swap(to_x[:half], "hb"), swap(to_y[half:], "sy")
    work = meanwhile(0)
    via_x, via_y, *work = tie(via_x, via_y, *work)
    meanwhile(0, work)
    y_low = swap(add_low(to_y[:half], via_x), "sy")
    x_high = swap(add_low(to_x[half:], via_y), "hb")
    work = meanwhile(1)
    y_low, x_high, *work = tie(y_low, x_high, *work)
    meanwhile(1, work)
    low = own[:half].astype(F32) + x_low.astype(F32) + y_low.astype(F32)
    high = own[half:].astype(F32) + x_high.astype(F32) + y_high.astype(F32)
    return jnp.concatenate([low, high], axis=0)


def core_sum(a, b):
    size_y, core = lax.axis_size("sy"), lax.axis_index("sc")
    size = b.shape[1] // (size_y * 2)

    def of_core(c):
        columns = [lax.dynamic_slice_in_dim(b, (i * 2 + c) * size, size, 1) for i in range(size_y)]
        return jnp.concatenate(columns, axis=1)

    given = swap(dot(a, of_core(1 - core), TN).astype(BF), "sc")
    part = (dot(a, of_core(core), TN) + given.astype(F32)).astype(BF)
    return jnp.stack([part[:, i * size : (i + 1) * size] for i in range(size_y)])


def quad_sum(parts, meanwhile):
    if len(parts) == 4:
        return ring_sum(parts, meanwhile)
    for stage in (0, 1):
        meanwhile(stage)
    return lax.psum_scatter(parts[0], QUAD, scatter_dimension=0, tiled=True).astype(F32)


def ff_group(chunks, cots, mine, theirs):
    *kept, part = ff_pass(chunks, cots, mine, theirs)
    grads, branch = [], []
    width = chunks.shape[-1]
    flat = [k.reshape(2, -1, k.shape[-1]) for k in kept] + [chunks.reshape(-1, width), cots.reshape(-1, width)]
    pairs = [(flat[0], flat[3]), (flat[1], flat[3]), (flat[2], flat[4])]

    def meanwhile(stage, results=None):
        if results is not None:
            grads[:] = results[:3]
            branch[:] = results[3:]
            return None
        if stage == 0:
            grads.extend(swap(dot(a[1], b, TN).astype(BF), "sc") for a, b in pairs)
            return grads
        for i, (a, b) in enumerate(pairs):
            grads[i] = (dot(a[0], b, TN) + grads[i].astype(F32)).astype(BF)
        branch.append(branch_product(kept[2], mine, theirs))
        return grads + branch

    return quad_sum([part[i] for i in range(part.shape[0])], meanwhile), grads, branch[0]


def rms_scale(x):
    return lax.rsqrt(jnp.mean(x * x, axis=-1, keepdims=True) + EPS)


def on_device(
    inputs,
    attn_gain,
    w_query,
    w_key,
    w_value,
    w_out,
    out_bias,
    mlp_gain,
    gate_weight,
    up_weight,
    down_weight,
    cotangent,
    doc_lengths,
):
    every = ("sy", "sc", "ha", "hb")
    blocks = lax.axis_size("sy") * 2
    size_a, size_b = lax.axis_size("ha"), lax.axis_size("hb")
    count = size_a * size_b
    sub_len, rows_n, width = inputs.shape
    docs = doc_lengths.shape[1]
    nh = w_query.shape[1] // FEAT
    vd = w_value.shape[1] // nh
    vw = nh * vd
    xw = vw + 128
    length = sub_len * count
    tokens = rows_n * sub_len
    meta = own_place()[0].astype(jnp.int32).reshape(1)
    pa, pb, frows, align = feature_tables(nh)
    scalars = (doc_lengths, meta)

    x = jnp.transpose(inputs, (1, 0, 2)).astype(F32)
    cot = jnp.transpose(cotangent, (1, 0, 2))
    scale_one = rms_scale(x)
    normed_one = x * scale_one
    pad = jnp.zeros((128 - 2 * nh * FEAT, width), BF)
    w_in = jnp.concatenate([w_value.T, w_query.T, w_key.T, pad], axis=0)
    units = down_weight.shape[0]
    windows = [unit_window(w, blocks) for w in (gate_weight.T, up_weight.T, down_weight)]
    w_in_piece = my_columns(w_in, False)
    to_fetch = jnp.concatenate(windows, axis=0)
    normed_full, w_in_home, w_out_piece = start((normed_one * attn_gain).astype(BF), w_in, vw + 2 * nh * FEAT, my_columns(w_out, True), 3)
    to_fetch, normed_full = tie(to_fetch, normed_full)
    fetched = lax.all_gather(to_fetch, "ha", axis=0)
    window = windows[0].shape[0]

    qkv = jnp.einsum("grtd,cd->grtc", normed_full, w_in_home, preferred_element_type=F32).astype(BF)
    pair = nh * rows_n * length * length
    (states,) = row_call(
        functools.partial(state_kernel, nh, vd, docs),
        rows_n,
        scalars,
        [(qkv, 1), (pa, None), (pb, None), (frows, None)],
        [((rows_n, nh, AUX, TILE), BF, 0)],
        nh * rows_n * length * 256 * 256 * 4,
    )
    earlier = chain_pieces(states, chain_reach(blocks, length), False)
    num, den = row_call(
        functools.partial(intra_kernel, nh, vd, docs),
        rows_n,
        scalars,
        [(qkv, 1), (align, None)],
        [((rows_n, length, vw), F32, 0), ((rows_n, length, 128), F32, 0)],
        pair * 256 * 4,
    )
    att, den, state_in = row_call(
        functools.partial(attend_kernel, nh, vd, docs, blocks),
        rows_n,
        scalars,
        [(qkv, 1), (num, 0), (den, 0), (pa, None), (pb, None), (frows, None)]
        + [(e, 0) for e in earlier],
        [
            ((count, rows_n, sub_len, vw), BF, 1),
            ((rows_n, length, 128), F32, 0),
            ((rows_n, nh, AUX, TILE), BF, 0),
        ],
        nh * rows_n * length * 256 * 256 * 6,
    )
    flat_cot, to_owners = cot.reshape(tokens, width), att.reshape(count, tokens, vw)
    if square():
        attended, cots, w_out_other = exchange(
            to_owners, False, vw, 0, "gather", (flat_cot, w_out_piece), ((4, tokens, width), w_out_piece.shape)
        )
    else:
        (attended,) = exchange(to_owners, False, vw, 0)
        cots = lax.all_gather(flat_cot, QUAD, axis=0, tiled=True)[None]
        w_out_other = swap(w_out_piece, "sc")
    w_out_halves = [w.reshape(count * vw, width // 2) for w in (w_out_piece, w_out_other)]
    attn_branch = by_halves(attended, *w_out_halves).reshape(rows_n, sub_len, width)
    middle = x + attn_branch + out_bias
    scale_two = rms_scale(middle)
    normed_two = middle * scale_two
    normed_two_low = (normed_two * mlp_gain).astype(BF)

    chunks, theirs = gather_near(normed_two_low.reshape(tokens, width), fetched, 3 * window, 4)
    w_in_piece, chunks = tie(w_in_piece, chunks)
    w_in_all = lax.all_gather(w_in_piece, ("sy", "sc", "hb", "ha"), axis=0)
    grad_two, ff_grads, branch = ff_group(chunks, cots, fetched, theirs)
    grad_two = grad_two.reshape(rows_n, sub_len, width)
    gain_two_part = jnp.sum(grad_two * normed_two, axis=(0, 1))
    scaled = grad_two * mlp_gain
    grad_middle = cot.astype(F32) + scale_two * (
        scaled - normed_two * jnp.mean(scaled * normed_two, axis=-1, keepdims=True)
    )
    bias_part = jnp.sum(grad_middle, axis=(0, 1))
    grad_branch = grad_middle.astype(BF)

    flat_branch = grad_branch.reshape(tokens, width)
    grad_att = by_halves_back(flat_branch, *w_out_halves).astype(BF)
    branch, w_in_all = tie(branch, w_in_all)
    branch = lax.psum_scatter(branch, QUAD, scatter_dimension=0, tiled=True)
    grad_att, ff_grads = tie(grad_att, jnp.concatenate(ff_grads, axis=1))
    (grad_att,) = exchange(grad_att, True, vw, 1)
    ff_grads, branch, grad_att = tie(ff_grads, branch, grad_att)
    ff_grads = lax.psum_scatter(ff_grads, "ha", scatter_dimension=0, tiled=True)
    grad_att = grad_att.reshape(count, rows_n, sub_len, vw)
    output = (middle + branch.astype(F32).reshape(rows_n, sub_len, width)).astype(BF)
    part = core_sum(attended, flat_branch).reshape(-1, size_a, size_b, vw, width // blocks)
    part = jnp.transpose(part, (0, 2, 1, 3, 4)).reshape(-1, size_a * vw, width // blocks)
    ff_grads = jnp.transpose(ff_grads.reshape(-1, 3, blocks, width // blocks), (2, 1, 0, 3))
    ff_grads = ff_grads.reshape(blocks, -1, width // blocks)
    gn, grad_states = row_call(
        functools.partial(back_state_kernel, nh, vd, docs),
        rows_n,
        scalars,
        [(qkv, 1), (grad_att, 1), (att, 1), (den, 0), (pa, None), (pb, None), (frows, None)],
        [((rows_n, length, nh * 256), BF, 0), ((rows_n, nh, AUX, TILE), BF, 0)],
        nh * rows_n * length * 256 * 256 * 4,
    )
    later = chain_pieces(grad_states, chain_reach(blocks, length), True)
    gqk, gv = row_call(
        functools.partial(back_intra_kernel, nh, vd, docs),
        rows_n,
        scalars,
        [(qkv, 1), (gn, 0), (state_in, 0), (pa, None), (pb, None), (frows, None), (align, None)],
        [((rows_n, length, 128), F32, 0), ((rows_n, length, vw), F32, 0)],
        pair * 256 * 8,
    )
    (gqkv,) = row_call(
        functools.partial(back_key_kernel, nh, vd, docs, blocks),
        rows_n,
        scalars,
        [(qkv, 1), (gqk, 0), (gv, 0), (pa, None), (pb, None), (frows, None)] + [(e, 0) for e in later],
        [((count, rows_n, sub_len, xw), BF, 1)],
        nh * rows_n * length * 256 * 256 * 6,
    )
    to_owners = gqkv.reshape(count, tokens, xw)
    if square():
        y, b = lax.axis_index("sy"), lax.axis_index("hb")
        turns = (y * 2 + b, y * 2 + 1 - b, (1 - y) * 2 + b, (1 - y) * 2 + 1 - b)
        part = jnp.stack([lax.dynamic_index_in_dim(part, i, 0, False) for i in turns])
        shape = part.shape[1:]
        relay = (2, shape[0] // 2, shape[1])
        grad_in, got, _ = exchange(
            to_owners, False, xw, 2, "scatter", (part,), ((3,) + shape, relay), last_major=True
        )
        grad_w_out = sum((got[i].astype(F32) for i in range(3)), part[0].astype(F32)).astype(BF)
    else:
        (grad_in,) = exchange(to_owners, False, xw, 2, last_major=True)
        grad_w_out = lax.psum_scatter(part, QUAD, scatter_dimension=0, tiled=True)
    grad_w_out = grad_w_out.reshape(size_a, vw, width // blocks)
    w_in_all = w_in_all.reshape(blocks, count * xw, width // blocks)
    grad_one = jnp.concatenate([dot(grad_in, w_in_all[i]) for i in range(blocks)], axis=1)
    grad_one = grad_one.reshape(rows_n, sub_len, width)
    gain_one_part = jnp.sum(grad_one * normed_one, axis=(0, 1))
    scaled = grad_one * attn_gain
    input_grad = (
        grad_middle
        + scale_one * (scaled - normed_one * jnp.mean(scaled * normed_one, axis=-1, keepdims=True))
    ).astype(BF)

    flat_tokens = count * tokens
    grad_w_in = dot(gqkv.reshape(flat_tokens, xw), normed_full.reshape(flat_tokens, width), TN)
    live = vw + 2 * nh * FEAT
    grad_w_in = grad_w_in.astype(BF)[:live].reshape(live, blocks, width // blocks)
    grad_w_in = jnp.transpose(grad_w_in, (1, 0, 2))
    vectors = jnp.stack([gain_one_part, bias_part, gain_two_part])
    vectors, grad_w_in, ff_grads, grad_w_out = send_home(vectors, grad_w_in, ff_grads, grad_w_out, 5)
    ff_grads = ff_grads.astype(F32).reshape(blocks, 3, -1, width // blocks)
    grad_gate_w, grad_up_w, grad_down_w = (windows_joined(ff_grads[:, i], units) for i in range(3))
    qk_cut = vw + nh * FEAT
    return (
        jnp.transpose(output, (1, 0, 2)),
        jnp.transpose(input_grad, (1, 0, 2)),
        vectors[0],
        grad_w_in[vw:qk_cut].T,
        grad_w_in[qk_cut : qk_cut + nh * FEAT].T,
        grad_w_in[:vw].T,
        grad_w_out,
        vectors[1],
        vectors[2],
        grad_gate_w.T,
        grad_up_w.T,
        grad_down_w,
    )


def solution(mesh):
    seq, head = mesh.shape["seq"], mesh.shape["head"]
    inner = Mesh(mesh.devices.reshape(seq // 2, 2, seq, head // seq), ("sy", "sc", "ha", "hb"))
    every, heads = ("sy", "sc", "ha", "hb"), ("ha", "hb")
    placed = (
        P(every, None, None),
        P(),
        P(None, heads),
        P(None, heads),
        P(None, heads),
        P(heads, None),
        P(),
        P(),
        P(None, heads),
        P(None, heads),
        P(heads, None),
        P(every, None, None),
        P(),
    )
    return jax.shard_map(
        on_device,
        mesh=inner,
        in_specs=placed,
        out_specs=(
            P(every, None, None),
            P(every, None, None),
            P(every),
            P(SEQ, heads),
            P(SEQ, heads),
            P(SEQ, heads),
            P(heads, SEQ),
            P(every),
            P(every),
            P(SEQ, heads),
            P(SEQ, heads),
            P(heads, SEQ),
        ),
        check_vma=False,
    )
```
